32 devices in a mesh: dp: 4 (over y, x), ctx: 2 (over core), tp: 4 (over z).
Axes of the slice: x: 2, y: 2, z: 4, core: 2. Of those that a mesh axis runs over, the one named last changes fastest.
Arguments:
- tokens: bfloat16 [4096, 1024], P(('dp', 'ctx')), may hold values from -6 to 6
- norm_gain: float32 [1024], replicated, may hold values from 0.5 to 1.5
- gate_weight: bfloat16 [1024, 2048], P(('dp', 'ctx'), 'tp'), may hold values from -0.1875 to 0.1875
- input_weight: bfloat16 [1024, 2048], P(('dp', 'ctx'), 'tp'), may hold values from -0.1875 to 0.1875
- state_weight: bfloat16 [1024, 256], P(('dp', 'ctx'), 'tp'), may hold values from -0.1875 to 0.1875
- step_weight: bfloat16 [1024, 32], P(('dp', 'ctx'), 'tp'), may hold values from -0.1875 to 0.1875
- input_kernel: float32 [4, 2048], P(None, 'tp'), may hold values from -0.5 to 0.5
- input_offset: float32 [2048], P('tp'), may hold values from -0.5 to 0.5
- state_kernel: float32 [4, 256], P(None, 'tp'), may hold values from -0.5 to 0.5
- state_offset: float32 [256], P('tp'), may hold values from -0.5 to 0.5
- step_bias: float32 [32], P('tp'), may hold values from -5.5 to -3.5
- decay_log: float32 [32], P('tp'), may hold values from -4.6 to 1.1
- skip_gain: float32 [32], P('tp'), may hold values from 0.5 to 1.5
- gated_gain: float32 [2048], P('tp'), may hold values from 0.5 to 1.5
- out_weight: bfloat16 [2048, 1024], P('tp', ('dp', 'ctx')), may hold values from -0.125 to 0.125
- cotangent: bfloat16 [4096, 1024], P(('dp', 'ctx')), may hold values from -6 to 6
Outputs:
- block_out: bfloat16 [4096, 1024], P(('dp', 'ctx'))
- grad_tokens: float32 [4096, 1024], P(('dp', 'ctx'))
- grad_norm_gain: float32 [1024], replicated
- grad_gate_weight: float32 [1024, 2048], P(('dp', 'ctx'), 'tp')
- grad_input_weight: float32 [1024, 2048], P(('dp', 'ctx'), 'tp')
- grad_state_weight: float32 [1024, 256], P(('dp', 'ctx'), 'tp')
- grad_step_weight: float32 [1024, 32], P(('dp', 'ctx'), 'tp')
- grad_input_kernel: float32 [4, 2048], P(None, 'tp')
- grad_input_offset: float32 [2048], P('tp')
- grad_state_kernel: float32 [4, 256], P(None, 'tp')
- grad_state_offset: float32 [256], P('tp')
- grad_step_bias: float32 [32], P('tp')
- grad_decay_log: float32 [32], P('tp')
- grad_skip_gain: float32 [32], P('tp')
- grad_gated_gain: float32 [2048], P('tp')
- grad_out_weight: float32 [2048, 1024], P('tp', ('dp', 'ctx'))
The draws below stay inside these ranges and needn't reach their ends.
All inputs are finite; a program needn't handle non-finite values.
Results may differ from the reference program's by a relative error of at most 0.012.
Values may be sent and summed in bfloat16 or wider, within the bound.
A program may use at most 128 MiB of HBM per device.

```python
import jax
import jax.numpy as jnp
from jax import lax

D = 1024
DI = 2048
HEADS = 32
STATE = 128
CONV = 4
STRETCH = 256
SEQ = 1024
TOKENS = 4096


def shard_levels(own_key, dims, split, smallest, top_value):
    gain, own = 1.0, jax.random.fold_in(own_key, 6)
    for position, parts in split:
        draws = jnp.exp(jax.random.uniform(jax.random.fold_in(own, position), (parts,), jnp.float32, smallest / len(split), top_value / len(split)))
        gain = gain * jnp.repeat(draws, dims[position] // parts).reshape([-1 if axis == position else 1 for axis in range(len(dims))])
    return gain


def noise(own_key, dims, width, bound, pieces=(), dtype=jnp.bfloat16):
    drawn = jax.random.normal(own_key, dims, jnp.float32) * width
    if len(pieces) > 0:
        drawn = shard_levels(own_key, dims, pieces, -0.22, 0.18) * drawn
    return jnp.clip(drawn, min=-bound, max=bound).astype(dtype)


def setup_inputs(seed: int = 0) -> dict:
    splits = jax.random.split(jax.random.key(seed), 17)
    return {
        "tokens": noise(splits[0], (TOKENS, D), 1.0, 6.0, ((0, 8),)),
        "norm_gain": jnp.clip(1.0 + 0.1 * jax.random.normal(splits[1], (D,), jnp.float32), 0.5, 1.5),
        "gate_weight": noise(splits[2], (D, DI), D ** -0.5, 0.1875, ((0, 8), (1, 4))),
        "input_weight": noise(splits[3], (D, DI), D ** -0.5, 0.1875, ((0, 8), (1, 4))),
        "state_weight": noise(splits[4], (D, 2 * STATE), D ** -0.5, 0.1875, ((0, 8), (1, 4))),
        "step_weight": noise(splits[5], (D, HEADS), D ** -0.5, 0.1875, ((0, 8), (1, 4))),
        "input_kernel": jnp.clip(jax.random.uniform(splits[6], (CONV, DI), jnp.float32, -0.5, 0.5) * shard_levels(splits[6], (CONV, DI), ((1, 4),), -0.4, 0.0), -0.5, 0.5),
        "input_offset": jnp.clip(jax.random.uniform(splits[7], (DI,), jnp.float32, -0.5, 0.5) * shard_levels(splits[7], (DI,), ((0, 4),), -0.4, 0.0), -0.5, 0.5),
        "state_kernel": jnp.clip(jax.random.uniform(splits[8], (CONV, 2 * STATE), jnp.float32, -0.5, 0.5) * shard_levels(splits[8], (CONV, 2 * STATE), ((1, 4),), -0.4, 0.0), -0.5, 0.5),
        "state_offset": jnp.clip(jax.random.uniform(splits[9], (2 * STATE,), jnp.float32, -0.5, 0.5) * shard_levels(splits[9], (2 * STATE,), ((0, 4),), -0.4, 0.0), -0.5, 0.5),
        "step_bias": jnp.clip(-5.5 + 2.0 * jax.random.uniform(splits[10], (HEADS,), jnp.float32) ** shard_levels(splits[10], (HEADS,), ((0, 4),), -0.2, 0.2), -5.5, -3.5),
        "decay_log": jnp.clip(-4.6 + 5.7 * jax.random.uniform(splits[11], (HEADS,), jnp.float32) ** shard_levels(splits[11], (HEADS,), ((0, 4),), -0.2, 0.2), -4.6, 1.1),
        "skip_gain": jnp.clip(0.5 + 1.0 * jax.random.uniform(splits[12], (HEADS,), jnp.float32) ** shard_levels(splits[12], (HEADS,), ((0, 4),), -0.2, 0.2), 0.5, 1.5),
        "gated_gain": jnp.clip(1.0 + 0.1 * jax.random.normal(splits[13], (DI,), jnp.float32), 0.5, 1.5),
        "out_weight": noise(splits[14], (DI, D), DI ** -0.5, 0.125, ((0, 4), (1, 8))),
        "cotangent": noise(splits[15], (TOKENS, D), 1.0, 6.0, ((0, 8),)),
    }


epsilon = 1e-05
exact_mode = lax.Precision.HIGHEST

@jax.custom_vjp
def low(v):
    return lax.optimization_barrier(v.astype(jnp.bfloat16)).astype(jnp.float32)

@jax.custom_vjp
def low_back(v):
    return v

def low_keep(v):
    return (low(v), None)

def low_pass(kept, grad):
    return (grad,)

def back_keep(v):
    return (v, None)

def back_low(kept, grad):
    return (low(grad),)
low.defvjp(low_keep, low_pass)
low_back.defvjp(back_keep, back_low)

def rms_norm(values, norm_scale):
    meansq = lax.optimization_barrier(jnp.mean(values * values, axis=-1, keepdims=True))
    return values * lax.rsqrt(meansq + epsilon) * norm_scale

def causal_conv(padded, kernel, offset):
    tap_count = kernel.shape[0]
    length = padded.shape[0] - tap_count + 1
    summed = offset[None, :] + kernel[0][None, :] * padded[0:length]
    for tap_index in range(1, tap_count):
        summed = summed + kernel[tap_index][None, :] * padded[tap_index:tap_index + length]
    return jax.nn.silu(summed)

def block_step(carry_state, block_in):
    values, step_sizes, decays, inputs_b, readout_c = block_in
    running = jnp.cumsum(decays, axis=0)
    length = running.shape[0]
    rowpos = lax.broadcasted_iota(jnp.int32, (length, length), 0)
    colpos = lax.broadcasted_iota(jnp.int32, (length, length), 1)
    causal = (rowpos >= colpos)[:, :, None]
    spread = running[:, None, :] - running[None, :, :]
    weights = jnp.exp(jnp.where(causal, spread, -jnp.inf))
    scores = jnp.dot(readout_c, inputs_b.T, precision=exact_mode)
    mixing = weights * scores[:, :, None] * step_sizes[None, :, :]
    within = jnp.einsum('ijh,jhp->ihp', mixing, values, precision=exact_mode)
    carried = jnp.einsum('in,hpn->ihp', readout_c, carry_state, precision=exact_mode) * jnp.exp(running)[:, :, None]
    block_total = running[-1]
    tail_weight = jnp.exp(block_total[None, :] - running) * step_sizes
    fresh_state = jnp.einsum('jh,jn,jhp->hpn', tail_weight, inputs_b, values, precision=exact_mode)
    new_state = jnp.exp(block_total)[:, None, None] * carry_state + fresh_state
    return (new_state, within + carried)

def scan_local(values, step_sizes, decays, inputs_b, readout_c, start):
    length, head_count, headdim = values.shape
    blocks_n = length // STRETCH
    blocks = (values.reshape(blocks_n, STRETCH, head_count, headdim), step_sizes.reshape(blocks_n, STRETCH, head_count), decays.reshape(blocks_n, STRETCH, head_count), inputs_b.reshape(blocks_n, STRETCH, inputs_b.shape[1]), readout_c.reshape(blocks_n, STRETCH, readout_c.shape[1]))
    final_state, outputs = lax.scan(jax.checkpoint(block_step), start, blocks)
    return (outputs.reshape(length, head_count, headdim), final_state)

def forward(tokens, norm_gain, gate_weight, input_weight, state_weight, step_weight, input_kernel, input_offset, state_kernel, state_offset, step_bias, decay_log, skip_gain, gated_gain, out_weight):
    normed = low(rms_norm(tokens, norm_gain))
    gate_val = low_back(jnp.dot(normed, gate_weight, precision=exact_mode))
    input_pre = low_back(jnp.dot(normed, input_weight, precision=exact_mode))
    state_pre = low_back(jnp.dot(normed, state_weight, precision=exact_mode))
    step_pre = low_back(jnp.dot(normed, step_weight, precision=exact_mode))
    row_count = tokens.shape[0]
    seq_count = row_count // SEQ
    rim_rows = input_kernel.shape[0] - 1

    def conv_all(projection, kernel, offset):
        grouped = projection.reshape(seq_count, SEQ, projection.shape[1])
        padded = jnp.pad(grouped, ((0, 0), (rim_rows, 0), (0, 0)))
        convolved = jax.vmap(causal_conv, in_axes=(0, None, None))(padded, kernel, offset)
        return convolved.reshape(row_count, projection.shape[1])
    values = conv_all(input_pre, input_kernel, input_offset)
    states_bc = low(conv_all(state_pre, state_kernel, state_offset))
    head_count = step_weight.shape[1]
    headdim = values.shape[1] // head_count
    nstate = states_bc.shape[1] // 2
    step_sizes = jax.nn.softplus(step_pre + step_bias)
    decays = -step_sizes * jnp.exp(decay_log)
    values_heads = values.reshape(seq_count, SEQ, head_count, headdim)
    zero_state = jnp.zeros((seq_count, head_count, headdim, nstate), jnp.float32)
    scanned, ignored = jax.vmap(scan_local)(values_heads, step_sizes.reshape(seq_count, SEQ, head_count), decays.reshape(seq_count, SEQ, head_count), states_bc[:, :nstate].reshape(seq_count, SEQ, nstate), states_bc[:, nstate:].reshape(seq_count, SEQ, nstate), zero_state)
    scanned = scanned + skip_gain[None, None, :, None] * values_heads
    gated_out = scanned.reshape(row_count, head_count * headdim) * jax.nn.silu(gate_val)
    inv_rms = lax.rsqrt(lax.optimization_barrier(jnp.mean(gated_out * gated_out, axis=1, keepdims=True)) + epsilon)
    scaled = low(gated_out * gated_gain)
    projected = low_back(jnp.dot(scaled, out_weight, precision=exact_mode))
    return tokens + inv_rms * projected

def reference(tokens, norm_gain, gate_weight, input_weight, state_weight, step_weight, input_kernel, input_offset, state_kernel, state_offset, step_bias, decay_log, skip_gain, gated_gain, out_weight, cotangent):
    floats = tuple((argument.astype(jnp.float32) for argument in (tokens, norm_gain, gate_weight, input_weight, state_weight, step_weight, input_kernel, input_offset, state_kernel, state_offset, step_bias, decay_log, skip_gain, gated_gain, out_weight)))
    result, pullback = jax.vjp(forward, *floats)
    gradients = pullback(cotangent.astype(jnp.float32))
    return (result.astype(jnp.bfloat16), gradients[0], gradients[1], gradients[2], gradients[3], gradients[4], gradients[5], gradients[6], gradients[7], gradients[8], gradients[9], gradients[10], gradients[11], gradients[12], gradients[13], gradients[14])
```

```python
import functools
from types import SimpleNamespace

import jax
import jax.numpy as jnp
from jax import lax
from jax.experimental import pallas as pl
from jax.experimental.pallas import tpu as pltpu
from jax.sharding import PartitionSpec as P

STRETCH = 256
LANES = 128
HALO = 16
MISC = 80
CHUNK = 32
HOP = 2
STORES = (
    "block",
    "tokens",
    "gain",
    "gate",
    "in",
    "state",
    "step",
    "in_kernel",
    "in_offset",
    "st_kernel",
    "st_offset",
    "bias",
    "decay",
    "skip",
    "gated",
    "out",
)
SMALL_INPUTS = (
    "state_t",
    "step_t",
    "norm_gain",
    "input_kernel",
    "input_offset",
    "state_kernel",
    "state_offset",
    "step_bias",
    "decay_log",
    "skip_gain",
    "gated_gain",
)
epsilon = 1e-05
exact_mode = lax.Precision.HIGHEST
MESH = pl.DeviceIdType.MESH
low = jnp.bfloat16
wide = jnp.float32


def mm(left, right, dims, precision=None):
    return lax.dot_general(
        left, right, (dims, ((), ())), precision=precision, preferred_element_type=wide
    )


def line_up(peers):
    barrier = pltpu.get_barrier_semaphore()
    for peer in peers:
        pl.semaphore_signal(barrier, inc=1, device_id=peer, device_id_type=MESH)
    pl.semaphore_wait(barrier, len(peers))


def send_to(source, target, sends, recvs, peer):
    return pltpu.make_async_remote_copy(
        src_ref=source,
        dst_ref=target,
        send_sem=sends,
        recv_sem=recvs,
        device_id=peer,
        device_id_type=MESH,
    )


def span(index, size):
    return pl.ds(pl.multiple_of(index * size, size), size)


def each(count, body, carry=None):
    def step(i, carry):
        return body(i, carry)

    return lax.fori_loop(0, count, step, carry)


def causal_mask(size):
    down = lax.broadcasted_iota(jnp.int32, (size, size), 0)
    right = lax.broadcasted_iota(jnp.int32, (size, size), 1)
    return down >= right


def widen(columns, width):
    rows, heads = columns.shape
    return jnp.concatenate(
        [jnp.broadcast_to(columns[:, h : h + 1], (rows, width)) for h in range(heads)], axis=1
    )


def tallen(column, width, lanes):
    return jnp.concatenate(
        [
            jnp.broadcast_to(column[h : h + 1, :], (width, lanes))
            for h in range(column.shape[0])
        ],
        axis=0,
    )


def per_head(values, heads):
    width = values.shape[1] // heads
    return jnp.concatenate(
        [
            jnp.sum(values[:, h * width : (h + 1) * width], axis=1, keepdims=True)
            for h in range(heads)
        ],
        axis=1,
    )


def turned(row):
    size = row.shape[1]
    down = lax.broadcasted_iota(jnp.int32, (size, size), 0)
    right = lax.broadcasted_iota(jnp.int32, (size, size), 1)
    return jnp.sum(
        jnp.where(down == right, jnp.broadcast_to(row, (size, size)), 0.0), axis=1, keepdims=True
    )


def laid(column):
    size = column.shape[0]
    down = lax.broadcasted_iota(jnp.int32, (size, size), 0)
    right = lax.broadcasted_iota(jnp.int32, (size, size), 1)
    return jnp.sum(
        jnp.where(down == right, jnp.broadcast_to(column, (size, size)), 0.0), axis=0, keepdims=True
    )


def fold(values):
    total = values[:8]
    for k in range(1, values.shape[0] // 8):
        total = total + values[8 * k : 8 * k + 8]
    return total


def summed(values):
    return jnp.sum(values, axis=0, keepdims=True)


class Stored:
    def __init__(self, copy):
        self.drain = copy.wait


class Spots:
    def __init__(self, n, ctxn, tpn):
        self.n, self.ctxn, self.tpn = n, ctxn, tpn
        self.ctx = lax.axis_index("ctx")
        self.here = lax.axis_index("dp") * ctxn + self.ctx
        self.mine = lax.axis_index("tp")
        self.half = n // 2
        self.chip, self.core = lax.div(self.here, 2), lax.rem(self.here, 2)
        self.sibling = self.spot(2 * self.chip + 1 - self.core)
        self.group = [self.spot(lax.rem(self.here + step, n)) for step in range(1, n)]
        self.line = [{"tp": lax.rem(self.mine + step, tpn)} for step in range(1, tpn)]
        self.row = [{"ctx": lax.rem(self.ctx + step, ctxn)} for step in range(1, ctxn)]
        self.after = {"ctx": lax.rem(self.ctx + 1, ctxn)}
        self.before = {"ctx": lax.rem(self.ctx + ctxn - 1, ctxn)}

    def spot(self, index):
        return {"dp": lax.div(index, self.ctxn), "ctx": lax.rem(index, self.ctxn)}

    def across(self, step):
        return 2 * lax.rem(self.chip + step, self.half) + self.core


class Gather:
    def __init__(self, at, source, place, sems):
        self.at, self.source, self.place, self.sems = at, source, place, sems

    def launch(self):
        at, sems = self.at, self.sems
        here = self.place(at.here)
        self.own = pltpu.make_async_copy(self.source, here, sems.at[4, 0])
        self.own.start()
        self.copies = []
        for step in range(1, at.half):
            copy = send_to(
                self.source, here, sems.at[0, step], sems.at[1, step], at.spot(at.across(step))
            )
            copy.start()
            self.copies.append(copy)
        self.beside = send_to(self.source, here, sems.at[0, 0], sems.at[1, 0], at.sibling)
        self.beside.start()

    def relay(self):
        at, sems = self.at, self.sems
        self.passed = []
        for step in range(1, at.half):
            origin = self.place(at.across(at.half - step))
            self.copies[step - 1].wait_recv()
            copy = send_to(origin, origin, sems.at[2, step], sems.at[3, step], at.sibling)
            copy.start()
            self.passed.append(copy)

    def finish(self):
        self.own.wait()
        self.beside.wait_recv()
        for copy in self.passed:
            copy.wait_recv()

    def drain(self):
        self.beside.wait_send()
        for copy in self.copies + self.passed:
            copy.wait_send()


class Swap:
    def __init__(self, peers, places, slots, sems):
        self.copies = []
        for step, peer in enumerate(peers):
            copy = send_to(places(step), slots, sems.at[0, step], sems.at[1, step], peer)
            copy.start()
            self.copies.append(copy)

    def arrive(self):
        for copy in self.copies:
            copy.wait_recv()

    def drain(self):
        for copy in self.copies:
            copy.wait_send()


class Shift:
    def __init__(self, source, target, sems, peer, sends, receives):
        self.copy = send_to(source, target, sems.at[0], sems.at[1], peer)
        self.sends, self.receives = sends, receives

        @pl.when(sends)
        def _():
            self.copy.start()

    def arrive(self):
        @pl.when(self.receives)
        def _():
            self.copy.wait_recv()

    def drain(self):
        @pl.when(self.sends)
        def _():
            self.copy.wait_send()


class LineSum:
    def __init__(self, at, part, full, inbox, outbox, sems, chunk, finish):
        self.at, self.part, self.full, self.finish = at, part, full, finish
        self.inbox, self.outbox, self.sems, self.chunk = inbox, outbox, sems, chunk
        self.count = part.shape[0] // 2 // chunk
        tpn = at.tpn
        self.steps = self.count + HOP * (2 * tpn - 3)
        self.far = [tpn - 1 - at.mine, at.mine]
        up, down = {"tp": lax.rem(at.mine + 1, tpn)}, {"tp": lax.rem(at.mine + tpn - 1, tpn)}
        self.ahead, self.back = [down, up], [up, down]

    def rows(self, stream, j):
        return span(stream * self.count + j, self.chunk)

    def reduction(self, stream, j, source):
        return send_to(
            source,
            self.inbox.at[stream, j],
            self.sems.at[0, stream, j],
            self.sems.at[1, stream, j],
            self.ahead[stream],
        )

    def spreading(self, stream, j):
        where = self.full.at[self.rows(stream, j)]
        return send_to(
            where, where, self.sems.at[2, stream, j], self.sems.at[3, stream, j], self.back[stream]
        )

    def begin(self, stream):
        @pl.when(self.far[stream] == 0)
        def _():
            for j in range(self.count):
                self.reduction(stream, j, self.part.at[self.rows(stream, j)]).start()

    def tick(self, stream, t):
        if t < 0 or t >= self.steps:
            return
        far, tpn = self.far[stream], self.at.tpn
        j = t - HOP * (far - 1)

        @pl.when((far > 0) & (j >= 0) & (j < self.count))
        def _():
            rows = self.rows(stream, j)
            self.reduction(stream, j, self.outbox.at[stream, j]).wait_recv()
            total = (self.part[rows].astype(wide) + self.inbox[stream, j].astype(wide)).astype(low)

            @pl.when(far < tpn - 1)
            def _():
                self.outbox[stream, j] = total
                self.reduction(stream, j, self.outbox.at[stream, j]).start()

            @pl.when(far == tpn - 1)
            def _():
                self.full[rows] = total
                self.spreading(stream, j).start()
                self.finish(rows)

        i = t - HOP * (2 * tpn - 3 - far)

        @pl.when((far < tpn - 1) & (i >= 0) & (i < self.count))
        def _():
            self.spreading(stream, i).wait_recv()

            @pl.when(far > 0)
            def _():
                self.spreading(stream, i).start()

            self.finish(self.rows(stream, i))

    def drain(self):
        def one(j, carry):
            for stream in range(2):

                @pl.when(self.far[stream] < self.at.tpn - 1)
                def _():
                    self.reduction(stream, j, self.outbox.at[stream, j]).wait_send()

                @pl.when(self.far[stream] > 0)
                def _():
                    self.spreading(stream, j).wait_send()

            return carry

        each(self.count, one)


class Scatter:
    def __init__(self, at, slot, beside_buf, out_buf, in_buf, sems):
        self.at, self.slot, self.sems = at, slot, sems
        self.beside_buf, self.out_buf, self.in_buf = beside_buf, out_buf, in_buf

    def pair(self):
        at, sems = self.at, self.sems
        self.beside = {}
        for step in list(range(1, at.half)) + [0]:
            other = 2 * lax.rem(at.chip + step, at.half) + 1 - at.core
            copy = send_to(
                self.slot(other),
                self.beside_buf.at[step],
                sems.at[0, step],
                sems.at[1, step],
                at.sibling,
            )
            copy.start()
            self.beside[step] = copy

    def cross(self):
        at, sems = self.at, self.sems
        self.copies = []
        for step in range(1, at.half):
            target = at.across(step)
            self.beside[step].wait_recv()
            self.out_buf[step] = (
                self.slot(target)[...].astype(wide) + self.beside_buf[step].astype(wide)
            ).astype(low)
            copy = send_to(
                self.out_buf.at[step],
                self.in_buf.at[step],
                sems.at[2, step],
                sems.at[3, step],
                at.spot(target),
            )
            copy.start()
            self.copies.append(copy)

    def collect(self):
        at = self.at
        self.beside[0].wait_recv()
        total = self.slot(at.here)[...].astype(wide) + self.beside_buf[0].astype(wide)
        for step in range(1, at.half):
            self.copies[step - 1].wait_recv()
            total = total + self.in_buf[step].astype(wide)
        return total

    def drain(self):
        for copy in list(self.beside.values()) + self.copies:
            copy.wait_send()


def chained(slots, count, here, heads, backward):
    rows = slots.shape[1] - heads
    width, lanes = rows // heads, slots.shape[2]
    before = jnp.zeros((rows, lanes), wide)
    for k in range(count):
        at = count - 1 - k if backward else k
        reached = at > here if backward else at < here
        grown = tallen(jnp.exp(slots[at, rows:]), width, lanes)
        before = jnp.where(reached, slots[at, :rows] + grown * before, before)
    return before


def conv_block(source, start, rows, width, kernel, offset):
    taps = kernel.shape[0]
    around = source[pl.ds(start + HALO - 8, rows + 8), :width]
    total = offset
    for k in range(taps):
        first = 9 - taps + k
        total = total + kernel[k : k + 1] * around[first : first + rows]
    return total


def front(at, r, heads):
    length, width = r.tok.shape
    inner = r.x.shape[1]
    head = inner // heads
    state_width = r.state_t.shape[0]
    nstate = r.bc.shape[1] // 2
    rows, columns = r.in_w.shape[0], r.out_w.shape[1]
    size, count = STRETCH, length // STRETCH
    half_length = length // 2

    loads = [
        pltpu.make_async_copy(getattr(r, "h_" + name), getattr(r, name), r.load_sems.at[3 + k])
        for k, name in enumerate(SMALL_INPUTS)
    ]
    for copy in loads:
        copy.start()
    load = pltpu.make_async_copy(r.tokens, r.tok, r.load_sems.at[0])
    load.start()
    load_cot = pltpu.make_async_copy(r.cotangent, r.cot, r.load_sems.at[1])
    load_cot.start()
    load_out = pltpu.make_async_copy(r.out_w, r.out_v, r.load_sems.at[2])
    load_out.start()
    for copy in loads:
        copy.wait()
    for h in range(heads):
        r.skip_row[:, h * head : (h + 1) * head] = jnp.broadcast_to(
            r.skip_gain[:, h : h + 1], (1, head)
        )
    r.misc_own[...] = jnp.concatenate(
        [
            r.state_t[...].astype(wide),
            r.step_t[...].astype(wide),
            jnp.zeros((MISC - state_width - heads, rows), wide),
        ],
        axis=0,
    ).astype(low)

    line_up(at.group + at.line)

    g_in = Gather(at, r.in_w, lambda i: r.full_in.at[span(i, rows)], r.gather_sems.at[0])
    g_misc = Gather(at, r.misc_own, lambda i: r.misc_slots.at[i], r.gather_sems.at[1])
    g_gate = Gather(at, r.gate_w, lambda i: r.full_gate.at[span(i, rows)], r.gather_sems.at[2])
    g_out = Gather(
        at, r.out_own, lambda i: r.full_out.at[span(i, columns)], r.gather_sems.at[3]
    )
    g_misc.launch()
    g_in.launch()
    rim = Shift(
        r.tokens.at[pl.ds(length - HALO, HALO)],
        r.tok_rim,
        r.rim_sems,
        at.after,
        at.ctx < at.ctxn - 1,
        at.ctx > 0,
    )

    load.wait()
    gain = r.norm_gain[...]

    def normal(tokens):
        tokens = tokens.astype(wide)
        inv = lax.rsqrt(jnp.mean(tokens * tokens, axis=-1, keepdims=True) + epsilon)
        return (tokens * inv * gain).astype(low)

    def norm_block(i, carry):
        r.norm[pl.ds(pl.multiple_of(HALO + i * 32, 16), 32)] = normal(r.tok[span(i, 32)])
        return carry

    each(length // 32, norm_block)

    @pl.when(at.ctx == 0)
    def _():
        r.tok_rim[...] = jnp.zeros_like(r.tok_rim)

    rim.arrive()
    r.norm[:HALO] = normal(r.tok_rim[...])
    for k in range(length // LANES):
        r.norm_t[:, k * LANES : (k + 1) * LANES] = r.norm[
            HALO + k * LANES : HALO + (k + 1) * LANES
        ].T

    load_out.wait()
    r.out_own[...] = r.out_v[...].T
    g_misc.relay()
    g_in.relay()
    g_gate.launch()
    g_out.launch()
    g_misc.finish()
    for k in range(at.n):
        r.full_misc[:, k * rows : (k + 1) * rows] = r.misc_slots[k]
    r.sp[:, :MISC] = mm(r.norm[...], r.full_misc[...], ((1,), (1,)))

    acts = []
    for k in range(2):
        pre = conv_block(
            r.sp, k * half_length, half_length, state_width, r.state_kernel, r.state_offset[...]
        )
        sig = jax.nn.sigmoid(pre)
        act = pre * sig
        r.dsil_st[k * half_length : (k + 1) * half_length] = sig + act * (1.0 - sig)
        acts.append(act)
    packed = jnp.concatenate(acts, axis=1).astype(low)
    r.bc_own[...] = packed
    r.bc_all[at.mine] = packed
    bc_swap = Swap(at.line, lambda k: r.bc_own, r.bc_all.at[at.mine], r.bc_sems)

    g_in.finish()
    r.xp[...] = mm(r.norm[...], r.full_in[...], ((1,), (0,)))

    step_row = r.sp[HALO:, state_width : state_width + heads].T + turned(r.step_bias[...])
    dt_row = jnp.maximum(step_row, 0.0) + jnp.log1p(jnp.exp(-jnp.abs(step_row)))
    r.sig_row[...] = jax.nn.sigmoid(step_row)
    r.dt_row[...] = dt_row
    decays = -dt_row * turned(jnp.exp(r.decay_log[...]))
    r.decays[...] = decays
    causal = causal_mask(size)
    ones = jnp.where(causal, 1.0, 0.0)
    totals = []
    for s in range(count):
        cut = slice(s * size, (s + 1) * size)
        run = mm(decays[:, cut], ones, ((1,), (1,)), exact_mode)
        r.run_row[:, cut] = run
        total = run[:, size - 1 :]
        totals.append(total)
        left = jnp.exp(total - run)
        dts = dt_row[:, cut]
        r.cols[cut, : 5 * heads] = jnp.concatenate(
            [run, dts, left * dts, jnp.exp(run), left], axis=0
        ).T

    def value_block(i, carry):
        start = pl.multiple_of(i * 32, 32)
        pre = conv_block(r.xp, start, 32, inner, r.input_kernel, r.input_offset[...])
        sig = jax.nn.sigmoid(pre)
        act = pre * sig
        r.x[pl.ds(start, 32)] = act
        r.dsil_in[pl.ds(start, 32)] = sig + act * (1.0 - sig)
        return carry

    each(length // 32, value_block)

    bc_swap.arrive()
    for k in range(at.tpn):
        both = r.bc_all[k]
        for j in range(2):
            r.bc[
                j * half_length : (j + 1) * half_length, k * state_width : (k + 1) * state_width
            ] = both[:, j * state_width : (j + 1) * state_width]

    fresh = []
    state = jnp.zeros((inner, nstate), wide)
    for s in range(count):
        cut = slice(s * size, (s + 1) * size)
        tail = widen(r.cols[cut, 2 * heads : 3 * heads], head)
        added = mm((r.x[cut] * tail).astype(low), r.bc[cut, :nstate], ((0,), (0,)))
        r.fresh[s] = added
        state = tallen(jnp.exp(totals[s]), head, nstate) * state + added
    logs = jnp.broadcast_to(sum(totals), (heads, nstate))
    r.chain_own[:inner] = state
    r.chain_own[inner:] = logs
    r.chain_all[at.ctx] = r.chain_own[...]
    chain = Swap(at.row, lambda k: r.chain_own, r.chain_all.at[at.ctx], r.chain_sems)

    g_gate.relay()
    for s in range(count):
        cut = slice(s * size, (s + 1) * size)
        scores = mm(r.bc[cut, nstate:], r.bc[cut, :nstate], ((1,), (1,)))
        r.scores[s] = scores
        run = r.cols[cut, :heads]
        for h in range(0, heads, 2):
            pair = []
            for k in (h, h + 1):
                fall = jnp.exp(
                    jnp.where(causal, run[:, k : k + 1] - r.run_row[k : k + 1, cut], -1e30)
                )
                mixing = (fall * scores * r.dt_row[k : k + 1, cut]).astype(low)
                x_low = r.x[cut, k * head : (k + 1) * head].astype(low)
                pair.append(mm(mixing, x_low, ((1,), (0,))))
            r.scanned[cut, h * head : (h + 2) * head] = jnp.concatenate(pair, axis=1)
        if s == 0:
            g_gate.finish()
            r.gate[...] = mm(r.norm[HALO:], r.full_gate[...], ((1,), (0,)))
            g_out.relay()

    g_out.finish()
    load_cot.wait()
    r.pull[...] = mm(r.cot[...], r.full_out[...], ((1,), (0,)))

    chain.arrive()
    state = chained(r.chain_all, at.ctxn, at.ctx, heads, False)
    for s in range(count):
        cut = slice(s * size, (s + 1) * size)
        kept = state.astype(low)
        r.kept[s] = kept
        if s + 1 < count:
            state = tallen(jnp.exp(totals[s]), head, nstate) * state + r.fresh[s]
        grown = widen(r.cols[cut, 3 * heads : 4 * heads], head)
        r.carried[cut] = mm(r.bc[cut, nstate:], kept, ((1,), (1,))) * grown

    def gate_block(i, carry):
        here = span(i, 32)
        gate = r.gate[here]
        sig = jax.nn.sigmoid(gate)
        scanned = r.scanned[here] + r.carried[here] + r.skip_row[...] * r.x[here]
        r.scanned[here] = scanned
        gated = scanned * (gate * sig)
        scaled = (gated * r.gated_gain[...]).astype(low)
        r.scaled[here] = scaled
        squares = jnp.sum(gated * gated, axis=1, keepdims=True)
        dots = jnp.sum(scaled.astype(wide) * r.pull[here], axis=1, keepdims=True)
        r.stat[here] = jnp.concatenate([squares, dots, jnp.zeros((32, 6), wide)], axis=1)
        return carry

    each(length // 32, gate_block)
    mine = r.stat[...].T
    r.stat_own[...] = mine
    r.stat_all[at.mine] = mine
    stats = Swap(at.line, lambda k: r.stat_own, r.stat_all.at[at.mine], r.stat_sems)
    r.po[...] = mm(r.scaled[...], r.full_out[...], ((1,), (1,))).astype(low)
    stats.arrive()
    total = r.stat_all[0]
    for k in range(1, at.tpn):
        total = total + r.stat_all[k]
    channels = inner * at.tpn
    inv = lax.rsqrt(total[0:1] / channels + epsilon)
    rms = -0.5 * inv * inv * inv * total[1:2] / channels
    r.inv[...] = jnp.concatenate([inv, rms, jnp.zeros((6, length), wide)], axis=0).T
    return [g_in, g_misc, g_gate, g_out, rim, bc_swap, chain, stats]


def back(at, r, heads):
    length, width = r.tok.shape
    inner = r.x.shape[1]
    head = inner // heads
    state_width = r.state_t.shape[0]
    nstate = r.bc.shape[1] // 2
    rows, columns = r.in_w.shape[0], r.out_w.shape[1]
    taps = r.input_kernel.shape[0]
    size, count = STRETCH, length // STRETCH
    half_length = length // 2
    causal = causal_mask(size)
    ones = jnp.where(causal, 1.0, 0.0)
    drains = []

    def store(name):
        index = STORES.index(name)
        copy = pltpu.make_async_copy(
            getattr(r, "v_" + name), getattr(r, "o_" + name), r.store_sems.at[index]
        )
        copy.start()
        drains.append(Stored(copy))

    def block_rows(here):
        r.v_block[here] = (
            r.tok[here].astype(wide) + r.inv[here, 0:1] * r.po_full[here].astype(wide)
        ).astype(low)

    out_sum = LineSum(at, r.po, r.po_full, r.po_in, r.po_out, r.po_sems, CHUNK, block_rows)
    out_ticks = iter(range(out_sum.steps))

    def serve():
        t = next(out_ticks, None)
        if t is None:
            return False
        for stream in range(2):
            out_sum.tick(stream, t)
        return True

    for stream in range(2):
        out_sum.begin(stream)
    def grad_block(i, carry):
        gains, skips = carry
        here = span(i, 32)
        inv, rms = r.inv[here, 0:1], r.inv[here, 1:2]
        gate, scanned = r.gate[here], r.scanned[here]
        sig = jax.nn.sigmoid(gate)
        silu = gate * sig
        gated = scanned * silu
        scaled_grad = inv * r.pull[here]
        gains = gains + fold(scaled_grad * gated)
        gated_grad = scaled_grad * r.gated_gain[...] + 2.0 * rms * gated
        dy = gated_grad * silu
        r.dy[here] = dy
        r.gate_low[here] = (gated_grad * scanned * (sig + silu * (1.0 - sig))).astype(low)
        skips = skips + fold(dy * r.x[here])
        r.proj_grad[here] = (inv * r.cot[here].astype(wide)).astype(low)
        return gains, skips

    zero = jnp.zeros((8, inner), wide)
    gains, skips = each(length // 32, grad_block, (zero, zero))
    gain_row, skip_row = summed(gains), per_head(summed(skips), heads)

    serve()
    state = jnp.zeros((inner, nstate), wide)
    totals = [r.run_row[:, (s + 1) * size - 1 : (s + 1) * size] for s in range(count)]
    for s in reversed(range(count)):
        cut = slice(s * size, (s + 1) * size)
        grown = widen(r.cols[cut, 3 * heads : 4 * heads], head)
        dy_grown = r.dy[cut] * grown
        dy_low = dy_grown.astype(low)
        added = mm(dy_low, r.bc[cut, nstate:], ((0,), (0,)))
        r.fresh[s] = added
        state = tallen(jnp.exp(totals[s]), head, nstate) * state + added
        kept = r.kept[s]
        r.dyc[cut] = per_head(dy_grown * mm(r.bc[cut, nstate:], kept, ((1,), (1,))), heads)
        r.dbc[cut, nstate:] = mm(dy_low, kept, ((1,), (0,)))
        serve()
    r.turn_own[:inner] = state
    r.turn_own[inner:] = jnp.broadcast_to(sum(totals), (heads, nstate))
    r.turn_all[at.ctx] = r.turn_own[...]
    chain = Swap(at.row, lambda k: r.turn_own, r.turn_all.at[at.ctx], r.turn_sems)
    drains.append(chain)

    serve()
    r.g_gate[...] = mm(r.norm_t[...], r.gate_low[...], ((1,), (0,))).astype(low)
    s_gate = Scatter(
        at,
        lambda i: r.g_gate.at[span(i, rows)],
        r.gate_b,
        r.gate_o,
        r.gate_i,
        r.scatter_sems.at[0],
    )
    s_gate.pair()
    serve()
    for k in range(length // LANES):
        r.proj_t[:, k * LANES : (k + 1) * LANES] = r.proj_grad[k * LANES : (k + 1) * LANES].T
    r.g_out[...] = mm(r.proj_t[...], r.scaled[...], ((1,), (0,))).astype(low)
    s_out = Scatter(
        at,
        lambda i: r.g_out.at[span(i, columns)],
        r.out_b,
        r.out_o,
        r.out_i,
        r.scatter_sems.at[1],
    )
    s_out.pair()
    serve()
    s_gate.cross()
    s_out.cross()

    for s in reversed(range(count)):
        cut = slice(s * size, (s + 1) * size)
        b, c = r.bc[cut, :nstate], r.bc[cut, nstate:]
        run = r.cols[cut, :heads]
        scores = r.scores[s]
        dscores = jnp.zeros((size, size), wide)
        across, down = [], []
        for h in range(0, heads, 2):
            pair = []
            for k in (h, h + 1):
                lanes = slice(k * head, (k + 1) * head)
                fall = jnp.exp(
                    jnp.where(causal, run[:, k : k + 1] - r.run_row[k : k + 1, cut], -1e30)
                )
                dt = r.dt_row[k : k + 1, cut]
                dy_low = r.dy[cut, lanes].astype(low)
                products = mm(dy_low, r.x[cut, lanes].astype(low), ((1,), (1,))) * fall
                dscores = dscores + products * dt
                terms = products * scores
                down.append(jnp.sum(terms, axis=0, keepdims=True))
                across.append(jnp.sum(terms * dt, axis=1, keepdims=True))
                mixing = (fall * scores * dt).astype(low)
                pair.append(mm(mixing, dy_low, ((0,), (0,))))
            r.dx[cut, h * head : (h + 2) * head] = jnp.concatenate(pair, axis=1)
            serve()
        dscores = dscores.astype(low)
        r.dbc[cut, :nstate] = mm(dscores, c, ((0,), (0,)))
        r.dbc[cut, nstate:] += mm(dscores, b, ((1,), (0,)))
        r.down[:, cut] = jnp.concatenate(down, axis=0)
        r.dyc[cut] += jnp.concatenate(across, axis=1)

    chain.arrive()
    state = chained(r.turn_all, at.ctxn, at.ctx, heads, True)
    decay_rates = turned(jnp.exp(r.decay_log[...]))
    bias_grad = jnp.zeros((heads, 1), wide)
    decay_grad = jnp.zeros((heads, 1), wide)
    for s in reversed(range(count)):
        cut = slice(s * size, (s + 1) * size)
        state_low = state.astype(low)
        x = r.x[cut]
        spare = widen(r.cols[cut, 2 * heads : 3 * heads], head)
        fade = widen(r.cols[cut, 4 * heads : 5 * heads], head)
        pulled = mm(r.bc[cut, :nstate], state_low, ((1,), (1,)))
        r.dbc[cut, :nstate] += mm((x * spare).astype(low), state_low, ((1,), (0,)))
        tail_grad = per_head(x * fade * pulled, heads)
        r.dx[cut] += spare * pulled + r.skip_row[...] * r.dy[cut]
        shrink = tallen(jnp.exp(totals[s]), head, nstate)
        lost = shrink * state * r.kept[s].astype(wide)
        lost = jnp.concatenate(
            [summed(lost[h * head : (h + 1) * head]) for h in range(heads)], axis=0
        )
        both = jnp.concatenate([tail_grad, r.dyc[cut]], axis=1).T
        tail_row, drun = both[:heads], both[heads:]
        dt, down = r.dt_row[:, cut], r.down[:, cut]
        out_tail = tail_row * dt
        drun = drun - out_tail - down * dt
        dtotal = jnp.sum(lost, axis=1, keepdims=True) + jnp.sum(out_tail, axis=1, keepdims=True)
        ddecay = dtotal + mm(drun, ones, ((1,), (0,)), exact_mode)
        step_grad = (down + tail_row - ddecay * decay_rates) * r.sig_row[:, cut]
        bias_grad = bias_grad + jnp.sum(step_grad, axis=1, keepdims=True)
        decay_grad = decay_grad + jnp.sum(ddecay * r.decays[:, cut], axis=1, keepdims=True)
        r.step_cols[cut] = step_grad.T
        if s > 0:
            state = shrink * state + r.fresh[s]

    for k in range(at.tpn):
        piece = [
            r.dbc[j * half_length : (j + 1) * half_length, k * state_width : (k + 1) * state_width]
            for j in range(2)
        ]
        r.ds_own[k] = jnp.concatenate(piece, axis=1).astype(low)
    turn = Swap(
        at.line,
        lambda k: r.ds_own.at[lax.rem(at.mine + k + 1, at.tpn)],
        r.ds_all.at[at.mine],
        r.ds_sems,
    )
    drains.append(turn)
    r.ds_all[at.mine] = r.ds_own[at.mine]

    r.dp[:length] = r.dx[...] * r.dsil_in[...]
    is_last, is_first = at.ctx == at.ctxn - 1, at.ctx == 0

    @pl.when(is_last)
    def _():
        r.dp[length:] = jnp.zeros((8, inner), wide)
        r.dps[length:] = jnp.zeros((8, state_width), wide)

    in_rim = Shift(
        r.dp.at[pl.ds(0, 8)],
        r.dp.at[pl.ds(length, 8)],
        r.back_sems.at[0],
        at.before,
        jnp.logical_not(is_first),
        jnp.logical_not(is_last),
    )
    drains.append(in_rim)
    serve()

    def tap_block(i, carry):
        around = r.xp[pl.ds(pl.multiple_of(i * 32, 32) + HALO - 8, 40)]
        grad = r.dp[span(i, 32)]
        out = [carry[0] + fold(grad)]
        for k in range(taps):
            first = 9 - taps + k
            out.append(carry[1 + k] + fold(grad * around[first : first + 32]))
        return tuple(out)

    tap_sums = each(length // 32, tap_block, (zero,) * (1 + taps))
    tap_sums = [summed(value) for value in tap_sums]
    in_rim.arrive()

    def input_block(i, carry):
        around = r.dp[pl.ds(pl.multiple_of(i * 32, 32), 40)]
        total = r.input_kernel[taps - 1 : taps] * around[:32]
        for k in range(taps - 1):
            total = total + r.input_kernel[k : k + 1] * around[taps - 1 - k : taps - 1 - k + 32]
        r.input_low[span(i, 32)] = total.astype(low)
        return carry

    each(length // 32, input_block)
    serve()
    r.g_in[...] = mm(r.norm_t[...], r.input_low[...], ((1,), (0,))).astype(low)
    s_in = Scatter(
        at, lambda i: r.g_in.at[span(i, rows)], r.in_b, r.in_o, r.in_i, r.scatter_sems.at[2]
    )
    s_in.pair()
    serve()

    turn.arrive()
    mine = r.ds_all[0].astype(wide)
    for k in range(1, at.tpn):
        mine = mine + r.ds_all[k].astype(wide)
    for k in range(2):
        cut = slice(k * half_length, (k + 1) * half_length)
        r.dps[cut] = mine[:, k * state_width : (k + 1) * state_width] * r.dsil_st[cut]
    st_rim = Shift(
        r.dps.at[pl.ds(0, 8)],
        r.dps.at[pl.ds(length, 8)],
        r.back_sems.at[1],
        at.before,
        jnp.logical_not(is_first),
        jnp.logical_not(is_last),
    )
    drains.append(st_rim)
    s_in.cross()
    st_grad = r.dps[:length]
    st_sums = [summed(st_grad)]
    for k in range(taps):
        first = HALO + 1 - taps + k
        st_sums.append(summed(st_grad * r.sp[first : first + length, :state_width]))
    r.np_[...] = mm(r.gate_low[...], r.full_gate[...], ((1,), (1,)))
    serve()
    st_rim.arrive()
    total = r.state_kernel[taps - 1 : taps] * r.dps[:length]
    for k in range(taps - 1):
        first = taps - 1 - k
        total = total + r.state_kernel[k : k + 1] * r.dps[first : first + length]
    r.misc_low[...] = jnp.concatenate(
        [total, r.step_cols[...], jnp.zeros((length, MISC - state_width - heads), wide)], axis=1
    ).astype(low)
    while serve():
        pass
    store("block")

    def token_rows(here):
        tokens = r.tok[here].astype(wide)
        inv = lax.rsqrt(jnp.mean(tokens * tokens, axis=-1, keepdims=True) + epsilon)
        scaled = r.npl_full[here].astype(wide) * r.norm_gain[...]
        along = jnp.mean(scaled * tokens, axis=-1, keepdims=True)
        r.v_tokens[here] = (
            r.cot[here].astype(wide) + inv * scaled - tokens * (inv * inv * inv * along)
        )

    norm_sum = LineSum(
        at, r.npl, r.npl_full, r.npl_in, r.npl_out, r.npl_sems, CHUNK, token_rows
    )
    norm_ticks = iter(range(norm_sum.steps))

    def tail():
        t = next(norm_ticks, None)
        if t is None:
            return False
        for stream in range(2):
            norm_sum.tick(stream, t)
        return True

    gain_sums = jnp.zeros((8, width), wide)
    for k in reversed(range(2)):
        cut = slice(k * half_length, (k + 1) * half_length)
        r.np_[cut] += mm(r.input_low[cut], r.full_in[...], ((1,), (1,))) + mm(
            r.misc_low[cut], r.full_misc[...], ((1,), (0,))
        )

        def part_block(i, carry):
            here = pl.ds(pl.multiple_of(k * half_length + i * 32, 32), 32)
            tokens = r.tok[here].astype(wide)
            inv = lax.rsqrt(jnp.mean(tokens * tokens, axis=-1, keepdims=True) + epsilon)
            value = r.np_[here]
            r.npl[here] = value.astype(low)
            return carry + fold(value * (tokens * inv))

        gain_sums = each(half_length // 32, part_block, gain_sums)
        norm_sum.begin(k)
    gain_part = summed(gain_sums)
    tail()

    grads = mm(r.misc_low[...], r.norm[HALO:], ((0,), (0,))).astype(low)
    for k in range(at.n):
        r.g_misc[k] = grads[:, k * rows : (k + 1) * rows]
    s_misc = Scatter(
        at, lambda i: r.g_misc.at[i], r.misc_b, r.misc_o, r.misc_i, r.scatter_sems.at[3]
    )
    s_misc.pair()

    r.small[...] = jnp.zeros_like(r.small)

    def put(row, values):
        lanes = values.shape[1]
        for k in range(-(-lanes // LANES)):
            stop = min(LANES, lanes - k * LANES)
            r.small[row + k : row + k + 1, :stop] = values[:, k * LANES : k * LANES + stop]

    per_row = inner // LANES
    place = {}
    at_row = 0
    for name, values in (
        [("gain", gain_part)]
        + [("in%d" % k, tap_sums[1 + k]) for k in range(taps)]
        + [("inoff", tap_sums[0]), ("gated", gain_row)]
        + [("st%d" % k, st_sums[1 + k]) for k in range(taps)]
        + [("stoff", st_sums[0]), ("skip", skip_row)]
        + [("bias", laid(bias_grad)), ("decay", laid(decay_grad))]
    ):
        place[name] = (at_row, values.shape[1])
        put(at_row, values)
        at_row += -(-values.shape[1] // LANES)
    r.small_in[at.here] = r.small[...]
    smalls = Swap(at.group, lambda k: r.small, r.small_in.at[at.here], r.small_sems)
    drains.append(smalls)
    tail()
    s_misc.cross()

    r.v_gate[...] = s_gate.collect()
    store("gate")
    tail()
    r.v_out[...] = s_out.collect().T
    store("out")
    tail()

    smalls.arrive()
    total = r.small_in[0]
    for k in range(1, at.n):
        total = total + r.small_in[k]
    r.total[...] = total
    gain_rows = width // LANES
    r.gain_own[...] = total[:gain_rows]
    r.gain_all[at.mine] = total[:gain_rows]
    gains = Swap(at.line, lambda k: r.gain_own, r.gain_all.at[at.mine], r.gain_sems)
    drains.append(gains)

    def get(name):
        row, lanes = place[name]
        return [
            r.total[row + k : row + k + 1, : min(LANES, lanes - k * LANES)]
            for k in range(-(-lanes // LANES))
        ]

    def lay(target, row, name):
        for k, value in enumerate(get(name)):
            target[row : row + 1, k * LANES : k * LANES + value.shape[1]] = value

    for k in range(taps):
        lay(r.v_in_kernel, k, "in%d" % k)
        lay(r.v_st_kernel, k, "st%d" % k)
    lay(r.v_in_offset, 0, "inoff")
    lay(r.v_st_offset, 0, "stoff")
    lay(r.v_gated, 0, "gated")
    lay(r.v_skip, 0, "skip")
    lay(r.v_bias, 0, "bias")
    lay(r.v_decay, 0, "decay")
    store("in_kernel")
    store("st_kernel")
    store("in_offset")
    store("st_offset")
    store("gated")
    store("skip")
    store("bias")
    store("decay")

    tail()

    tail()
    r.v_in[...] = s_in.collect()
    store("in")
    tail()
    misc = s_misc.collect()
    r.v_state[...] = misc[:state_width]
    r.v_step[...] = misc[state_width : state_width + heads]
    store("state")
    store("step")
    tail()
    gains.arrive()
    total = r.gain_all[0]
    for k in range(1, at.tpn):
        total = total + r.gain_all[k]
    r.v_gain[...] = total
    store("gain")

    while tail():
        pass
    store("tokens")

    for scatter in (s_gate, s_out, s_in, s_misc):
        scatter.drain()
    out_sum.drain()
    norm_sum.drain()
    return drains


def whole_kernel(n, ctxn, tpn, heads, names, *refs):
    r = SimpleNamespace(**dict(zip(names, refs)))
    r.dx, r.dy, r.np_ = r.carried, r.pull, r.v_tokens
    at = Spots(n, ctxn, tpn)
    drains = front(at, r, heads)
    drains += back(at, r, heads)
    for item in drains:
        item.drain()


def emit_kernel(count, *refs):
    sources, targets, sems = refs[:count], refs[count : 2 * count], refs[2 * count]
    copies = [
        pltpu.make_async_copy(source, target, sems.at[k])
        for k, (source, target) in enumerate(zip(sources, targets))
    ]
    for copy in copies:
        copy.start()
    for copy in copies:
        copy.wait()


def emit(arrays):
    count = len(arrays)
    return pl.pallas_call(
        functools.partial(emit_kernel, count),
        out_shape=tuple(jax.ShapeDtypeStruct(a.shape, a.dtype) for a in arrays),
        in_specs=[pl.BlockSpec(memory_space=pl.ANY)] * count,
        out_specs=(pl.BlockSpec(memory_space=pl.ANY),) * count,
        scratch_shapes=[pltpu.SemaphoreType.DMA((count,))],
        compiler_params=pltpu.CompilerParams(vmem_limit_bytes=8 * 2**20),
    )(*arrays)


def per_device(
    tokens,
    norm_gain,
    gate_weight,
    input_weight,
    state_weight,
    step_weight,
    input_kernel,
    input_offset,
    state_kernel,
    state_offset,
    step_bias,
    decay_log,
    skip_gain,
    gated_gain,
    out_weight,
    cotangent,
):
    ctxn = lax.axis_size("ctx")
    n, tpn = lax.axis_size("dp") * ctxn, lax.axis_size("tp")
    length, width = tokens.shape
    rows, inner = input_weight.shape
    state_width, heads = state_weight.shape[1], step_weight.shape[1]
    columns = out_weight.shape[1]
    nstate = state_width * tpn // 2
    head = inner // heads
    taps = input_kernel.shape[0]
    count = length // STRETCH
    half = n // 2
    steps = length // 2 // CHUNK
    hl = length // 2
    row = lambda a: a.reshape(1, a.shape[0])
    inputs = dict(
        tokens=tokens,
        cotangent=cotangent,
        in_w=input_weight,
        gate_w=gate_weight,
        out_w=out_weight,
        h_state_t=state_weight.T,
        h_step_t=step_weight.T,
        h_norm_gain=row(norm_gain),
        h_input_kernel=input_kernel,
        h_input_offset=row(input_offset),
        h_state_kernel=state_kernel,
        h_state_offset=row(state_offset),
        h_step_bias=row(step_bias),
        h_decay_log=row(decay_log),
        h_skip_gain=row(skip_gain),
        h_gated_gain=row(gated_gain),
    )
    outputs = dict(
        o_block=((length, width), low),
        o_tokens=((length, width), wide),
        o_gain=((width // LANES, LANES), wide),
        o_gate=((rows, inner), wide),
        o_in=((rows, inner), wide),
        o_state=((state_width, rows), wide),
        o_step=((heads, rows), wide),
        o_in_kernel=((taps, inner), wide),
        o_in_offset=((1, inner), wide),
        o_st_kernel=((taps, state_width), wide),
        o_st_offset=((1, state_width), wide),
        o_bias=((1, heads), wide),
        o_decay=((1, heads), wide),
        o_skip=((1, heads), wide),
        o_gated=((1, inner), wide),
        o_out=((inner, columns), wide),
    )
    small_rows = width // LANES + (taps + 2) * inner // LANES + (taps + 1) + 3
    small_rows = -(-small_rows // 8) * 8
    both = (length, inner)
    scratch = {
        name: (inputs["h_" + name].shape, inputs["h_" + name].dtype) for name in SMALL_INPUTS
    }
    scratch.update({"v" + name[1:]: value for name, value in outputs.items()})
    scratch.update(
        skip_row=((1, inner), wide),
        tok=((length, width), low),
        cot=((length, width), low),
        tok_rim=((HALO, width), low),
        misc_own=((MISC, rows), low),
        norm=((HALO + length, width), low),
        norm_t=((width, length), low),
        full_in=((width, inner), low),
        full_gate=((width, inner), low),
        full_misc=((MISC, width), low),
        full_out=((width, inner), low),
        out_v=((inner, columns), low),
        out_own=((columns, inner), low),
        misc_slots=((n, MISC, rows), low),
        sp=((HALO + length, LANES), wide),
        dsil_st=((length, state_width), wide),
        bc_own=((hl, 2 * state_width), low),
        bc_all=((tpn, hl, 2 * state_width), low),
        bc=((length, 2 * nstate), low),
        xp=((HALO + length, inner), wide),
        x=(both, wide),
        dsil_in=(both, wide),
        sig_row=((heads, length), wide),
        dt_row=((heads, length), wide),
        decays=((heads, length), wide),
        run_row=((heads, length), wide),
        cols=((length, 5 * heads), wide),
        fresh=((count, inner, nstate), wide),
        chain_own=((inner + heads, nstate), wide),
        chain_all=((ctxn, inner + heads, nstate), wide),
        turn_own=((inner + heads, nstate), wide),
        turn_all=((ctxn, inner + heads, nstate), wide),
        scores=((count, STRETCH, STRETCH), wide),
        scanned=(both, wide),
        carried=(both, wide),
        gate=(both, wide),
        pull=(both, wide),
        kept=((count, inner, nstate), low),
        scaled=(both, low),
        proj_t=((width, length), low),
        stat=((length, 8), wide),
        stat_own=((8, length), wide),
        stat_all=((tpn, 8, length), wide),
        inv=((length, 8), wide),
        po=((length, width), low),
        po_full=((length, width), low),
        po_in=((2, steps, CHUNK, width), low),
        po_out=((2, steps, CHUNK, width), low),
        gate_low=(both, low),
        proj_grad=((length, width), low),
        dyc=((length, heads), wide),
        dbc=((length, 2 * nstate), wide),
        g_gate=((width, inner), low),
        gate_b=((half, rows, inner), low),
        gate_o=((half, rows, inner), low),
        gate_i=((half, rows, inner), low),
        g_in=((width, inner), low),
        in_b=((half, rows, inner), low),
        in_o=((half, rows, inner), low),
        in_i=((half, rows, inner), low),
        g_out=((width, inner), low),
        out_b=((half, columns, inner), low),
        out_o=((half, columns, inner), low),
        out_i=((half, columns, inner), low),
        g_misc=((n, MISC, rows), low),
        misc_b=((half, MISC, rows), low),
        misc_o=((half, MISC, rows), low),
        misc_i=((half, MISC, rows), low),
        down=((heads, length), wide),
        step_cols=((length, heads), wide),
        ds_own=((tpn, hl, 2 * state_width), low),
        ds_all=((tpn, hl, 2 * state_width), low),
        dp=((length + 8, inner), wide),
        dps=((length + 8, state_width), wide),
        input_low=(both, low),
        misc_low=((length, MISC), low),
        npl=((length, width), low),
        npl_full=((length, width), low),
        npl_in=((2, steps, CHUNK, width), low),
        npl_out=((2, steps, CHUNK, width), low),
        small=((small_rows, LANES), wide),
        small_in=((n, small_rows, LANES), wide),
        total=((small_rows, LANES), wide),
        gain_own=((width // LANES, LANES), wide),
        gain_all=((tpn, width // LANES, LANES), wide),
    )
    sems = dict(
        store_sems=(len(STORES),),
        load_sems=(3 + len(SMALL_INPUTS),),
        gather_sems=(4, 5, half),
        rim_sems=(2,),
        bc_sems=(2, tpn),
        chain_sems=(2, ctxn),
        turn_sems=(2, ctxn),
        stat_sems=(2, tpn),
        po_sems=(4, 2, steps),
        npl_sems=(4, 2, steps),
        scatter_sems=(4, 4, half),
        ds_sems=(2, tpn),
        back_sems=(2, 2),
        small_sems=(2, n),
        gain_sems=(2, tpn),
    )
    names = list(inputs) + list(outputs) + list(scratch) + list(sems)
    results = pl.pallas_call(
        functools.partial(whole_kernel, n, ctxn, tpn, heads, names),
        out_shape=tuple(jax.ShapeDtypeStruct(*o) for o in outputs.values()),
        in_specs=[pl.BlockSpec(memory_space=pl.ANY)] * len(inputs),
        out_specs=(pl.BlockSpec(memory_space=pl.ANY),) * len(outputs),
        scratch_shapes=[pltpu.VMEM(*s) for s in scratch.values()]
        + [pltpu.SemaphoreType.DMA(s) for s in sems.values()],
        compiler_params=pltpu.CompilerParams(
            collective_id=0, has_side_effects=True, vmem_limit_bytes=62 * 2**20
        ),
    )(*inputs.values())
    o = SimpleNamespace(**dict(zip(outputs, emit(results))))
    return (
        o.o_block,
        o.o_tokens,
        o.o_gain.reshape(-1),
        o.o_gate,
        o.o_in,
        o.o_state.T,
        o.o_step.T,
        o.o_in_kernel,
        o.o_in_offset.reshape(-1),
        o.o_st_kernel,
        o.o_st_offset.reshape(-1),
        o.o_bias.reshape(-1),
        o.o_decay.reshape(-1),
        o.o_skip.reshape(-1),
        o.o_gated.reshape(-1),
        o.o_out,
    )


def solution(mesh):
    placed = (
        P(("dp", "ctx"), None),
        P(),
        P(("dp", "ctx"), "tp"),
        P(("dp", "ctx"), "tp"),
        P(("dp", "ctx"), "tp"),
        P(("dp", "ctx"), "tp"),
        P(None, "tp"),
        P("tp"),
        P(None, "tp"),
        P("tp"),
        P("tp"),
        P("tp"),
        P("tp"),
        P("tp"),
        P("tp", ("dp", "ctx")),
        P(("dp", "ctx"), None),
    )
    return jax.shard_map(
        per_device,
        mesh=mesh,
        in_specs=placed,
        out_specs=(
            P(("dp", "ctx"), None),
            P(("dp", "ctx"), None),
            P(),
            P(("dp", "ctx"), "tp"),
            P(("dp", "ctx"), "tp"),
            P(("dp", "ctx"), "tp"),
            P(("dp", "ctx"), "tp"),
            P(None, "tp"),
            P("tp"),
            P(None, "tp"),
            P("tp"),
            P("tp"),
            P("tp"),
            P("tp"),
            P("tp"),
            P("tp", ("dp", "ctx")),
        ),
        check_vma=False,
    )
```

```python
import functools
from types import SimpleNamespace

import jax
import jax.numpy as jnp
from jax import lax
from jax.experimental import pallas as pl
from jax.experimental.pallas import tpu as pltpu
from jax.sharding import PartitionSpec as P

STRETCH = 128
LANES = 128
HALO = 16
MISC = 80
PAD = 16
CHUNK = 32
LEAD = 2
STORES = (
    "block",
    "tokens",
    "gain",
    "gate",
    "in",
    "state",
    "step",
    "in_kernel",
    "in_offset",
    "st_kernel",
    "st_offset",
    "bias",
    "decay",
    "skip",
    "gated",
    "out",
)
SMALL_INPUTS = (
    "state_t",
    "step_t",
    "norm_gain",
    "input_kernel",
    "input_offset",
    "state_kernel",
    "state_offset",
    "step_bias",
    "decay_log",
    "skip_gain",
    "gated_gain",
)
epsilon = 1e-05
exact_mode = lax.Precision.HIGHEST
MESH = pl.DeviceIdType.MESH
low = jnp.bfloat16
wide = jnp.float32


def mm(left, right, dims, precision=None):
    return lax.dot_general(
        left, right, (dims, ((), ())), precision=precision, preferred_element_type=wide
    )


def line_up(peers):
    barrier = pltpu.get_barrier_semaphore()
    for peer in peers:
        pl.semaphore_signal(barrier, inc=1, device_id=peer, device_id_type=MESH)
    pl.semaphore_wait(barrier, len(peers))


def send_to(source, target, sends, recvs, peer):
    return pltpu.make_async_remote_copy(
        src_ref=source,
        dst_ref=target,
        send_sem=sends,
        recv_sem=recvs,
        device_id=peer,
        device_id_type=MESH,
    )


def span(index, size):
    return pl.ds(pl.multiple_of(index * size, size), size)


def each(count, body, carry=None):
    def step(i, carry):
        return body(i, carry)

    return lax.fori_loop(0, count, step, carry)


def causal_mask(size):
    down = lax.broadcasted_iota(jnp.int32, (size, size), 0)
    right = lax.broadcasted_iota(jnp.int32, (size, size), 1)
    return down >= right


def widen(columns, width):
    rows, heads = columns.shape
    return jnp.concatenate(
        [jnp.broadcast_to(columns[:, h : h + 1], (rows, width)) for h in range(heads)], axis=1
    )


def tallen(column, width, lanes):
    return jnp.concatenate(
        [
            jnp.broadcast_to(column[h : h + 1, :], (width, lanes))
            for h in range(column.shape[0])
        ],
        axis=0,
    )


def per_head(values, heads):
    width = values.shape[1] // heads
    return jnp.concatenate(
        [
            jnp.sum(values[:, h * width : (h + 1) * width], axis=1, keepdims=True)
            for h in range(heads)
        ],
        axis=1,
    )


def turned(row):
    size = row.shape[1]
    down = lax.broadcasted_iota(jnp.int32, (size, size), 0)
    right = lax.broadcasted_iota(jnp.int32, (size, size), 1)
    return jnp.sum(
        jnp.where(down == right, jnp.broadcast_to(row, (size, size)), 0.0), axis=1, keepdims=True
    )


def laid(column):
    size = column.shape[0]
    down = lax.broadcasted_iota(jnp.int32, (size, size), 0)
    right = lax.broadcasted_iota(jnp.int32, (size, size), 1)
    return jnp.sum(
        jnp.where(down == right, jnp.broadcast_to(column, (size, size)), 0.0), axis=0, keepdims=True
    )


def fold(values):
    total = values[:8]
    for k in range(1, values.shape[0] // 8):
        total = total + values[8 * k : 8 * k + 8]
    return total


def summed(values):
    return jnp.sum(values, axis=0, keepdims=True)


class Stored:
    def __init__(self, copy):
        self.drain = copy.wait


class Spots:
    def __init__(self, n, ctxn, tpn):
        self.n, self.ctxn, self.tpn = n, ctxn, tpn
        self.ctx = lax.axis_index("ctx")
        self.here = lax.axis_index("dp") * ctxn + self.ctx
        self.mine = lax.axis_index("tp")
        self.half = n // 2
        self.chip, self.core = lax.div(self.here, 2), lax.rem(self.here, 2)
        self.sibling = self.spot(2 * self.chip + 1 - self.core)
        self.group = [self.spot(lax.rem(self.here + step, n)) for step in range(1, n)]
        self.line = [{"tp": lax.rem(self.mine + step, tpn)} for step in range(1, tpn)]
        self.row = [{"ctx": lax.rem(self.ctx + step, ctxn)} for step in range(1, ctxn)]
        self.after = {"ctx": lax.rem(self.ctx + 1, ctxn)}
        self.before = {"ctx": lax.rem(self.ctx + ctxn - 1, ctxn)}

    def spot(self, index):
        return {"dp": lax.div(index, self.ctxn), "ctx": lax.rem(index, self.ctxn)}

    def across(self, step):
        return 2 * lax.rem(self.chip + step, self.half) + self.core


class Gather:
    def __init__(self, at, source, place, sems):
        self.at, self.source, self.place, self.sems = at, source, place, sems

    def launch(self):
        at, sems = self.at, self.sems
        here = self.place(at.here)
        self.own = pltpu.make_async_copy(self.source, here, sems.at[4, 0])
        self.own.start()
        self.copies = []
        for step in range(1, at.half):
            copy = send_to(
                self.source, here, sems.at[0, step], sems.at[1, step], at.spot(at.across(step))
            )
            copy.start()
            self.copies.append(copy)
        self.beside = send_to(self.source, here, sems.at[0, 0], sems.at[1, 0], at.sibling)
        self.beside.start()

    def relay(self):
        at, sems = self.at, self.sems
        self.passed = []
        for step in range(1, at.half):
            origin = self.place(at.across(at.half - step))
            self.copies[step - 1].wait_recv()
            copy = send_to(origin, origin, sems.at[2, step], sems.at[3, step], at.sibling)
            copy.start()
            self.passed.append(copy)

    def finish(self):
        self.own.wait()
        self.beside.wait_recv()
        for copy in self.passed:
            copy.wait_recv()

    def drain(self):
        self.beside.wait_send()
        for copy in self.copies + self.passed:
            copy.wait_send()


class Swap:
    def __init__(self, peers, places, slots, sems):
        self.copies = []
        for step, peer in enumerate(peers):
            copy = send_to(places(step), slots, sems.at[0, step], sems.at[1, step], peer)
            copy.start()
            self.copies.append(copy)

    def arrive(self):
        for copy in self.copies:
            copy.wait_recv()

    def drain(self):
        for copy in self.copies:
            copy.wait_send()


class Shift:
    def __init__(self, source, target, sems, peer, sends, receives):
        self.copy = send_to(source, target, sems.at[0], sems.at[1], peer)
        self.sends, self.receives = sends, receives

        @pl.when(sends)
        def _():
            self.copy.start()

    def arrive(self):
        @pl.when(self.receives)
        def _():
            self.copy.wait_recv()

    def drain(self):
        @pl.when(self.sends)
        def _():
            self.copy.wait_send()


class LineSum:
    def __init__(self, at, part, full, inbox, outbox, sems, chunk, hop, finish):
        self.at, self.part, self.full, self.finish = at, part, full, finish
        self.inbox, self.outbox, self.sems, self.chunk = inbox, outbox, sems, chunk
        self.count = part.shape[0] // 2 // chunk
        self.hop = hop
        tpn = at.tpn
        self.steps = self.count + hop * (2 * tpn - 3)
        self.far = [tpn - 1 - at.mine, at.mine]
        up, down = {"tp": lax.rem(at.mine + 1, tpn)}, {"tp": lax.rem(at.mine + tpn - 1, tpn)}
        self.ahead, self.back = [down, up], [up, down]

    def rows(self, stream, j):
        return span(stream * self.count + j, self.chunk)

    def reduction(self, stream, j, source):
        return send_to(
            source,
            self.inbox.at[stream, j],
            self.sems.at[0, stream, j],
            self.sems.at[1, stream, j],
            self.ahead[stream],
        )

    def spreading(self, stream, j):
        where = self.full.at[self.rows(stream, j)]
        return send_to(
            where, where, self.sems.at[2, stream, j], self.sems.at[3, stream, j], self.back[stream]
        )

    def begin(self, stream, start=0, stop=LEAD):
        @pl.when(self.far[stream] == 0)
        def _():
            for j in range(start, min(stop, self.count)):
                self.reduction(stream, j, self.part.at[self.rows(stream, j)]).start()

    def tick(self, stream, t):
        if t < 0 or t >= self.steps:
            return
        self.begin(stream, t + LEAD, t + LEAD + 1)
        far, tpn = self.far[stream], self.at.tpn
        j = t - self.hop * (far - 1)

        @pl.when((far > 0) & (j >= 0) & (j < self.count))
        def _():
            rows = self.rows(stream, j)
            self.reduction(stream, j, self.outbox.at[stream, j]).wait_recv()
            total = (self.part[rows].astype(wide) + self.inbox[stream, j].astype(wide)).astype(low)

            @pl.when(far < tpn - 1)
            def _():
                self.outbox[stream, j] = total
                self.reduction(stream, j, self.outbox.at[stream, j]).start()

            @pl.when(far == tpn - 1)
            def _():
                self.full[rows] = total
                self.spreading(stream, j).start()
                self.finish(rows)

        i = t - self.hop * (2 * tpn - 3 - far)

        @pl.when((far < tpn - 1) & (i >= 0) & (i < self.count))
        def _():
            self.spreading(stream, i).wait_recv()

            @pl.when(far > 0)
            def _():
                self.spreading(stream, i).start()

            self.finish(self.rows(stream, i))

    def drain(self):
        def one(j, carry):
            for stream in range(2):

                @pl.when(self.far[stream] < self.at.tpn - 1)
                def _():
                    self.reduction(stream, j, self.outbox.at[stream, j]).wait_send()

                @pl.when(self.far[stream] > 0)
                def _():
                    self.spreading(stream, j).wait_send()

            return carry

        each(self.count, one)


class Scatter:
    def __init__(self, at, slot, beside_buf, out_buf, in_buf, sems):
        self.at, self.slot, self.sems = at, slot, sems
        self.beside_buf, self.out_buf, self.in_buf = beside_buf, out_buf, in_buf

    def pair(self):
        at, sems = self.at, self.sems
        self.beside = {}
        for step in list(range(1, at.half)) + [0]:
            other = 2 * lax.rem(at.chip + step, at.half) + 1 - at.core
            copy = send_to(
                self.slot(other),
                self.beside_buf.at[step],
                sems.at[0, step],
                sems.at[1, step],
                at.sibling,
            )
            copy.start()
            self.beside[step] = copy

    def cross(self):
        at, sems = self.at, self.sems
        self.copies = []
        for step in range(1, at.half):
            target = at.across(step)
            self.beside[step].wait_recv()
            self.out_buf[step] = (
                self.slot(target)[...].astype(wide) + self.beside_buf[step].astype(wide)
            ).astype(low)
            copy = send_to(
                self.out_buf.at[step],
                self.in_buf.at[step],
                sems.at[2, step],
                sems.at[3, step],
                at.spot(target),
            )
            copy.start()
            self.copies.append(copy)

    def collect(self):
        at = self.at
        self.beside[0].wait_recv()
        total = self.slot(at.here)[...].astype(wide) + self.beside_buf[0].astype(wide)
        for step in range(1, at.half):
            self.copies[step - 1].wait_recv()
            total = total + self.in_buf[step].astype(wide)
        return total

    def drain(self):
        for copy in list(self.beside.values()) + self.copies:
            copy.wait_send()


def chained(slots, count, here, heads, backward):
    rows = slots.shape[1] - heads
    width, lanes = rows // heads, slots.shape[2]
    before = jnp.zeros((rows, lanes), wide)
    for k in range(count):
        at = count - 1 - k if backward else k
        reached = at > here if backward else at < here
        grown = tallen(jnp.exp(slots[at, rows:]), width, lanes)
        before = jnp.where(reached, slots[at, :rows] + grown * before, before)
    return before


def conv_block(source, start, rows, width, kernel, offset):
    taps = kernel.shape[0]
    around = source[pl.ds(start + HALO - 8, rows + 8), :width]
    total = offset
    for k in range(taps):
        first = 9 - taps + k
        total = total + kernel[k : k + 1] * around[first : first + rows]
    return total


def front(at, r, heads, out_sum):
    length, width = r.tok.shape
    inner = r.x.shape[1]
    head = inner // heads
    state_width = r.state_t.shape[0]
    nstate = r.bc.shape[1] // 2
    rows, columns = r.in_w.shape[0], r.out_w.shape[1]
    size, count = STRETCH, length // STRETCH
    half_length = length // 2

    loads = [
        pltpu.make_async_copy(getattr(r, "h_" + name), getattr(r, name), r.load_sems.at[3 + k])
        for k, name in enumerate(SMALL_INPUTS)
    ]
    for copy in loads:
        copy.start()
    load = pltpu.make_async_copy(r.tokens, r.tok, r.load_sems.at[0])
    load.start()
    load_cot = pltpu.make_async_copy(r.cotangent, r.cot, r.load_sems.at[1])
    load_cot.start()
    load_out = pltpu.make_async_copy(r.out_w, r.out_v, r.load_sems.at[2])
    load_out.start()
    for copy in loads:
        copy.wait()
    for h in range(heads):
        r.skip_row[:, h * head : (h + 1) * head] = jnp.broadcast_to(
            r.skip_gain[:, h : h + 1], (1, head)
        )
    taps = r.state_kernel.shape[0]
    r.taps_own[...] = jnp.concatenate(
        [r.state_kernel[...], r.state_offset[...], jnp.zeros((7 - taps, state_width), wide)], axis=0
    )
    r.taps_all[at.mine] = r.taps_own[...]
    r.step_own[...] = jnp.concatenate(
        [r.step_t[...].astype(wide), jnp.zeros((PAD - heads, rows), wide)], axis=0
    ).astype(low)

    line_up(at.group + at.line)

    g_in = Gather(at, r.in_w, lambda i: r.full_in.at[span(i, rows)], r.gather_sems.at[0])
    g_step = Gather(at, r.step_own, lambda i: r.step_slots.at[i], r.gather_sems.at[1])
    g_state = Gather(
        at, r.state_own, lambda i: r.full_state.at[span(i, rows)], r.gather_sems.at[4]
    )
    g_gate = Gather(at, r.gate_w, lambda i: r.full_gate.at[span(i, rows)], r.gather_sems.at[2])
    g_out = Gather(
        at, r.out_own, lambda i: r.full_out.at[span(i, columns)], r.gather_sems.at[3]
    )
    r.state_all[at.mine] = r.state_t[...]
    taps_swap = Swap(at.line, lambda k: r.taps_own, r.taps_all.at[at.mine], r.taps_sems)
    st_swap = Swap(at.line, lambda k: r.state_t, r.state_all.at[at.mine], r.bc_sems)
    g_step.launch()
    g_in.launch()
    rim = Shift(
        r.tokens.at[pl.ds(length - HALO, HALO)],
        r.tok_rim,
        r.rim_sems,
        at.after,
        at.ctx < at.ctxn - 1,
        at.ctx > 0,
    )

    load.wait()
    gain = r.norm_gain[...]

    def normal(tokens):
        tokens = tokens.astype(wide)
        inv = lax.rsqrt(jnp.mean(tokens * tokens, axis=-1, keepdims=True) + epsilon)
        return (tokens * inv * gain).astype(low)

    def norm_block(i, carry):
        r.norm[pl.ds(pl.multiple_of(HALO + i * 32, 16), 32)] = normal(r.tok[span(i, 32)])
        return carry

    each(length // 32, norm_block)

    @pl.when(at.ctx == 0)
    def _():
        r.tok_rim[...] = jnp.zeros_like(r.tok_rim)

    for k in range(length // LANES):
        r.norm_t[:, k * LANES : (k + 1) * LANES] = r.norm[
            HALO + k * LANES : HALO + (k + 1) * LANES
        ].T
    load_out.wait()
    r.out_own[...] = r.out_v[...].T
    st_swap.arrive()
    r.state_own[...] = jnp.concatenate([r.state_all[k] for k in range(at.tpn)], axis=0).T
    g_state.launch()
    g_gate.launch()
    rim.arrive()
    r.norm[:HALO] = normal(r.tok_rim[...])
    g_step.relay()
    g_in.relay()
    g_step.finish()
    for k in range(at.n):
        r.full_step[:, k * rows : (k + 1) * rows] = r.step_slots[k]
    g_in.finish()
    r.xp[...] = mm(r.norm[...], r.full_in[...], ((1,), (0,)))
    step_pre = mm(r.norm[HALO:], r.full_step[...], ((1,), (1,)))
    g_state.relay()
    g_out.launch()
    step_row = step_pre[:, :heads].T + turned(r.step_bias[...])
    dt_row = jnp.maximum(step_row, 0.0) + jnp.log1p(jnp.exp(-jnp.abs(step_row)))
    r.sig_row[...] = jax.nn.sigmoid(step_row)
    r.dt_row[...] = dt_row
    decays = -dt_row * turned(jnp.exp(r.decay_log[...]))
    r.decays[...] = decays
    causal = causal_mask(size)
    ones = jnp.where(causal, 1.0, 0.0)
    totals = []
    for s in range(count):
        cut = slice(s * size, (s + 1) * size)
        run = mm(decays[:, cut], ones, ((1,), (1,)), exact_mode)
        r.run_row[:, cut] = run
        total = run[:, size - 1 :]
        totals.append(total)
        left = jnp.exp(total - run)
        dts = dt_row[:, cut]
        r.cols[cut, : 5 * heads] = jnp.concatenate(
            [run, dts, left * dts, jnp.exp(run), left], axis=0
        ).T

    def value_block(i, carry):
        start = pl.multiple_of(i * 32, 32)
        pre = conv_block(r.xp, start, 32, inner, r.input_kernel, r.input_offset[...])
        sig = jax.nn.sigmoid(pre)
        act = pre * sig
        r.x[pl.ds(start, 32)] = act
        r.dsil_in[pl.ds(start, 32)] = sig + act * (1.0 - sig)
        return carry

    each(length // 32, value_block)

    g_state.finish()
    r.sp[...] = mm(r.norm[...], r.full_state[...], ((1,), (0,)))

    def state_block(i, carry):
        start = pl.multiple_of(i * 32, 32)
        pre = conv_block(
            r.sp, start, 32, 2 * nstate, r.full_kernel[...], r.full_offset[...]
        )
        sig = jax.nn.sigmoid(pre)
        act = pre * sig
        r.dsil_st[pl.ds(start, 32)] = sig + act * (1.0 - sig)
        r.bc[pl.ds(start, 32)] = act.astype(low)
        return carry

    taps_swap.arrive()
    r.full_kernel[...] = jnp.concatenate(
        [r.taps_all[k, : r.full_kernel.shape[0]] for k in range(at.tpn)], axis=1
    )
    r.full_offset[...] = jnp.concatenate(
        [r.taps_all[k, r.full_kernel.shape[0] : r.full_kernel.shape[0] + 1] for k in range(at.tpn)],
        axis=1,
    )
    each(length // 32, state_block)

    fresh = []
    state = jnp.zeros((inner, nstate), wide)
    for s in range(count):
        cut = slice(s * size, (s + 1) * size)
        tail = widen(r.cols[cut, 2 * heads : 3 * heads], head)
        added = mm((r.x[cut] * tail).astype(low), r.bc[cut, :nstate], ((0,), (0,)))
        r.fresh[s] = added
        state = tallen(jnp.exp(totals[s]), head, nstate) * state + added
    logs = jnp.broadcast_to(sum(totals), (heads, nstate))
    r.chain_own[:inner] = state
    r.chain_own[inner:] = logs
    r.chain_all[at.ctx] = r.chain_own[...]
    chain = Swap(at.row, lambda k: r.chain_own, r.chain_all.at[at.ctx], r.chain_sems)

    g_gate.relay()
    for s in range(count):
        cut = slice(s * size, (s + 1) * size)
        scores = mm(r.bc[cut, nstate:], r.bc[cut, :nstate], ((1,), (1,)))
        r.scores[s] = scores
        run = r.cols[cut, :heads]
        for h in range(0, heads, 2):
            pair = []
            for k in (h, h + 1):
                fall = jnp.exp(
                    jnp.where(causal, run[:, k : k + 1] - r.run_row[k : k + 1, cut], -1e30)
                )
                mixing = (fall * scores * r.dt_row[k : k + 1, cut]).astype(low)
                x_low = r.x[cut, k * head : (k + 1) * head].astype(low)
                pair.append(mm(mixing, x_low, ((1,), (0,))))
            r.scanned[cut, h * head : (h + 2) * head] = jnp.concatenate(pair, axis=1)
        if s == 0:
            g_gate.finish()
            r.gate[...] = mm(r.norm[HALO:], r.full_gate[...], ((1,), (0,)))

    g_out.relay()
    g_out.finish()
    load_cot.wait()
    r.pull[...] = mm(r.cot[...], r.full_out[...], ((1,), (0,)))

    chain.arrive()
    state = chained(r.chain_all, at.ctxn, at.ctx, heads, False)
    for s in range(count):
        cut = slice(s * size, (s + 1) * size)
        kept = state.astype(low)
        r.kept[s] = kept
        if s + 1 < count:
            state = tallen(jnp.exp(totals[s]), head, nstate) * state + r.fresh[s]
        grown = widen(r.cols[cut, 3 * heads : 4 * heads], head)
        r.carried[cut] = mm(r.bc[cut, nstate:], kept, ((1,), (1,))) * grown

    def gate_block(i, carry):
        here = span(i, 32)
        gate = r.gate[here]
        sig = jax.nn.sigmoid(gate)
        scanned = r.scanned[here] + r.carried[here] + r.skip_row[...] * r.x[here]
        r.scanned[here] = scanned
        gated = scanned * (gate * sig)
        scaled = (gated * r.gated_gain[...]).astype(low)
        r.scaled[here] = scaled
        squares = jnp.sum(gated * gated, axis=1, keepdims=True)
        dots = jnp.sum(scaled.astype(wide) * r.pull[here], axis=1, keepdims=True)
        r.stat[here] = jnp.concatenate([squares, dots, jnp.zeros((32, 6), wide)], axis=1)
        return carry

    each(length // 32, gate_block)
    mine = r.stat[...].T
    r.stat_own[...] = mine
    r.stat_all[at.mine] = mine
    stats = Swap(at.line, lambda k: r.stat_own, r.stat_all.at[at.mine], r.stat_sems)
    r.po[...] = mm(r.scaled[...], r.full_out[...], ((1,), (1,))).astype(low)
    for stream in range(2):
        out_sum.begin(stream)
    stats.arrive()
    total = r.stat_all[0]
    for k in range(1, at.tpn):
        total = total + r.stat_all[k]
    channels = inner * at.tpn
    inv = lax.rsqrt(total[0:1] / channels + epsilon)
    rms = -0.5 * inv * inv * inv * total[1:2] / channels
    r.inv[...] = jnp.concatenate([inv, rms, jnp.zeros((6, length), wide)], axis=0).T
    return [g_in, g_step, g_state, g_gate, g_out, rim, st_swap, taps_swap, chain, stats]


def out_line(at, r):
    def block_rows(here):
        r.v_block[here] = (
            r.tok[here].astype(wide) + r.inv[here, 0:1] * r.po_full[here].astype(wide)
        ).astype(low)

    return LineSum(at, r.po, r.po_full, r.po_in, r.po_out, r.po_sems, CHUNK, 3, block_rows)


def back(at, r, heads, out_sum):
    length, width = r.tok.shape
    inner = r.x.shape[1]
    head = inner // heads
    state_width = r.state_t.shape[0]
    nstate = r.bc.shape[1] // 2
    states = 2 * nstate
    rows, columns = r.in_w.shape[0], r.out_w.shape[1]
    taps = r.input_kernel.shape[0]
    size, count = STRETCH, length // STRETCH
    hl = length // 2
    causal = causal_mask(size)
    ones = jnp.where(causal, 1.0, 0.0)
    drains = []

    def store(name):
        index = STORES.index(name)
        copy = pltpu.make_async_copy(
            getattr(r, "v_" + name), getattr(r, "o_" + name), r.store_sems.at[index]
        )
        copy.start()
        drains.append(Stored(copy))

    def token_rows(here):
        tokens = r.tok[here].astype(wide)
        inv = lax.rsqrt(jnp.mean(tokens * tokens, axis=-1, keepdims=True) + epsilon)
        scaled = r.npl_full[here].astype(wide) * r.norm_gain[...]
        along = jnp.mean(scaled * tokens, axis=-1, keepdims=True)
        r.v_tokens[here] = (
            r.cot[here].astype(wide) + inv * scaled - tokens * (inv * inv * inv * along)
        )

    norm_sum = LineSum(
        at, r.npl, r.npl_full, r.npl_in, r.npl_out, r.npl_sems, CHUNK, 2, token_rows
    )
    early = norm_sum.count - 1
    out_ticks = iter(range(out_sum.steps))
    late_ticks = iter(range(norm_sum.steps))
    first_ticks = iter(range(norm_sum.steps))

    def serve():
        t = next(out_ticks, None)
        if t is None:
            return False
        for stream in range(2):
            out_sum.tick(stream, t)
        if t == out_sum.steps - 1:
            store("block")
        return True

    def lead():
        norm_sum.tick(1, next(late_ticks, -1))

    def tail():
        serve()
        t = next(first_ticks, None)
        if t is None:
            return False
        norm_sum.tick(0, t)
        lead()
        return True

    serve()
    def grad_block(i, carry):
        gains, skips = carry
        here = span(i, 32)
        inv, rms = r.inv[here, 0:1], r.inv[here, 1:2]
        gate, scanned = r.gate[here], r.scanned[here]
        sig = jax.nn.sigmoid(gate)
        silu = gate * sig
        gated = scanned * silu
        scaled_grad = inv * r.pull[here]
        gains = gains + fold(scaled_grad * gated)
        gated_grad = scaled_grad * r.gated_gain[...] + 2.0 * rms * gated
        dy = gated_grad * silu
        r.dy[here] = dy
        r.gate_low[here] = (gated_grad * scanned * (sig + silu * (1.0 - sig))).astype(low)
        skips = skips + fold(dy * r.x[here])
        r.proj_grad[here] = (inv * r.cot[here].astype(wide)).astype(low)
        return gains, skips

    zero = jnp.zeros((8, inner), wide)
    gains, skips = each(length // 32, grad_block, (zero, zero))
    gain_row, skip_row = summed(gains), per_head(summed(skips), heads)
    serve()

    state = jnp.zeros((inner, nstate), wide)
    totals = [r.run_row[:, (s + 1) * size - 1 : (s + 1) * size] for s in range(count)]
    for s in reversed(range(count)):
        cut = slice(s * size, (s + 1) * size)
        grown = widen(r.cols[cut, 3 * heads : 4 * heads], head)
        dy_grown = r.dy[cut] * grown
        dy_low = dy_grown.astype(low)
        added = mm(dy_low, r.bc[cut, nstate:], ((0,), (0,)))
        r.fresh[s] = added
        state = tallen(jnp.exp(totals[s]), head, nstate) * state + added
        kept = r.kept[s]
        r.dyc[cut] = per_head(dy_grown * mm(r.bc[cut, nstate:], kept, ((1,), (1,))), heads)
        r.dbc[cut, nstate:] = mm(dy_low, kept, ((1,), (0,)))
    r.turn_own[:inner] = state
    r.turn_own[inner:] = jnp.broadcast_to(sum(totals), (heads, nstate))
    r.turn_all[at.ctx] = r.turn_own[...]
    chain = Swap(at.row, lambda k: r.turn_own, r.turn_all.at[at.ctx], r.turn_sems)
    drains.append(chain)
    serve()

    def within(s, serves):
        cut = slice(s * size, (s + 1) * size)
        b, c = r.bc[cut, :nstate], r.bc[cut, nstate:]
        run = r.cols[cut, :heads]
        scores = r.scores[s]
        dscores = jnp.zeros((size, size), wide)
        across, down = [], []
        for h in range(0, heads, 2):
            pair = []
            for k in (h, h + 1):
                lanes = slice(k * head, (k + 1) * head)
                fall = jnp.exp(
                    jnp.where(causal, run[:, k : k + 1] - r.run_row[k : k + 1, cut], -1e30)
                )
                dt = r.dt_row[k : k + 1, cut]
                dy_low = r.dy[cut, lanes].astype(low)
                products = mm(dy_low, r.x[cut, lanes].astype(low), ((1,), (1,))) * fall
                dscores = dscores + products * dt
                terms = products * scores
                down.append(jnp.sum(terms, axis=0, keepdims=True))
                across.append(jnp.sum(terms * dt, axis=1, keepdims=True))
                mixing = (fall * scores * dt).astype(low)
                pair.append(mm(mixing, dy_low, ((0,), (0,))))
                if k == h:
                    serves()
            r.dx[cut, h * head : (h + 2) * head] = jnp.concatenate(pair, axis=1)
            serves()
        dscores = dscores.astype(low)
        r.dbc[cut, :nstate] = mm(dscores, c, ((0,), (0,)))
        r.dbc[cut, nstate:] += mm(dscores, b, ((1,), (0,)))
        r.down[:, cut] = jnp.concatenate(down, axis=0)
        r.dyc[cut] += jnp.concatenate(across, axis=1)

    decay_rates = turned(jnp.exp(r.decay_log[...]))
    bias_grad = jnp.zeros((heads, 1), wide)
    decay_grad = jnp.zeros((heads, 1), wide)

    def between(s, state):
        cut = slice(s * size, (s + 1) * size)
        state_low = state.astype(low)
        x = r.x[cut]
        spare = widen(r.cols[cut, 2 * heads : 3 * heads], head)
        fade = widen(r.cols[cut, 4 * heads : 5 * heads], head)
        pulled = mm(r.bc[cut, :nstate], state_low, ((1,), (1,)))
        r.dbc[cut, :nstate] += mm((x * spare).astype(low), state_low, ((1,), (0,)))
        tail_grad = per_head(x * fade * pulled, heads)
        r.dx[cut] += spare * pulled + r.skip_row[...] * r.dy[cut]
        shrink = tallen(jnp.exp(totals[s]), head, nstate)
        lost = shrink * state * r.kept[s].astype(wide)
        lost = jnp.concatenate(
            [summed(lost[h * head : (h + 1) * head]) for h in range(heads)], axis=0
        )
        both = jnp.concatenate([tail_grad, r.dyc[cut]], axis=1).T
        tail_row, drun = both[:heads], both[heads:]
        dt, down = r.dt_row[:, cut], r.down[:, cut]
        out_tail = tail_row * dt
        drun = drun - out_tail - down * dt
        dtotal = jnp.sum(lost, axis=1, keepdims=True) + jnp.sum(out_tail, axis=1, keepdims=True)
        ddecay = dtotal + mm(drun, ones, ((1,), (0,)), exact_mode)
        step_grad = (down + tail_row - ddecay * decay_rates) * r.sig_row[:, cut]
        r.step_low[cut] = jnp.concatenate(
            [step_grad.T, jnp.zeros((size, PAD - heads), wide)], axis=1
        ).astype(low)
        if s > 0:
            state = shrink * state + r.fresh[s]
        return (
            state,
            jnp.sum(step_grad, axis=1, keepdims=True),
            jnp.sum(ddecay * r.decays[:, cut], axis=1, keepdims=True),
        )

    def unpull(source, kernel, start, size):
        around = source[pl.ds(start, size + 8)]
        total = kernel[taps - 1 : taps] * around[:size]
        for k in range(taps - 1):
            first = taps - 1 - k
            total = total + kernel[k : k + 1] * around[first : first + size]
        return total

    def low_blocks(start, blocks):
        def block(i, carry):
            here = pl.ds(pl.multiple_of(start + i * 32, 32), 32)
            first = pl.multiple_of(start + i * 32, 32)
            r.input_low[here] = unpull(r.dp, r.input_kernel[...], first, 32).astype(low)
            r.st_low[here] = unpull(r.dpt, r.full_kernel[...], first, 32).astype(low)
            return carry

        each(blocks, block)

    def scale_blocks(start):
        def block(i, carry):
            here = pl.ds(pl.multiple_of(start + i * 32, 32), 32)
            r.dp[here] = r.dx[here] * r.dsil_in[here]
            r.dpt[here] = r.dbc[here] * r.dsil_st[here]
            return carry

        each(hl // 32, block)

    def norm_part(pieces):
        def take(ref):
            if len(pieces) == 1:
                return ref[pieces[0]]
            return jnp.concatenate([ref[cut] for cut in pieces], axis=0)

        value = (
            mm(take(r.gate_low), r.full_gate[...], ((1,), (1,)))
            + mm(take(r.input_low), r.full_in[...], ((1,), (1,)))
            + mm(take(r.st_low), r.full_state[...], ((1,), (1,)))
            + mm(take(r.step_low), r.full_step[...], ((1,), (0,)))
        )
        first = 0
        for cut in pieces:
            r.np_[cut] = value[first : first + cut.stop - cut.start]
            first += cut.stop - cut.start

    def part_blocks(start, blocks, carry):
        def block(i, carry):
            here = pl.ds(pl.multiple_of(start + i * 32, 32), 32)
            tokens = r.tok[here].astype(wide)
            inv = lax.rsqrt(jnp.mean(tokens * tokens, axis=-1, keepdims=True) + epsilon)
            value = r.np_[here]
            r.npl[here] = value.astype(low)
            return carry + fold(value * (tokens * inv))

        return each(blocks, block, carry)

    def send_states(half):
        base = half * hl
        quarter = hl // 2
        for k in range(at.tpn):
            lanes = slice(k * state_width, (k + 1) * state_width)
            r.ds_own[half, k] = jnp.concatenate(
                [
                    r.dbc[base : base + quarter, lanes],
                    r.dbc[base + quarter : base + hl, lanes],
                ],
                axis=1,
            ).astype(low)
        turn = Swap(
            at.line,
            lambda k: r.ds_own.at[half, lax.rem(at.mine + k + 1, at.tpn)],
            r.ds_all.at[half, at.mine],
            r.ds_sems.at[half],
        )
        drains.append(turn)
        r.ds_all[half, at.mine] = r.ds_own[half, at.mine]
        return turn

    half_count = count // 2
    turns = {}
    gain_sums = jnp.zeros((8, width), wide)
    is_last, is_first = at.ctx == at.ctxn - 1, at.ctx == 0
    calls = []

    def some():
        calls.append(0)
        if len(calls) % 6 == 0:
            serve()

    for s in reversed(range(half_count, count)):
        within(s, some)
    chain.arrive()
    state = chained(r.turn_all, at.ctxn, at.ctx, heads, True)
    for s in reversed(range(half_count, count)):
        state, more_bias, more_decay = between(s, state)
        bias_grad, decay_grad = bias_grad + more_bias, decay_grad + more_decay
        serve()
    scale_blocks(hl)
    low_blocks(hl, early)
    serve()
    norm_part([slice(hl, length - CHUNK)])
    gain_sums = part_blocks(hl, early, gain_sums)
    norm_sum.begin(1)
    serve()
    turns[1] = send_states(1)

    r.g_gate[...] = mm(r.norm_t[...], r.gate_low[...], ((1,), (0,))).astype(low)
    s_gate = Scatter(
        at,
        lambda i: r.g_gate.at[span(i, rows)],
        r.gate_b,
        r.gate_o,
        r.gate_i,
        r.scatter_sems.at[0],
    )
    s_gate.pair()
    serve()
    for k in range(length // LANES):
        r.proj_t[:, k * LANES : (k + 1) * LANES] = r.proj_grad[k * LANES : (k + 1) * LANES].T
    r.g_out[...] = mm(r.proj_t[...], r.scaled[...], ((1,), (0,))).astype(low)
    s_out = Scatter(
        at,
        lambda i: r.g_out.at[span(i, columns)],
        r.out_b,
        r.out_o,
        r.out_i,
        r.scatter_sems.at[1],
    )
    s_gate.cross()
    s_out.pair()
    serve()

    turn_taken = []

    def both_lines():
        turn_taken.append(0)
        if len(turn_taken) % 5 == 0:
            serve()
            lead_early()

    early_ticks = iter(range(early - LEAD))

    def lead_early():
        if next(early_ticks, None) is not None:
            lead()

    for s in reversed(range(half_count)):
        within(s, both_lines)
    s_out.cross()
    for s in reversed(range(half_count)):
        state, more_bias, more_decay = between(s, state)
        bias_grad, decay_grad = bias_grad + more_bias, decay_grad + more_decay
    turns[0] = send_states(0)
    scale_blocks(0)

    @pl.when(is_last)
    def _():
        r.dp[length:] = jnp.zeros((8, inner), wide)
        r.dpt[length:] = jnp.zeros((8, states), wide)

    rims = []
    for k, ref in enumerate((r.dp, r.dpt)):
        rims.append(
            Shift(
                ref.at[pl.ds(0, 8)],
                ref.at[pl.ds(length, 8)],
                r.back_sems.at[k],
                at.before,
                jnp.logical_not(is_first),
                jnp.logical_not(is_last),
            )
        )
    drains.extend(rims)
    serve()
    low_blocks(0, hl // 32)
    for rim in rims:
        rim.arrive()
    low_blocks(length - CHUNK, 1)
    lead_early()
    serve()
    norm_part([slice(length - CHUNK, length), slice(0, hl)])
    gain_sums = part_blocks(length - CHUNK, 1, gain_sums)
    gain_sums = part_blocks(0, hl // 32, gain_sums)
    for k in range(early):
        lead_early()
    norm_sum.begin(0)
    gain_part = summed(gain_sums)
    r.g_in[...] = mm(r.norm_t[...], r.input_low[...], ((1,), (0,))).astype(low)
    s_in = Scatter(
        at, lambda i: r.g_in.at[span(i, rows)], r.in_b, r.in_o, r.in_i, r.scatter_sems.at[2]
    )
    s_in.pair()
    tail()
    def tap_block(i, carry):
        around = r.xp[pl.ds(pl.multiple_of(i * 32, 32) + HALO - 8, 40)]
        grad = r.dp[span(i, 32)]
        out = [carry[0] + fold(grad)]
        for k in range(taps):
            first = 9 - taps + k
            out.append(carry[1 + k] + fold(grad * around[first : first + 32]))
        return tuple(out)

    tap_sums = each(length // 32, tap_block, (zero,) * (1 + taps))
    tap_sums = [summed(value) for value in tap_sums]
    s_in.cross()
    tail()

    tail()
    tail()
    quarter = hl // 2
    at_tp = lambda array: sum(
        jnp.where(at.mine == k, array[:, k * state_width : (k + 1) * state_width], 0.0)
        for k in range(at.tpn)
    )
    for half in (1, 0):
        turns[half].arrive()
        mine = r.ds_all[half, 0].astype(wide)
        for k in range(1, at.tpn):
            mine = mine + r.ds_all[half, k].astype(wide)
        for k in range(2):
            cut = slice(half * hl + k * quarter, half * hl + (k + 1) * quarter)
            r.dps[cut] = mine[:, k * state_width : (k + 1) * state_width] * at_tp(r.dsil_st[cut])

    @pl.when(is_last)
    def _():
        r.dps[length:] = jnp.zeros((8, state_width), wide)

    st_rim = Shift(
        r.dps.at[pl.ds(0, 8)],
        r.dps.at[pl.ds(length, 8)],
        r.back_sems.at[2],
        at.before,
        jnp.logical_not(is_first),
        jnp.logical_not(is_last),
    )
    drains.append(st_rim)
    st_grad = r.dps[:length]
    r.sp_own[...] = at_tp(r.sp[...])
    st_sums = [summed(st_grad)]
    for k in range(taps):
        first = HALO + 1 - taps + k
        st_sums.append(summed(st_grad * r.sp_own[first : first + length]))
    tail()
    st_rim.arrive()
    total = unpull(r.dps, r.state_kernel[...], 0, length)
    r.misc_low[...] = jnp.concatenate(
        [total, r.step_low[...].astype(wide)], axis=1
    ).astype(low)
    grads = mm(r.misc_low[...], r.norm[HALO:], ((0,), (0,))).astype(low)
    for k in range(at.n):
        r.g_misc[k] = grads[:, k * rows : (k + 1) * rows]
    s_misc = Scatter(
        at, lambda i: r.g_misc.at[i], r.misc_b, r.misc_o, r.misc_i, r.scatter_sems.at[3]
    )
    s_misc.pair()
    tail()

    r.small[...] = jnp.zeros_like(r.small)

    def put(row, values):
        lanes = values.shape[1]
        for k in range(-(-lanes // LANES)):
            stop = min(LANES, lanes - k * LANES)
            r.small[row + k : row + k + 1, :stop] = values[:, k * LANES : k * LANES + stop]

    place = {}
    at_row = 0
    for name, values in (
        [("gain", gain_part)]
        + [("in%d" % k, tap_sums[1 + k]) for k in range(taps)]
        + [("inoff", tap_sums[0]), ("gated", gain_row)]
        + [("st%d" % k, st_sums[1 + k]) for k in range(taps)]
        + [("stoff", st_sums[0]), ("skip", skip_row)]
        + [("bias", laid(bias_grad)), ("decay", laid(decay_grad))]
    ):
        place[name] = (at_row, values.shape[1])
        put(at_row, values)
        at_row += -(-values.shape[1] // LANES)
    r.small_in[at.here] = r.small[...]
    smalls = Swap(at.group, lambda k: r.small, r.small_in.at[at.here], r.small_sems)
    drains.append(smalls)
    tail()
    s_misc.cross()

    r.v_gate[...] = s_gate.collect()
    store("gate")
    tail()
    r.v_out[...] = s_out.collect().T
    store("out")
    tail()

    smalls.arrive()
    total = r.small_in[0]
    for k in range(1, at.n):
        total = total + r.small_in[k]
    r.total[...] = total
    gain_rows = width // LANES
    r.gain_own[...] = total[:gain_rows]
    r.gain_all[at.mine] = total[:gain_rows]
    gains = Swap(at.line, lambda k: r.gain_own, r.gain_all.at[at.mine], r.gain_sems)
    drains.append(gains)
    tail()

    def get(name):
        row, lanes = place[name]
        return [
            r.total[row + k : row + k + 1, : min(LANES, lanes - k * LANES)]
            for k in range(-(-lanes // LANES))
        ]

    def lay(target, row, name):
        for k, value in enumerate(get(name)):
            target[row : row + 1, k * LANES : k * LANES + value.shape[1]] = value

    for k in range(taps):
        lay(r.v_in_kernel, k, "in%d" % k)
        lay(r.v_st_kernel, k, "st%d" % k)
    lay(r.v_in_offset, 0, "inoff")
    lay(r.v_st_offset, 0, "stoff")
    lay(r.v_gated, 0, "gated")
    lay(r.v_skip, 0, "skip")
    lay(r.v_bias, 0, "bias")
    lay(r.v_decay, 0, "decay")
    for name in ("in_kernel", "st_kernel", "in_offset", "st_offset", "gated", "skip"):
        store(name)
    store("bias")
    store("decay")
    tail()
    r.v_in[...] = s_in.collect()
    store("in")
    tail()
    misc = s_misc.collect()
    r.v_state[...] = misc[:state_width]
    r.v_step[...] = misc[state_width : state_width + heads]
    store("state")
    store("step")
    tail()
    gains.arrive()
    total = r.gain_all[0]
    for k in range(1, at.tpn):
        total = total + r.gain_all[k]
    r.v_gain[...] = total
    store("gain")

    while tail():
        pass
    store("tokens")

    for scatter in (s_gate, s_out, s_in, s_misc):
        scatter.drain()
    out_sum.drain()
    norm_sum.drain()
    return drains


def whole_kernel(n, ctxn, tpn, heads, names, *refs):
    r = SimpleNamespace(**dict(zip(names, refs)))
    r.dx, r.dy, r.np_ = r.carried, r.pull, r.v_tokens
    at = Spots(n, ctxn, tpn)
    out_sum = out_line(at, r)
    drains = front(at, r, heads, out_sum)
    drains += back(at, r, heads, out_sum)
    for item in drains:
        item.drain()


def emit_kernel(count, *refs):
    sources, targets, held = refs[:count], refs[count : 2 * count], refs[2 * count : 3 * count]
    sems = refs[3 * count]
    loads = [pltpu.make_async_copy(sources[k], held[k], sems.at[0, k]) for k in range(count)]
    stores = [pltpu.make_async_copy(held[k], targets[k], sems.at[1, k]) for k in range(count)]
    for copy in loads:
        copy.start()
    for k in range(count):
        loads[k].wait()
        stores[k].start()
    for copy in stores:
        copy.wait()


def emit(arrays):
    count = len(arrays)
    return pl.pallas_call(
        functools.partial(emit_kernel, count),
        out_shape=tuple(jax.ShapeDtypeStruct(a.shape, a.dtype) for a in arrays),
        in_specs=[pl.BlockSpec(memory_space=pl.ANY)] * count,
        out_specs=(pl.BlockSpec(memory_space=pl.ANY),) * count,
        scratch_shapes=[pltpu.VMEM(a.shape, a.dtype) for a in arrays]
        + [pltpu.SemaphoreType.DMA((2, count))],
        compiler_params=pltpu.CompilerParams(vmem_limit_bytes=62 * 2**20),
    )(*arrays)


def per_device(
    tokens,
    norm_gain,
    gate_weight,
    input_weight,
    state_weight,
    step_weight,
    input_kernel,
    input_offset,
    state_kernel,
    state_offset,
    step_bias,
    decay_log,
    skip_gain,
    gated_gain,
    out_weight,
    cotangent,
):
    ctxn = lax.axis_size("ctx")
    n, tpn = lax.axis_size("dp") * ctxn, lax.axis_size("tp")
    length, width = tokens.shape
    rows, inner = input_weight.shape
    state_width, heads = state_weight.shape[1], step_weight.shape[1]
    columns = out_weight.shape[1]
    nstate = state_width * tpn // 2
    head = inner // heads
    taps = input_kernel.shape[0]
    count = length // STRETCH
    half = n // 2
    steps = length // 2 // CHUNK
    hl = length // 2
    row = lambda a: a.reshape(1, a.shape[0])
    inputs = dict(
        tokens=tokens,
        cotangent=cotangent,
        in_w=input_weight,
        gate_w=gate_weight,
        out_w=out_weight,
        h_state_t=state_weight.T,
        h_step_t=step_weight.T,
        h_norm_gain=row(norm_gain),
        h_input_kernel=input_kernel,
        h_input_offset=row(input_offset),
        h_state_kernel=state_kernel,
        h_state_offset=row(state_offset),
        h_step_bias=row(step_bias),
        h_decay_log=row(decay_log),
        h_skip_gain=row(skip_gain),
        h_gated_gain=row(gated_gain),
    )
    outputs = dict(
        o_block=((length, width), low),
        o_tokens=((length, width), wide),
        o_gain=((width // LANES, LANES), wide),
        o_gate=((rows, inner), wide),
        o_in=((rows, inner), wide),
        o_state=((state_width, rows), wide),
        o_step=((heads, rows), wide),
        o_in_kernel=((taps, inner), wide),
        o_in_offset=((1, inner), wide),
        o_st_kernel=((taps, state_width), wide),
        o_st_offset=((1, state_width), wide),
        o_bias=((1, heads), wide),
        o_decay=((1, heads), wide),
        o_skip=((1, heads), wide),
        o_gated=((1, inner), wide),
        o_out=((inner, columns), wide),
    )
    small_rows = width // LANES + (taps + 2) * inner // LANES + (taps + 1) + 3
    small_rows = -(-small_rows // 8) * 8
    both = (length, inner)
    scratch = {
        name: (inputs["h_" + name].shape, inputs["h_" + name].dtype) for name in SMALL_INPUTS
    }
    scratch.update({"v" + name[1:]: value for name, value in outputs.items()})
    scratch.update(
        skip_row=((1, inner), wide),
        tok=((length, width), low),
        cot=((length, width), low),
        tok_rim=((HALO, width), low),
        step_own=((PAD, rows), low),
        step_slots=((n, PAD, rows), low),
        full_step=((PAD, width), low),
        state_own=((rows, 2 * nstate), low),
        state_all=((tpn, state_width, rows), low),
        full_state=((width, 2 * nstate), low),
        taps_own=((8, state_width), wide),
        taps_all=((tpn, 8, state_width), wide),
        full_kernel=((taps, 2 * nstate), wide),
        full_offset=((1, 2 * nstate), wide),
        norm=((HALO + length, width), low),
        norm_t=((width, length), low),
        full_in=((width, inner), low),
        full_gate=((width, inner), low),
        full_out=((width, inner), low),
        out_v=((inner, columns), low),
        out_own=((columns, inner), low),
        sp=((HALO + length, 2 * nstate), wide),
        sp_own=((HALO + length, state_width), wide),
        dsil_st=((length, 2 * nstate), wide),
        bc=((length, 2 * nstate), low),
        xp=((HALO + length, inner), wide),
        x=(both, wide),
        dsil_in=(both, wide),
        sig_row=((heads, length), wide),
        dt_row=((heads, length), wide),
        decays=((heads, length), wide),
        run_row=((heads, length), wide),
        cols=((length, 5 * heads), wide),
        fresh=((count, inner, nstate), wide),
        chain_own=((inner + heads, nstate), wide),
        chain_all=((ctxn, inner + heads, nstate), wide),
        turn_own=((inner + heads, nstate), wide),
        turn_all=((ctxn, inner + heads, nstate), wide),
        scores=((count, STRETCH, STRETCH), wide),
        scanned=(both, wide),
        carried=(both, wide),
        gate=(both, wide),
        pull=(both, wide),
        kept=((count, inner, nstate), low),
        scaled=(both, low),
        proj_t=((width, length), low),
        stat=((length, 8), wide),
        stat_own=((8, length), wide),
        stat_all=((tpn, 8, length), wide),
        inv=((length, 8), wide),
        po=((length, width), low),
        po_full=((length, width), low),
        po_in=((2, steps, CHUNK, width), low),
        po_out=((2, steps, CHUNK, width), low),
        gate_low=(both, low),
        proj_grad=((length, width), low),
        dyc=((length, heads), wide),
        dbc=((length, 2 * nstate), wide),
        g_gate=((width, inner), low),
        gate_b=((half, rows, inner), low),
        gate_o=((half, rows, inner), low),
        gate_i=((half, rows, inner), low),
        g_in=((width, inner), low),
        in_b=((half, rows, inner), low),
        in_o=((half, rows, inner), low),
        in_i=((half, rows, inner), low),
        g_out=((width, inner), low),
        out_b=((half, columns, inner), low),
        out_o=((half, columns, inner), low),
        out_i=((half, columns, inner), low),
        g_misc=((n, MISC, rows), low),
        misc_b=((half, MISC, rows), low),
        misc_o=((half, MISC, rows), low),
        misc_i=((half, MISC, rows), low),
        down=((heads, length), wide),
        step_low=((length, PAD), low),
        st_low=((length, 2 * nstate), low),
        ds_own=((2, tpn, hl // 2, 2 * state_width), low),
        ds_all=((2, tpn, hl // 2, 2 * state_width), low),
        dpt=((length + 8, 2 * nstate), wide),
        dp=((length + 8, inner), wide),
        dps=((length + 8, state_width), wide),
        input_low=(both, low),
        misc_low=((length, MISC), low),
        npl=((length, width), low),
        npl_full=((length, width), low),
        npl_in=((2, steps, CHUNK, width), low),
        npl_out=((2, steps, CHUNK, width), low),
        small=((small_rows, LANES), wide),
        small_in=((n, small_rows, LANES), wide),
        total=((small_rows, LANES), wide),
        gain_own=((width // LANES, LANES), wide),
        gain_all=((tpn, width // LANES, LANES), wide),
    )
    sems = dict(
        store_sems=(len(STORES),),
        load_sems=(3 + len(SMALL_INPUTS),),
        gather_sems=(5, 5, half),
        rim_sems=(2,),
        bc_sems=(2, tpn),
        taps_sems=(2, tpn),
        chain_sems=(2, ctxn),
        turn_sems=(2, ctxn),
        stat_sems=(2, tpn),
        po_sems=(4, 2, steps),
        npl_sems=(4, 2, steps),
        scatter_sems=(4, 4, half),
        ds_sems=(2, 2, tpn),
        back_sems=(3, 2),
        small_sems=(2, n),
        gain_sems=(2, tpn),
    )
    names = list(inputs) + list(outputs) + list(scratch) + list(sems)
    results = pl.pallas_call(
        functools.partial(whole_kernel, n, ctxn, tpn, heads, names),
        out_shape=tuple(jax.ShapeDtypeStruct(*o) for o in outputs.values()),
        in_specs=[pl.BlockSpec(memory_space=pl.ANY)] * len(inputs),
        out_specs=(pl.BlockSpec(memory_space=pl.ANY),) * len(outputs),
        scratch_shapes=[pltpu.VMEM(*s) for s in scratch.values()]
        + [pltpu.SemaphoreType.DMA(s) for s in sems.values()],
        compiler_params=pltpu.CompilerParams(
            collective_id=0, has_side_effects=True, vmem_limit_bytes=62 * 2**20
        ),
    )(*inputs.values())
    o = SimpleNamespace(**dict(zip(outputs, emit(results))))
    return (
        o.o_block,
        o.o_tokens,
        o.o_gain.reshape(-1),
        o.o_gate,
        o.o_in,
        o.o_state.T,
        o.o_step.T,
        o.o_in_kernel,
        o.o_in_offset.reshape(-1),
        o.o_st_kernel,
        o.o_st_offset.reshape(-1),
        o.o_bias.reshape(-1),
        o.o_decay.reshape(-1),
        o.o_skip.reshape(-1),
        o.o_gated.reshape(-1),
        o.o_out,
    )


def solution(mesh):
    placed = (
        P(("dp", "ctx"), None),
        P(),
        P(("dp", "ctx"), "tp"),
        P(("dp", "ctx"), "tp"),
        P(("dp", "ctx"), "tp"),
        P(("dp", "ctx"), "tp"),
        P(None, "tp"),
        P("tp"),
        P(None, "tp"),
        P("tp"),
        P("tp"),
        P("tp"),
        P("tp"),
        P("tp"),
        P("tp", ("dp", "ctx")),
        P(("dp", "ctx"), None),
    )
    return jax.shard_map(
        per_device,
        mesh=mesh,
        in_specs=placed,
        out_specs=(
            P(("dp", "ctx"), None),
            P(("dp", "ctx"), None),
            P(),
            P(("dp", "ctx"), "tp"),
            P(("dp", "ctx"), "tp"),
            P(("dp", "ctx"), "tp"),
            P(("dp", "ctx"), "tp"),
            P(None, "tp"),
            P("tp"),
            P(None, "tp"),
            P("tp"),
            P("tp"),
            P("tp"),
            P("tp"),
            P("tp"),
            P("tp", ("dp", "ctx")),
        ),
        check_vma=False,
    )
```

```python
import functools
from types import SimpleNamespace

import jax
import jax.numpy as jnp
from jax import lax
from jax.experimental import pallas as pl
from jax.experimental.pallas import tpu as pltpu
from jax.sharding import PartitionSpec as P

STRETCH = 128
LANES = 128
HALO = 16
MISC = 80
PAD = 16
CHUNK = 32
LEAD = 2
MOVED = 2
STORES = (
    "block",
    "tokens",
    "gain",
    "gate",
    "in",
    "state",
    "step",
    "in_kernel",
    "in_offset",
    "st_kernel",
    "st_offset",
    "bias",
    "decay",
    "skip",
    "gated",
    "out",
)
SMALL_INPUTS = (
    "state_t",
    "step_t",
    "norm_gain",
    "input_kernel",
    "input_offset",
    "state_kernel",
    "state_offset",
    "step_bias",
    "decay_log",
    "skip_gain",
    "gated_gain",
)
epsilon = 1e-05
exact_mode = lax.Precision.HIGHEST
MESH = pl.DeviceIdType.MESH
low = jnp.bfloat16
wide = jnp.float32


def mm(left, right, dims, precision=None):
    return lax.dot_general(
        left, right, (dims, ((), ())), precision=precision, preferred_element_type=wide
    )


def line_up(peers):
    barrier = pltpu.get_barrier_semaphore()
    for peer in peers:
        pl.semaphore_signal(barrier, inc=1, device_id=peer, device_id_type=MESH)
    pl.semaphore_wait(barrier, len(peers))


def send_to(source, target, sends, recvs, peer):
    return pltpu.make_async_remote_copy(
        src_ref=source,
        dst_ref=target,
        send_sem=sends,
        recv_sem=recvs,
        device_id=peer,
        device_id_type=MESH,
    )


def span(index, size):
    return pl.ds(pl.multiple_of(index * size, size), size)


def each(count, body, carry=None):
    def step(i, carry):
        return body(i, carry)

    return lax.fori_loop(0, count, step, carry)


def causal_mask(size):
    down = lax.broadcasted_iota(jnp.int32, (size, size), 0)
    right = lax.broadcasted_iota(jnp.int32, (size, size), 1)
    return down >= right


def widen(columns, width):
    rows, heads = columns.shape
    return jnp.concatenate(
        [jnp.broadcast_to(columns[:, h : h + 1], (rows, width)) for h in range(heads)], axis=1
    )


def tallen(column, width, lanes):
    return jnp.concatenate(
        [
            jnp.broadcast_to(column[h : h + 1, :], (width, lanes))
            for h in range(column.shape[0])
        ],
        axis=0,
    )


def per_head(values, heads):
    width = values.shape[1] // heads
    return jnp.concatenate(
        [
            jnp.sum(values[:, h * width : (h + 1) * width], axis=1, keepdims=True)
            for h in range(heads)
        ],
        axis=1,
    )


def turned(row):
    size = row.shape[1]
    down = lax.broadcasted_iota(jnp.int32, (size, size), 0)
    right = lax.broadcasted_iota(jnp.int32, (size, size), 1)
    return jnp.sum(
        jnp.where(down == right, jnp.broadcast_to(row, (size, size)), 0.0), axis=1, keepdims=True
    )


def laid(column):
    size = column.shape[0]
    down = lax.broadcasted_iota(jnp.int32, (size, size), 0)
    right = lax.broadcasted_iota(jnp.int32, (size, size), 1)
    return jnp.sum(
        jnp.where(down == right, jnp.broadcast_to(column, (size, size)), 0.0), axis=0, keepdims=True
    )


def fold(values):
    total = values[:8]
    for k in range(1, values.shape[0] // 8):
        total = total + values[8 * k : 8 * k + 8]
    return total


def summed(values):
    return jnp.sum(values, axis=0, keepdims=True)


class Stored:
    def __init__(self, copy):
        self.drain = copy.wait


class Spots:
    def __init__(self, n, ctxn, tpn):
        self.n, self.ctxn, self.tpn = n, ctxn, tpn
        self.ctx = lax.axis_index("ctx")
        self.here = lax.axis_index("dp") * ctxn + self.ctx
        self.mine = lax.axis_index("tp")
        self.half = n // 2
        self.chip, self.core = lax.div(self.here, 2), lax.rem(self.here, 2)
        self.sibling = self.spot(2 * self.chip + 1 - self.core)
        self.group = [self.spot(lax.rem(self.here + step, n)) for step in range(1, n)]
        self.line = [{"tp": lax.rem(self.mine + step, tpn)} for step in range(1, tpn)]
        self.row = [{"ctx": lax.rem(self.ctx + step, ctxn)} for step in range(1, ctxn)]
        self.after = {"ctx": lax.rem(self.ctx + 1, ctxn)}
        self.before = {"ctx": lax.rem(self.ctx + ctxn - 1, ctxn)}

    def spot(self, index):
        return {"dp": lax.div(index, self.ctxn), "ctx": lax.rem(index, self.ctxn)}

    def across(self, step):
        return 2 * lax.rem(self.chip + step, self.half) + self.core


class Gather:
    def __init__(self, at, source, place, sems):
        self.at, self.source, self.place, self.sems = at, source, place, sems

    def launch(self):
        at, sems = self.at, self.sems
        here = self.place(at.here)
        self.own = pltpu.make_async_copy(self.source, here, sems.at[4, 0])
        self.own.start()
        self.copies = []
        for step in range(1, at.half):
            copy = send_to(
                self.source, here, sems.at[0, step], sems.at[1, step], at.spot(at.across(step))
            )
            copy.start()
            self.copies.append(copy)
        self.beside = send_to(self.source, here, sems.at[0, 0], sems.at[1, 0], at.sibling)
        self.beside.start()

    def relay(self):
        at, sems = self.at, self.sems
        self.passed = []
        for step in range(1, at.half):
            origin = self.place(at.across(at.half - step))
            self.copies[step - 1].wait_recv()
            copy = send_to(origin, origin, sems.at[2, step], sems.at[3, step], at.sibling)
            copy.start()
            self.passed.append(copy)

    def finish(self):
        self.own.wait()
        self.beside.wait_recv()
        for copy in self.passed:
            copy.wait_recv()

    def drain(self):
        self.beside.wait_send()
        for copy in self.copies + self.passed:
            copy.wait_send()


class Swap:
    def __init__(self, peers, places, slots, sems):
        self.copies = []
        for step, peer in enumerate(peers):
            copy = send_to(places(step), slots, sems.at[0, step], sems.at[1, step], peer)
            copy.start()
            self.copies.append(copy)

    def arrive(self):
        for copy in self.copies:
            copy.wait_recv()

    def drain(self):
        for copy in self.copies:
            copy.wait_send()


class Shift:
    def __init__(self, source, target, sems, peer, sends, receives):
        self.copy = send_to(source, target, sems.at[0], sems.at[1], peer)
        self.sends, self.receives = sends, receives

        @pl.when(sends)
        def _():
            self.copy.start()

    def arrive(self):
        @pl.when(self.receives)
        def _():
            self.copy.wait_recv()

    def drain(self):
        @pl.when(self.sends)
        def _():
            self.copy.wait_send()


class LineSum:
    def __init__(self, at, part, full, inbox, outbox, sems, chunk, hop, counts, finish):
        self.at, self.part, self.full, self.finish = at, part, full, finish
        self.inbox, self.outbox, self.sems, self.chunk = inbox, outbox, sems, chunk
        self.half = part.shape[0] // 2 // chunk
        self.hop, self.counts, self.offsets = hop, counts, (0, counts[0])
        tpn = at.tpn
        self.steps = max(counts) + hop * (2 * tpn - 3)
        self.far = [tpn - 1 - at.mine, at.mine]
        up, down = {"tp": lax.rem(at.mine + 1, tpn)}, {"tp": lax.rem(at.mine + tpn - 1, tpn)}
        self.ahead, self.back = [down, up], [up, down]

    def rows(self, stream, j):
        if stream == 0:
            return span(j, self.chunk)
        return span(self.half + j - (j // self.half) * (2 * self.half - self.counts[0]), self.chunk)

    def reduction(self, stream, j, source):
        return send_to(
            source,
            self.inbox.at[self.offsets[stream] + j],
            self.sems.at[0, self.offsets[stream] + j],
            self.sems.at[1, self.offsets[stream] + j],
            self.ahead[stream],
        )

    def spreading(self, stream, j):
        where = self.full.at[self.rows(stream, j)]
        return send_to(
            where, where, self.sems.at[2, self.offsets[stream] + j], self.sems.at[3, self.offsets[stream] + j], self.back[stream]
        )

    def begin(self, stream, start=0, stop=LEAD):
        @pl.when(self.far[stream] == 0)
        def _():
            for j in range(start, min(stop, self.counts[stream])):
                self.reduction(stream, j, self.part.at[self.rows(stream, j)]).start()

    def tick(self, stream, t):
        if t < 0 or t >= self.steps:
            return
        self.begin(stream, t + LEAD, t + LEAD + 1)
        far, tpn = self.far[stream], self.at.tpn
        j = t - self.hop * (far - 1)

        @pl.when((far > 0) & (j >= 0) & (j < self.counts[stream]))
        def _():
            rows = self.rows(stream, j)
            self.reduction(stream, j, self.outbox.at[self.offsets[stream] + j]).wait_recv()
            total = (self.part[rows].astype(wide) + self.inbox[self.offsets[stream] + j].astype(wide)).astype(low)

            @pl.when(far < tpn - 1)
            def _():
                self.outbox[self.offsets[stream] + j] = total
                self.reduction(stream, j, self.outbox.at[self.offsets[stream] + j]).start()

            @pl.when(far == tpn - 1)
            def _():
                self.full[rows] = total
                self.spreading(stream, j).start()
                self.finish(rows)

        i = t - self.hop * (2 * tpn - 3 - far)

        @pl.when((far < tpn - 1) & (i >= 0) & (i < self.counts[stream]))
        def _():
            self.spreading(stream, i).wait_recv()

            @pl.when(far > 0)
            def _():
                self.spreading(stream, i).start()

            self.finish(self.rows(stream, i))

    def drain(self):
        for stream in range(2):

            def one(j, carry):
                @pl.when(self.far[stream] < self.at.tpn - 1)
                def _():
                    self.reduction(stream, j, self.outbox.at[self.offsets[stream] + j]).wait_send()

                @pl.when(self.far[stream] > 0)
                def _():
                    self.spreading(stream, j).wait_send()

                return carry

            each(self.counts[stream], one)


class Scatter:
    def __init__(self, at, slot, beside_buf, out_buf, in_buf, sems):
        self.at, self.slot, self.sems = at, slot, sems
        self.beside_buf, self.out_buf, self.in_buf = beside_buf, out_buf, in_buf

    def pair(self):
        at, sems = self.at, self.sems
        self.beside = {}
        for step in list(range(1, at.half)) + [0]:
            other = 2 * lax.rem(at.chip + step, at.half) + 1 - at.core
            copy = send_to(
                self.slot(other),
                self.beside_buf.at[step],
                sems.at[0, step],
                sems.at[1, step],
                at.sibling,
            )
            copy.start()
            self.beside[step] = copy

    def cross(self):
        at, sems = self.at, self.sems
        self.copies = []
        for step in range(1, at.half):
            target = at.across(step)
            self.beside[step].wait_recv()
            self.out_buf[step] = (
                self.slot(target)[...].astype(wide) + self.beside_buf[step].astype(wide)
            ).astype(low)
            copy = send_to(
                self.out_buf.at[step],
                self.in_buf.at[step],
                sems.at[2, step],
                sems.at[3, step],
                at.spot(target),
            )
            copy.start()
            self.copies.append(copy)

    def collect(self):
        at = self.at
        self.beside[0].wait_recv()
        total = self.slot(at.here)[...].astype(wide) + self.beside_buf[0].astype(wide)
        for step in range(1, at.half):
            self.copies[step - 1].wait_recv()
            total = total + self.in_buf[step].astype(wide)
        return total

    def drain(self):
        for copy in list(self.beside.values()) + self.copies:
            copy.wait_send()


def chained(slots, count, here, heads, backward):
    rows = slots.shape[1] - heads
    width, lanes = rows // heads, slots.shape[2]
    before = jnp.zeros((rows, lanes), wide)
    for k in range(count):
        at = count - 1 - k if backward else k
        reached = at > here if backward else at < here
        grown = tallen(jnp.exp(slots[at, rows:]), width, lanes)
        before = jnp.where(reached, slots[at, :rows] + grown * before, before)
    return before


def conv_block(source, start, rows, width, kernel, offset):
    taps = kernel.shape[0]
    around = source[pl.ds(start + HALO - 8, rows + 8), :width]
    total = offset
    for k in range(taps):
        first = 9 - taps + k
        total = total + kernel[k : k + 1] * around[first : first + rows]
    return total


def front(at, r, heads, out_sum):
    length, width = r.tok.shape
    inner = r.x.shape[1]
    head = inner // heads
    state_width = r.state_t.shape[0]
    nstate = r.bc.shape[1] // 2
    rows, columns = r.in_w.shape[0], r.out_w.shape[1]
    size, count = STRETCH, length // STRETCH
    half_length = length // 2

    loads = [
        pltpu.make_async_copy(getattr(r, "h_" + name), getattr(r, name), r.load_sems.at[3 + k])
        for k, name in enumerate(SMALL_INPUTS)
    ]
    for copy in loads:
        copy.start()
    load = pltpu.make_async_copy(r.tokens, r.tok, r.load_sems.at[0])
    load.start()
    load_cot = pltpu.make_async_copy(r.cotangent, r.cot, r.load_sems.at[1])
    load_cot.start()
    load_out = pltpu.make_async_copy(r.out_w, r.out_v, r.load_sems.at[2])
    load_out.start()
    for copy in loads:
        copy.wait()
    for h in range(heads):
        r.skip_row[:, h * head : (h + 1) * head] = jnp.broadcast_to(
            r.skip_gain[:, h : h + 1], (1, head)
        )
    taps = r.state_kernel.shape[0]
    r.taps_own[...] = jnp.concatenate(
        [r.state_kernel[...], r.state_offset[...], jnp.zeros((7 - taps, state_width), wide)], axis=0
    )
    r.taps_all[at.mine] = r.taps_own[...]
    r.step_own[...] = jnp.concatenate(
        [r.step_t[...].astype(wide), jnp.zeros((PAD - heads, rows), wide)], axis=0
    ).astype(low)

    line_up(at.group + at.line)

    g_in = Gather(at, r.in_w, lambda i: r.full_in.at[span(i, rows)], r.gather_sems.at[0])
    g_step = Gather(at, r.step_own, lambda i: r.step_slots.at[i], r.gather_sems.at[1])
    g_state = Gather(
        at, r.state_own, lambda i: r.full_state.at[span(i, rows)], r.gather_sems.at[4]
    )
    g_gate = Gather(at, r.gate_w, lambda i: r.full_gate.at[span(i, rows)], r.gather_sems.at[2])
    g_out = Gather(
        at, r.out_own, lambda i: r.full_out.at[span(i, columns)], r.gather_sems.at[3]
    )
    r.state_all[at.mine] = r.state_t[...]
    taps_swap = Swap(at.line, lambda k: r.taps_own, r.taps_all.at[at.mine], r.taps_sems)
    st_swap = Swap(at.line, lambda k: r.state_t, r.state_all.at[at.mine], r.bc_sems)
    g_step.launch()
    g_in.launch()
    rim = Shift(
        r.tokens.at[pl.ds(length - HALO, HALO)],
        r.tok_rim,
        r.rim_sems,
        at.after,
        at.ctx < at.ctxn - 1,
        at.ctx > 0,
    )

    load.wait()
    gain = r.norm_gain[...]

    def normal(tokens):
        tokens = tokens.astype(wide)
        inv = lax.rsqrt(jnp.mean(tokens * tokens, axis=-1, keepdims=True) + epsilon)
        return (tokens * inv * gain).astype(low)

    def norm_block(i, carry):
        r.norm[pl.ds(pl.multiple_of(HALO + i * 32, 16), 32)] = normal(r.tok[span(i, 32)])
        return carry

    each(length // 32, norm_block)

    @pl.when(at.ctx == 0)
    def _():
        r.tok_rim[...] = jnp.zeros_like(r.tok_rim)

    for k in range(length // LANES):
        r.norm_t[:, k * LANES : (k + 1) * LANES] = r.norm[
            HALO + k * LANES : HALO + (k + 1) * LANES
        ].T
    load_out.wait()
    r.out_own[...] = r.out_v[...].T
    st_swap.arrive()
    r.state_own[...] = jnp.concatenate([r.state_all[k] for k in range(at.tpn)], axis=0).T
    g_state.launch()
    g_gate.launch()
    rim.arrive()
    r.norm[:HALO] = normal(r.tok_rim[...])
    g_step.relay()
    g_in.relay()
    g_step.finish()
    for k in range(at.n):
        r.full_step[:, k * rows : (k + 1) * rows] = r.step_slots[k]
    g_in.finish()
    r.xp[...] = mm(r.norm[...], r.full_in[...], ((1,), (0,)))
    step_pre = mm(r.norm[HALO:], r.full_step[...], ((1,), (1,)))
    g_state.relay()
    g_out.launch()
    step_row = step_pre[:, :heads].T + turned(r.step_bias[...])
    dt_row = jnp.maximum(step_row, 0.0) + jnp.log1p(jnp.exp(-jnp.abs(step_row)))
    r.sig_row[...] = jax.nn.sigmoid(step_row)
    r.dt_row[...] = dt_row
    decays = -dt_row * turned(jnp.exp(r.decay_log[...]))
    r.decays[...] = decays
    causal = causal_mask(size)
    ones = jnp.where(causal, 1.0, 0.0)
    totals = []
    for s in range(count):
        cut = slice(s * size, (s + 1) * size)
        run = mm(decays[:, cut], ones, ((1,), (1,)), exact_mode)
        r.run_row[:, cut] = run
        total = run[:, size - 1 :]
        totals.append(total)
        left = jnp.exp(total - run)
        dts = dt_row[:, cut]
        r.cols[cut, : 5 * heads] = jnp.concatenate(
            [run, dts, left * dts, jnp.exp(run), left], axis=0
        ).T

    def value_block(i, carry):
        start = pl.multiple_of(i * 32, 32)
        pre = conv_block(r.xp, start, 32, inner, r.input_kernel, r.input_offset[...])
        sig = jax.nn.sigmoid(pre)
        act = pre * sig
        r.x[pl.ds(start, 32)] = act
        r.dsil_in[pl.ds(start, 32)] = sig + act * (1.0 - sig)
        return carry

    each(length // 32, value_block)

    g_state.finish()
    r.sp[...] = mm(r.norm[...], r.full_state[...], ((1,), (0,)))

    def state_block(i, carry):
        start = pl.multiple_of(i * 32, 32)
        pre = conv_block(
            r.sp, start, 32, 2 * nstate, r.full_kernel[...], r.full_offset[...]
        )
        sig = jax.nn.sigmoid(pre)
        act = pre * sig
        r.dsil_st[pl.ds(start, 32)] = sig + act * (1.0 - sig)
        r.bc[pl.ds(start, 32)] = act.astype(low)
        return carry

    taps_swap.arrive()
    r.full_kernel[...] = jnp.concatenate(
        [r.taps_all[k, : r.full_kernel.shape[0]] for k in range(at.tpn)], axis=1
    )
    r.full_offset[...] = jnp.concatenate(
        [r.taps_all[k, r.full_kernel.shape[0] : r.full_kernel.shape[0] + 1] for k in range(at.tpn)],
        axis=1,
    )
    each(length // 32, state_block)

    fresh = []
    state = jnp.zeros((inner, nstate), wide)
    for s in range(count):
        cut = slice(s * size, (s + 1) * size)
        tail = widen(r.cols[cut, 2 * heads : 3 * heads], head)
        added = mm((r.x[cut] * tail).astype(low), r.bc[cut, :nstate], ((0,), (0,)))
        r.fresh[s] = added
        state = tallen(jnp.exp(totals[s]), head, nstate) * state + added
    logs = jnp.broadcast_to(sum(totals), (heads, nstate))
    r.chain_own[:inner] = state
    r.chain_own[inner:] = logs
    r.chain_all[at.ctx] = r.chain_own[...]
    chain = Swap(at.row, lambda k: r.chain_own, r.chain_all.at[at.ctx], r.chain_sems)

    g_gate.relay()
    for s in range(count):
        cut = slice(s * size, (s + 1) * size)
        scores = mm(r.bc[cut, nstate:], r.bc[cut, :nstate], ((1,), (1,)))
        r.scores[s] = scores
        run = r.cols[cut, :heads]
        for h in range(0, heads, 2):
            pair = []
            for k in (h, h + 1):
                fall = jnp.exp(
                    jnp.where(causal, run[:, k : k + 1] - r.run_row[k : k + 1, cut], -1e30)
                )
                mixing = (fall * scores * r.dt_row[k : k + 1, cut]).astype(low)
                x_low = r.x[cut, k * head : (k + 1) * head].astype(low)
                pair.append(mm(mixing, x_low, ((1,), (0,))))
            r.scanned[cut, h * head : (h + 2) * head] = jnp.concatenate(pair, axis=1)
        if s == 0:
            g_gate.finish()
            r.gate[...] = mm(r.norm[HALO:], r.full_gate[...], ((1,), (0,)))

    g_out.relay()
    g_out.finish()
    load_cot.wait()
    r.pull[...] = mm(r.cot[...], r.full_out[...], ((1,), (0,)))

    chain.arrive()
    state = chained(r.chain_all, at.ctxn, at.ctx, heads, False)
    for s in range(count):
        cut = slice(s * size, (s + 1) * size)
        kept = state.astype(low)
        r.kept[s] = kept
        if s + 1 < count:
            state = tallen(jnp.exp(totals[s]), head, nstate) * state + r.fresh[s]
        grown = widen(r.cols[cut, 3 * heads : 4 * heads], head)
        r.carried[cut] = mm(r.bc[cut, nstate:], kept, ((1,), (1,))) * grown

    def gate_block(i, carry):
        here = span(i, 32)
        gate = r.gate[here]
        sig = jax.nn.sigmoid(gate)
        scanned = r.scanned[here] + r.carried[here] + r.skip_row[...] * r.x[here]
        r.scanned[here] = scanned
        gated = scanned * (gate * sig)
        scaled = (gated * r.gated_gain[...]).astype(low)
        r.scaled[here] = scaled
        squares = jnp.sum(gated * gated, axis=1, keepdims=True)
        dots = jnp.sum(scaled.astype(wide) * r.pull[here], axis=1, keepdims=True)
        r.stat[here] = jnp.concatenate([squares, dots, jnp.zeros((32, 6), wide)], axis=1)
        return carry

    each(length // 32, gate_block)
    mine = r.stat[...].T
    r.stat_own[...] = mine
    r.stat_all[at.mine] = mine
    stats = Swap(at.line, lambda k: r.stat_own, r.stat_all.at[at.mine], r.stat_sems)
    r.po[...] = mm(r.scaled[...], r.full_out[...], ((1,), (1,))).astype(low)
    for stream in range(2):
        out_sum.begin(stream)
    stats.arrive()
    total = r.stat_all[0]
    for k in range(1, at.tpn):
        total = total + r.stat_all[k]
    channels = inner * at.tpn
    inv = lax.rsqrt(total[0:1] / channels + epsilon)
    rms = -0.5 * inv * inv * inv * total[1:2] / channels
    r.inv[...] = jnp.concatenate([inv, rms, jnp.zeros((6, length), wide)], axis=0).T
    return [g_in, g_step, g_state, g_gate, g_out, rim, st_swap, taps_swap, chain, stats]


def out_line(at, r):
    def block_rows(here):
        r.v_block[here] = (
            r.tok[here].astype(wide) + r.inv[here, 0:1] * r.po_full[here].astype(wide)
        ).astype(low)

    half = r.po.shape[0] // 2 // CHUNK
    return LineSum(at, r.po, r.po_full, r.po_in, r.po_out, r.po_sems, CHUNK, 3, (half, half), block_rows)


def back(at, r, heads, out_sum):
    length, width = r.tok.shape
    inner = r.x.shape[1]
    head = inner // heads
    state_width = r.state_t.shape[0]
    nstate = r.bc.shape[1] // 2
    states = 2 * nstate
    rows, columns = r.in_w.shape[0], r.out_w.shape[1]
    taps = r.input_kernel.shape[0]
    size, count = STRETCH, length // STRETCH
    hl = length // 2
    causal = causal_mask(size)
    ones = jnp.where(causal, 1.0, 0.0)
    drains = []

    def store(name):
        index = STORES.index(name)
        copy = pltpu.make_async_copy(
            getattr(r, "v_" + name), getattr(r, "o_" + name), r.store_sems.at[index]
        )
        copy.start()
        drains.append(Stored(copy))

    def token_rows(here):
        tokens = r.tok[here].astype(wide)
        inv = lax.rsqrt(jnp.mean(tokens * tokens, axis=-1, keepdims=True) + epsilon)
        scaled = r.npl_full[here].astype(wide) * r.norm_gain[...]
        along = jnp.mean(scaled * tokens, axis=-1, keepdims=True)
        r.v_tokens[here] = (
            r.cot[here].astype(wide) + inv * scaled - tokens * (inv * inv * inv * along)
        )

    whole_half = hl // CHUNK
    norm_sum = LineSum(
        at, r.npl, r.npl_full, r.npl_in, r.npl_out, r.npl_sems, CHUNK, 2, (whole_half - MOVED, whole_half + MOVED), token_rows
    )
    early = whole_half - 1
    out_ticks = iter(range(out_sum.steps))
    late_ticks = iter(range(norm_sum.steps))
    first_ticks = iter(range(norm_sum.steps))

    def serve():
        t = next(out_ticks, None)
        if t is None:
            return False
        for stream in range(2):
            out_sum.tick(stream, t)
        if t == out_sum.steps - 1:
            store("block")
        return True

    def lead():
        norm_sum.tick(1, next(late_ticks, -1))

    def tail():
        serve()
        t = next(first_ticks, None)
        if t is None:
            return False
        norm_sum.tick(0, t)
        lead()
        return True

    serve()
    def grad_block(i, carry):
        gains, skips = carry
        here = span(i, 32)
        inv, rms = r.inv[here, 0:1], r.inv[here, 1:2]
        gate, scanned = r.gate[here], r.scanned[here]
        sig = jax.nn.sigmoid(gate)
        silu = gate * sig
        gated = scanned * silu
        scaled_grad = inv * r.pull[here]
        gains = gains + fold(scaled_grad * gated)
        gated_grad = scaled_grad * r.gated_gain[...] + 2.0 * rms * gated
        dy = gated_grad * silu
        r.dy[here] = dy
        r.gate_low[here] = (gated_grad * scanned * (sig + silu * (1.0 - sig))).astype(low)
        skips = skips + fold(dy * r.x[here])
        r.proj_grad[here] = (inv * r.cot[here].astype(wide)).astype(low)
        return gains, skips

    zero = jnp.zeros((8, inner), wide)
    gains, skips = each(length // 32, grad_block, (zero, zero))
    gain_row, skip_row = summed(gains), per_head(summed(skips), heads)
    serve()

    state = jnp.zeros((inner, nstate), wide)
    totals = [r.run_row[:, (s + 1) * size - 1 : (s + 1) * size] for s in range(count)]
    for s in reversed(range(count)):
        cut = slice(s * size, (s + 1) * size)
        grown = widen(r.cols[cut, 3 * heads : 4 * heads], head)
        dy_grown = r.dy[cut] * grown
        dy_low = dy_grown.astype(low)
        added = mm(dy_low, r.bc[cut, nstate:], ((0,), (0,)))
        r.fresh[s] = added
        state = tallen(jnp.exp(totals[s]), head, nstate) * state + added
        kept = r.kept[s]
        r.dyc[cut] = per_head(dy_grown * mm(r.bc[cut, nstate:], kept, ((1,), (1,))), heads)
        r.dbc[cut, nstate:] = mm(dy_low, kept, ((1,), (0,)))
    r.turn_own[:inner] = state
    r.turn_own[inner:] = jnp.broadcast_to(sum(totals), (heads, nstate))
    r.turn_all[at.ctx] = r.turn_own[...]
    chain = Swap(at.row, lambda k: r.turn_own, r.turn_all.at[at.ctx], r.turn_sems)
    drains.append(chain)
    serve()

    def within(s, serves):
        cut = slice(s * size, (s + 1) * size)
        b, c = r.bc[cut, :nstate], r.bc[cut, nstate:]
        run = r.cols[cut, :heads]
        scores = r.scores[s]
        dscores = jnp.zeros((size, size), wide)
        across, down = [], []
        for h in range(0, heads, 2):
            pair = []
            for k in (h, h + 1):
                lanes = slice(k * head, (k + 1) * head)
                fall = jnp.exp(
                    jnp.where(causal, run[:, k : k + 1] - r.run_row[k : k + 1, cut], -1e30)
                )
                dt = r.dt_row[k : k + 1, cut]
                dy_low = r.dy[cut, lanes].astype(low)
                products = mm(dy_low, r.x[cut, lanes].astype(low), ((1,), (1,))) * fall
                dscores = dscores + products * dt
                terms = products * scores
                down.append(jnp.sum(terms, axis=0, keepdims=True))
                across.append(jnp.sum(terms * dt, axis=1, keepdims=True))
                mixing = (fall * scores * dt).astype(low)
                pair.append(mm(mixing, dy_low, ((0,), (0,))))
                if k == h:
                    serves()
            r.dx[cut, h * head : (h + 2) * head] = jnp.concatenate(pair, axis=1)
            serves()
        dscores = dscores.astype(low)
        r.dbc[cut, :nstate] = mm(dscores, c, ((0,), (0,)))
        r.dbc[cut, nstate:] += mm(dscores, b, ((1,), (0,)))
        r.down[:, cut] = jnp.concatenate(down, axis=0)
        r.dyc[cut] += jnp.concatenate(across, axis=1)

    decay_rates = turned(jnp.exp(r.decay_log[...]))
    bias_grad = jnp.zeros((heads, 1), wide)
    decay_grad = jnp.zeros((heads, 1), wide)

    def between(s, state):
        cut = slice(s * size, (s + 1) * size)
        state_low = state.astype(low)
        x = r.x[cut]
        spare = widen(r.cols[cut, 2 * heads : 3 * heads], head)
        fade = widen(r.cols[cut, 4 * heads : 5 * heads], head)
        pulled = mm(r.bc[cut, :nstate], state_low, ((1,), (1,)))
        r.dbc[cut, :nstate] += mm((x * spare).astype(low), state_low, ((1,), (0,)))
        tail_grad = per_head(x * fade * pulled, heads)
        r.dx[cut] += spare * pulled + r.skip_row[...] * r.dy[cut]
        shrink = tallen(jnp.exp(totals[s]), head, nstate)
        lost = shrink * state * r.kept[s].astype(wide)
        lost = jnp.concatenate(
            [summed(lost[h * head : (h + 1) * head]) for h in range(heads)], axis=0
        )
        both = jnp.concatenate([tail_grad, r.dyc[cut]], axis=1).T
        tail_row, drun = both[:heads], both[heads:]
        dt, down = r.dt_row[:, cut], r.down[:, cut]
        out_tail = tail_row * dt
        drun = drun - out_tail - down * dt
        dtotal = jnp.sum(lost, axis=1, keepdims=True) + jnp.sum(out_tail, axis=1, keepdims=True)
        ddecay = dtotal + mm(drun, ones, ((1,), (0,)), exact_mode)
        step_grad = (down + tail_row - ddecay * decay_rates) * r.sig_row[:, cut]
        r.step_low[cut] = jnp.concatenate(
            [step_grad.T, jnp.zeros((size, PAD - heads), wide)], axis=1
        ).astype(low)
        if s > 0:
            state = shrink * state + r.fresh[s]
        return (
            state,
            jnp.sum(step_grad, axis=1, keepdims=True),
            jnp.sum(ddecay * r.decays[:, cut], axis=1, keepdims=True),
        )

    def unpull(source, kernel, start, size):
        around = source[pl.ds(start, size + 8)]
        total = kernel[taps - 1 : taps] * around[:size]
        for k in range(taps - 1):
            first = taps - 1 - k
            total = total + kernel[k : k + 1] * around[first : first + size]
        return total

    def low_blocks(start, blocks):
        def block(i, carry):
            here = pl.ds(pl.multiple_of(start + i * 32, 32), 32)
            first = pl.multiple_of(start + i * 32, 32)
            r.input_low[here] = unpull(r.dp, r.input_kernel[...], first, 32).astype(low)
            r.st_low[here] = unpull(r.dpt, r.full_kernel[...], first, 32).astype(low)
            return carry

        each(blocks, block)

    def scale_blocks(start):
        def block(i, carry):
            here = pl.ds(pl.multiple_of(start + i * 32, 32), 32)
            r.dp[here] = r.dx[here] * r.dsil_in[here]
            r.dpt[here] = r.dbc[here] * r.dsil_st[here]
            return carry

        each(hl // 32, block)

    def norm_part(pieces):
        def take(ref):
            if len(pieces) == 1:
                return ref[pieces[0]]
            return jnp.concatenate([ref[cut] for cut in pieces], axis=0)

        value = (
            mm(take(r.gate_low), r.full_gate[...], ((1,), (1,)))
            + mm(take(r.input_low), r.full_in[...], ((1,), (1,)))
            + mm(take(r.st_low), r.full_state[...], ((1,), (1,)))
            + mm(take(r.step_low), r.full_step[...], ((1,), (0,)))
        )
        first = 0
        for cut in pieces:
            r.np_[cut] = value[first : first + cut.stop - cut.start]
            first += cut.stop - cut.start

    def part_blocks(start, blocks, carry):
        def block(i, carry):
            here = pl.ds(pl.multiple_of(start + i * 32, 32), 32)
            tokens = r.tok[here].astype(wide)
            inv = lax.rsqrt(jnp.mean(tokens * tokens, axis=-1, keepdims=True) + epsilon)
            value = r.np_[here]
            r.npl[here] = value.astype(low)
            return carry + fold(value * (tokens * inv))

        return each(blocks, block, carry)

    def send_states(half):
        base = half * hl
        quarter = hl // 2
        for k in range(at.tpn):
            lanes = slice(k * state_width, (k + 1) * state_width)
            r.ds_own[half, k] = jnp.concatenate(
                [
                    r.dbc[base : base + quarter, lanes],
                    r.dbc[base + quarter : base + hl, lanes],
                ],
                axis=1,
            ).astype(low)
        turn = Swap(
            at.line,
            lambda k: r.ds_own.at[half, lax.rem(at.mine + k + 1, at.tpn)],
            r.ds_all.at[half, at.mine],
            r.ds_sems.at[half],
        )
        drains.append(turn)
        r.ds_all[half, at.mine] = r.ds_own[half, at.mine]
        return turn

    half_count = count // 2
    turns = {}
    gain_sums = jnp.zeros((8, width), wide)
    is_last, is_first = at.ctx == at.ctxn - 1, at.ctx == 0
    calls = []

    def some():
        calls.append(0)
        if len(calls) % 6 == 0:
            serve()

    for s in reversed(range(half_count, count)):
        within(s, some)
    chain.arrive()
    state = chained(r.turn_all, at.ctxn, at.ctx, heads, True)
    for s in reversed(range(half_count, count)):
        state, more_bias, more_decay = between(s, state)
        bias_grad, decay_grad = bias_grad + more_bias, decay_grad + more_decay
        serve()
    scale_blocks(hl)
    low_blocks(hl, early)
    serve()
    norm_part([slice(hl, length - CHUNK)])
    gain_sums = part_blocks(hl, early, gain_sums)
    norm_sum.begin(1)
    serve()
    turns[1] = send_states(1)

    r.g_gate[...] = mm(r.norm_t[...], r.gate_low[...], ((1,), (0,))).astype(low)
    s_gate = Scatter(
        at,
        lambda i: r.g_gate.at[span(i, rows)],
        r.gate_b,
        r.gate_o,
        r.gate_i,
        r.scatter_sems.at[0],
    )
    s_gate.pair()
    serve()
    for k in range(length // LANES):
        r.proj_t[:, k * LANES : (k + 1) * LANES] = r.proj_grad[k * LANES : (k + 1) * LANES].T
    r.g_out[...] = mm(r.proj_t[...], r.scaled[...], ((1,), (0,))).astype(low)
    s_out = Scatter(
        at,
        lambda i: r.g_out.at[span(i, columns)],
        r.out_b,
        r.out_o,
        r.out_i,
        r.scatter_sems.at[1],
    )
    s_gate.cross()
    s_out.pair()
    serve()

    turn_taken = []

    def both_lines():
        turn_taken.append(0)
        if len(turn_taken) % 5 == 0:
            serve()
            lead_early()

    early_ticks = iter(range(early - LEAD))

    def lead_early():
        if next(early_ticks, None) is not None:
            lead()

    for s in reversed(range(half_count)):
        within(s, both_lines)
    s_out.cross()
    for s in reversed(range(half_count)):
        state, more_bias, more_decay = between(s, state)
        bias_grad, decay_grad = bias_grad + more_bias, decay_grad + more_decay
    turns[0] = send_states(0)
    scale_blocks(0)

    @pl.when(is_last)
    def _():
        r.dp[length:] = jnp.zeros((8, inner), wide)
        r.dpt[length:] = jnp.zeros((8, states), wide)

    rims = []
    for k, ref in enumerate((r.dp, r.dpt)):
        rims.append(
            Shift(
                ref.at[pl.ds(0, 8)],
                ref.at[pl.ds(length, 8)],
                r.back_sems.at[k],
                at.before,
                jnp.logical_not(is_first),
                jnp.logical_not(is_last),
            )
        )
    drains.extend(rims)
    serve()
    low_blocks(0, hl // 32)
    for rim in rims:
        rim.arrive()
    low_blocks(length - CHUNK, 1)
    lead_early()
    serve()
    norm_part([slice(length - CHUNK, length), slice(0, hl)])
    gain_sums = part_blocks(length - CHUNK, 1, gain_sums)
    gain_sums = part_blocks(0, hl // 32, gain_sums)
    for k in range(early):
        lead_early()
    norm_sum.begin(0)
    gain_part = summed(gain_sums)
    r.g_in[...] = mm(r.norm_t[...], r.input_low[...], ((1,), (0,))).astype(low)
    s_in = Scatter(
        at, lambda i: r.g_in.at[span(i, rows)], r.in_b, r.in_o, r.in_i, r.scatter_sems.at[2]
    )
    s_in.pair()
    tail()
    def tap_block(i, carry):
        around = r.xp[pl.ds(pl.multiple_of(i * 32, 32) + HALO - 8, 40)]
        grad = r.dp[span(i, 32)]
        out = [carry[0] + fold(grad)]
        for k in range(taps):
            first = 9 - taps + k
            out.append(carry[1 + k] + fold(grad * around[first : first + 32]))
        return tuple(out)

    tap_sums = each(length // 32, tap_block, (zero,) * (1 + taps))
    tap_sums = [summed(value) for value in tap_sums]
    s_in.cross()
    tail()

    tail()
    tail()
    quarter = hl // 2
    at_tp = lambda array: sum(
        jnp.where(at.mine == k, array[:, k * state_width : (k + 1) * state_width], 0.0)
        for k in range(at.tpn)
    )
    for half in (1, 0):
        turns[half].arrive()
        mine = r.ds_all[half, 0].astype(wide)
        for k in range(1, at.tpn):
            mine = mine + r.ds_all[half, k].astype(wide)
        for k in range(2):
            cut = slice(half * hl + k * quarter, half * hl + (k + 1) * quarter)
            r.dps[cut] = mine[:, k * state_width : (k + 1) * state_width] * at_tp(r.dsil_st[cut])

    @pl.when(is_last)
    def _():
        r.dps[length:] = jnp.zeros((8, state_width), wide)

    st_rim = Shift(
        r.dps.at[pl.ds(0, 8)],
        r.dps.at[pl.ds(length, 8)],
        r.back_sems.at[2],
        at.before,
        jnp.logical_not(is_first),
        jnp.logical_not(is_last),
    )
    drains.append(st_rim)
    st_grad = r.dps[:length]
    r.sp_own[...] = at_tp(r.sp[...])
    st_sums = [summed(st_grad)]
    for k in range(taps):
        first = HALO + 1 - taps + k
        st_sums.append(summed(st_grad * r.sp_own[first : first + length]))
    tail()
    st_rim.arrive()
    total = unpull(r.dps, r.state_kernel[...], 0, length)
    r.misc_low[...] = jnp.concatenate(
        [total, r.step_low[...].astype(wide)], axis=1
    ).astype(low)
    grads = mm(r.misc_low[...], r.norm[HALO:], ((0,), (0,))).astype(low)
    for k in range(at.n):
        r.g_misc[k] = grads[:, k * rows : (k + 1) * rows]
    s_misc = Scatter(
        at, lambda i: r.g_misc.at[i], r.misc_b, r.misc_o, r.misc_i, r.scatter_sems.at[3]
    )
    s_misc.pair()
    tail()

    r.small[...] = jnp.zeros_like(r.small)

    def put(row, values):
        lanes = values.shape[1]
        for k in range(-(-lanes // LANES)):
            stop = min(LANES, lanes - k * LANES)
            r.small[row + k : row + k + 1, :stop] = values[:, k * LANES : k * LANES + stop]

    place = {}
    at_row = 0
    for name, values in (
        [("gain", gain_part)]
        + [("in%d" % k, tap_sums[1 + k]) for k in range(taps)]
        + [("inoff", tap_sums[0]), ("gated", gain_row)]
        + [("st%d" % k, st_sums[1 + k]) for k in range(taps)]
        + [("stoff", st_sums[0]), ("skip", skip_row)]
        + [("bias", laid(bias_grad)), ("decay", laid(decay_grad))]
    ):
        place[name] = (at_row, values.shape[1])
        put(at_row, values)
        at_row += -(-values.shape[1] // LANES)
    r.small_in[at.here] = r.small[...]
    smalls = Swap(at.group, lambda k: r.small, r.small_in.at[at.here], r.small_sems)
    drains.append(smalls)
    tail()
    s_misc.cross()

    r.v_gate[...] = s_gate.collect()
    store("gate")
    tail()
    r.v_out[...] = s_out.collect().T
    store("out")
    tail()

    smalls.arrive()
    total = r.small_in[0]
    for k in range(1, at.n):
        total = total + r.small_in[k]
    r.total[...] = total
    gain_rows = width // LANES
    r.gain_own[...] = total[:gain_rows]
    r.gain_all[at.mine] = total[:gain_rows]
    gains = Swap(at.line, lambda k: r.gain_own, r.gain_all.at[at.mine], r.gain_sems)
    drains.append(gains)
    tail()

    def get(name):
        row, lanes = place[name]
        return [
            r.total[row + k : row + k + 1, : min(LANES, lanes - k * LANES)]
            for k in range(-(-lanes // LANES))
        ]

    def lay(target, row, name):
        for k, value in enumerate(get(name)):
            target[row : row + 1, k * LANES : k * LANES + value.shape[1]] = value

    for k in range(taps):
        lay(r.v_in_kernel, k, "in%d" % k)
        lay(r.v_st_kernel, k, "st%d" % k)
    lay(r.v_in_offset, 0, "inoff")
    lay(r.v_st_offset, 0, "stoff")
    lay(r.v_gated, 0, "gated")
    lay(r.v_skip, 0, "skip")
    lay(r.v_bias, 0, "bias")
    lay(r.v_decay, 0, "decay")
    for name in ("in_kernel", "st_kernel", "in_offset", "st_offset", "gated", "skip"):
        store(name)
    store("bias")
    store("decay")
    tail()
    r.v_in[...] = s_in.collect()
    store("in")
    tail()
    misc = s_misc.collect()
    r.v_state[...] = misc[:state_width]
    r.v_step[...] = misc[state_width : state_width + heads]
    store("state")
    store("step")
    tail()
    gains.arrive()
    total = r.gain_all[0]
    for k in range(1, at.tpn):
        total = total + r.gain_all[k]
    r.v_gain[...] = total
    store("gain")

    while tail():
        pass
    store("tokens")

    for scatter in (s_gate, s_out, s_in, s_misc):
        scatter.drain()
    out_sum.drain()
    norm_sum.drain()
    return drains


def whole_kernel(n, ctxn, tpn, heads, names, *refs):
    r = SimpleNamespace(**dict(zip(names, refs)))
    r.dx, r.dy, r.np_ = r.carried, r.pull, r.v_tokens
    at = Spots(n, ctxn, tpn)
    out_sum = out_line(at, r)
    drains = front(at, r, heads, out_sum)
    drains += back(at, r, heads, out_sum)
    for item in drains:
        item.drain()


def emit_kernel(count, *refs):
    sources, targets, held = refs[:count], refs[count : 2 * count], refs[2 * count : 3 * count]
    sems = refs[3 * count]
    loads = [pltpu.make_async_copy(sources[k], held[k], sems.at[0, k]) for k in range(count)]
    stores = [pltpu.make_async_copy(held[k], targets[k], sems.at[1, k]) for k in range(count)]
    for copy in loads:
        copy.start()
    for k in range(count):
        loads[k].wait()
        stores[k].start()
    for copy in stores:
        copy.wait()


def emit(arrays):
    count = len(arrays)
    return pl.pallas_call(
        functools.partial(emit_kernel, count),
        out_shape=tuple(jax.ShapeDtypeStruct(a.shape, a.dtype) for a in arrays),
        in_specs=[pl.BlockSpec(memory_space=pl.ANY)] * count,
        out_specs=(pl.BlockSpec(memory_space=pl.ANY),) * count,
        scratch_shapes=[pltpu.VMEM(a.shape, a.dtype) for a in arrays]
        + [pltpu.SemaphoreType.DMA((2, count))],
        compiler_params=pltpu.CompilerParams(vmem_limit_bytes=62 * 2**20),
    )(*arrays)


def per_device(
    tokens,
    norm_gain,
    gate_weight,
    input_weight,
    state_weight,
    step_weight,
    input_kernel,
    input_offset,
    state_kernel,
    state_offset,
    step_bias,
    decay_log,
    skip_gain,
    gated_gain,
    out_weight,
    cotangent,
):
    ctxn = lax.axis_size("ctx")
    n, tpn = lax.axis_size("dp") * ctxn, lax.axis_size("tp")
    length, width = tokens.shape
    rows, inner = input_weight.shape
    state_width, heads = state_weight.shape[1], step_weight.shape[1]
    columns = out_weight.shape[1]
    nstate = state_width * tpn // 2
    head = inner // heads
    taps = input_kernel.shape[0]
    count = length // STRETCH
    half = n // 2
    steps = length // 2 // CHUNK
    hl = length // 2
    row = lambda a: a.reshape(1, a.shape[0])
    inputs = dict(
        tokens=tokens,
        cotangent=cotangent,
        in_w=input_weight,
        gate_w=gate_weight,
        out_w=out_weight,
        h_state_t=state_weight.T,
        h_step_t=step_weight.T,
        h_norm_gain=row(norm_gain),
        h_input_kernel=input_kernel,
        h_input_offset=row(input_offset),
        h_state_kernel=state_kernel,
        h_state_offset=row(state_offset),
        h_step_bias=row(step_bias),
        h_decay_log=row(decay_log),
        h_skip_gain=row(skip_gain),
        h_gated_gain=row(gated_gain),
    )
    outputs = dict(
        o_block=((length, width), low),
        o_tokens=((length, width), wide),
        o_gain=((width // LANES, LANES), wide),
        o_gate=((rows, inner), wide),
        o_in=((rows, inner), wide),
        o_state=((state_width, rows), wide),
        o_step=((heads, rows), wide),
        o_in_kernel=((taps, inner), wide),
        o_in_offset=((1, inner), wide),
        o_st_kernel=((taps, state_width), wide),
        o_st_offset=((1, state_width), wide),
        o_bias=((1, heads), wide),
        o_decay=((1, heads), wide),
        o_skip=((1, heads), wide),
        o_gated=((1, inner), wide),
        o_out=((inner, columns), wide),
    )
    small_rows = width // LANES + (taps + 2) * inner // LANES + (taps + 1) + 3
    small_rows = -(-small_rows // 8) * 8
    both = (length, inner)
    scratch = {
        name: (inputs["h_" + name].shape, inputs["h_" + name].dtype) for name in SMALL_INPUTS
    }
    scratch.update({"v" + name[1:]: value for name, value in outputs.items()})
    scratch.update(
        skip_row=((1, inner), wide),
        tok=((length, width), low),
        cot=((length, width), low),
        tok_rim=((HALO, width), low),
        step_own=((PAD, rows), low),
        step_slots=((n, PAD, rows), low),
        full_step=((PAD, width), low),
        state_own=((rows, 2 * nstate), low),
        state_all=((tpn, state_width, rows), low),
        full_state=((width, 2 * nstate), low),
        taps_own=((8, state_width), wide),
        taps_all=((tpn, 8, state_width), wide),
        full_kernel=((taps, 2 * nstate), wide),
        full_offset=((1, 2 * nstate), wide),
        norm=((HALO + length, width), low),
        norm_t=((width, length), low),
        full_in=((width, inner), low),
        full_gate=((width, inner), low),
        full_out=((width, inner), low),
        out_v=((inner, columns), low),
        out_own=((columns, inner), low),
        sp=((HALO + length, 2 * nstate), wide),
        sp_own=((HALO + length, state_width), wide),
        dsil_st=((length, 2 * nstate), wide),
        bc=((length, 2 * nstate), low),
        xp=((HALO + length, inner), wide),
        x=(both, wide),
        dsil_in=(both, wide),
        sig_row=((heads, length), wide),
        dt_row=((heads, length), wide),
        decays=((heads, length), wide),
        run_row=((heads, length), wide),
        cols=((length, 5 * heads), wide),
        fresh=((count, inner, nstate), wide),
        chain_own=((inner + heads, nstate), wide),
        chain_all=((ctxn, inner + heads, nstate), wide),
        turn_own=((inner + heads, nstate), wide),
        turn_all=((ctxn, inner + heads, nstate), wide),
        scores=((count, STRETCH, STRETCH), wide),
        scanned=(both, wide),
        carried=(both, wide),
        gate=(both, wide),
        pull=(both, wide),
        kept=((count, inner, nstate), low),
        scaled=(both, low),
        proj_t=((width, length), low),
        stat=((length, 8), wide),
        stat_own=((8, length), wide),
        stat_all=((tpn, 8, length), wide),
        inv=((length, 8), wide),
        po=((length, width), low),
        po_full=((length, width), low),
        po_in=((2 * steps, CHUNK, width), low),
        po_out=((2 * steps, CHUNK, width), low),
        gate_low=(both, low),
        proj_grad=((length, width), low),
        dyc=((length, heads), wide),
        dbc=((length, 2 * nstate), wide),
        g_gate=((width, inner), low),
        gate_b=((half, rows, inner), low),
        gate_o=((half, rows, inner), low),
        gate_i=((half, rows, inner), low),
        g_in=((width, inner), low),
        in_b=((half, rows, inner), low),
        in_o=((half, rows, inner), low),
        in_i=((half, rows, inner), low),
        g_out=((width, inner), low),
        out_b=((half, columns, inner), low),
        out_o=((half, columns, inner), low),
        out_i=((half, columns, inner), low),
        g_misc=((n, MISC, rows), low),
        misc_b=((half, MISC, rows), low),
        misc_o=((half, MISC, rows), low),
        misc_i=((half, MISC, rows), low),
        down=((heads, length), wide),
        step_low=((length, PAD), low),
        st_low=((length, 2 * nstate), low),
        ds_own=((2, tpn, hl // 2, 2 * state_width), low),
        ds_all=((2, tpn, hl // 2, 2 * state_width), low),
        dpt=((length + 8, 2 * nstate), wide),
        dp=((length + 8, inner), wide),
        dps=((length + 8, state_width), wide),
        input_low=(both, low),
        misc_low=((length, MISC), low),
        npl=((length, width), low),
        npl_full=((length, width), low),
        npl_in=((2 * steps, CHUNK, width), low),
        npl_out=((2 * steps, CHUNK, width), low),
        small=((small_rows, LANES), wide),
        small_in=((n, small_rows, LANES), wide),
        total=((small_rows, LANES), wide),
        gain_own=((width // LANES, LANES), wide),
        gain_all=((tpn, width // LANES, LANES), wide),
    )
    sems = dict(
        store_sems=(len(STORES),),
        load_sems=(3 + len(SMALL_INPUTS),),
        gather_sems=(5, 5, half),
        rim_sems=(2,),
        bc_sems=(2, tpn),
        taps_sems=(2, tpn),
        chain_sems=(2, ctxn),
        turn_sems=(2, ctxn),
        stat_sems=(2, tpn),
        po_sems=(4, 2 * steps),
        npl_sems=(4, 2 * steps),
        scatter_sems=(4, 4, half),
        ds_sems=(2, 2, tpn),
        back_sems=(3, 2),
        small_sems=(2, n),
        gain_sems=(2, tpn),
    )
    names = list(inputs) + list(outputs) + list(scratch) + list(sems)
    results = pl.pallas_call(
        functools.partial(whole_kernel, n, ctxn, tpn, heads, names),
        out_shape=tuple(jax.ShapeDtypeStruct(*o) for o in outputs.values()),
        in_specs=[pl.BlockSpec(memory_space=pl.ANY)] * len(inputs),
        out_specs=(pl.BlockSpec(memory_space=pl.ANY),) * len(outputs),
        scratch_shapes=[pltpu.VMEM(*s) for s in scratch.values()]
        + [pltpu.SemaphoreType.DMA(s) for s in sems.values()],
        compiler_params=pltpu.CompilerParams(
            collective_id=0, has_side_effects=True, vmem_limit_bytes=62 * 2**20
        ),
    )(*inputs.values())
    o = SimpleNamespace(**dict(zip(outputs, emit(results))))
    return (
        o.o_block,
        o.o_tokens,
        o.o_gain.reshape(-1),
        o.o_gate,
        o.o_in,
        o.o_state.T,
        o.o_step.T,
        o.o_in_kernel,
        o.o_in_offset.reshape(-1),
        o.o_st_kernel,
        o.o_st_offset.reshape(-1),
        o.o_bias.reshape(-1),
        o.o_decay.reshape(-1),
        o.o_skip.reshape(-1),
        o.o_gated.reshape(-1),
        o.o_out,
    )


def solution(mesh):
    placed = (
        P(("dp", "ctx"), None),
        P(),
        P(("dp", "ctx"), "tp"),
        P(("dp", "ctx"), "tp"),
        P(("dp", "ctx"), "tp"),
        P(("dp", "ctx"), "tp"),
        P(None, "tp"),
        P("tp"),
        P(None, "tp"),
        P("tp"),
        P("tp"),
        P("tp"),
        P("tp"),
        P("tp"),
        P("tp", ("dp", "ctx")),
        P(("dp", "ctx"), None),
    )
    return jax.shard_map(
        per_device,
        mesh=mesh,
        in_specs=placed,
        out_specs=(
            P(("dp", "ctx"), None),
            P(("dp", "ctx"), None),
            P(),
            P(("dp", "ctx"), "tp"),
            P(("dp", "ctx"), "tp"),
            P(("dp", "ctx"), "tp"),
            P(("dp", "ctx"), "tp"),
            P(None, "tp"),
            P("tp"),
            P(None, "tp"),
            P("tp"),
            P("tp"),
            P("tp"),
            P("tp"),
            P("tp"),
            P("tp", ("dp", "ctx")),
        ),
        check_vma=False,
    )
```

```python
import functools
from types import SimpleNamespace

import jax
import jax.numpy as jnp
from jax import lax
from jax.experimental import pallas as pl
from jax.experimental.pallas import tpu as pltpu
from jax.sharding import PartitionSpec as P

STRETCH = 128
LANES = 128
HALO = 16
MISC = 80
PAD = 16
CHUNK = 32
LEAD = 2
MOVED = 2
STORES = (
    "block",
    "tokens",
    "gain",
    "gate",
    "in",
    "state",
    "step",
    "in_kernel",
    "in_offset",
    "st_kernel",
    "st_offset",
    "bias",
    "decay",
    "skip",
    "gated",
    "out",
)
SMALL_INPUTS = (
    "state_t",
    "step_t",
    "norm_gain",
    "input_kernel",
    "input_offset",
    "state_kernel",
    "state_offset",
    "step_bias",
    "decay_log",
    "skip_gain",
    "gated_gain",
)
epsilon = 1e-05
exact_mode = lax.Precision.HIGHEST
MESH = pl.DeviceIdType.MESH
low = jnp.bfloat16
wide = jnp.float32


def mm(left, right, dims, precision=None):
    return lax.dot_general(
        left, right, (dims, ((), ())), precision=precision, preferred_element_type=wide
    )


def line_up(peers):
    barrier = pltpu.get_barrier_semaphore()
    for peer in peers:
        pl.semaphore_signal(barrier, inc=1, device_id=peer, device_id_type=MESH)
    pl.semaphore_wait(barrier, len(peers))


def send_to(source, target, sends, recvs, peer):
    return pltpu.make_async_remote_copy(
        src_ref=source,
        dst_ref=target,
        send_sem=sends,
        recv_sem=recvs,
        device_id=peer,
        device_id_type=MESH,
    )


def span(index, size):
    return pl.ds(pl.multiple_of(index * size, size), size)


def each(count, body, carry=None):
    def step(i, carry):
        return body(i, carry)

    return lax.fori_loop(0, count, step, carry)


def causal_mask(size):
    down = lax.broadcasted_iota(jnp.int32, (size, size), 0)
    right = lax.broadcasted_iota(jnp.int32, (size, size), 1)
    return down >= right


def widen(columns, width):
    rows, heads = columns.shape
    return jnp.concatenate(
        [jnp.broadcast_to(columns[:, h : h + 1], (rows, width)) for h in range(heads)], axis=1
    )


def tallen(column, width, lanes):
    return jnp.concatenate(
        [
            jnp.broadcast_to(column[h : h + 1, :], (width, lanes))
            for h in range(column.shape[0])
        ],
        axis=0,
    )


def per_head(values, heads):
    width = values.shape[1] // heads
    return jnp.concatenate(
        [
            jnp.sum(values[:, h * width : (h + 1) * width], axis=1, keepdims=True)
            for h in range(heads)
        ],
        axis=1,
    )


def turned(row):
    size = row.shape[1]
    down = lax.broadcasted_iota(jnp.int32, (size, size), 0)
    right = lax.broadcasted_iota(jnp.int32, (size, size), 1)
    return jnp.sum(
        jnp.where(down == right, jnp.broadcast_to(row, (size, size)), 0.0), axis=1, keepdims=True
    )


def laid(column):
    size = column.shape[0]
    down = lax.broadcasted_iota(jnp.int32, (size, size), 0)
    right = lax.broadcasted_iota(jnp.int32, (size, size), 1)
    return jnp.sum(
        jnp.where(down == right, jnp.broadcast_to(column, (size, size)), 0.0), axis=0, keepdims=True
    )


def fold(values):
    total = values[:8]
    for k in range(1, values.shape[0] // 8):
        total = total + values[8 * k : 8 * k + 8]
    return total


def summed(values):
    return jnp.sum(values, axis=0, keepdims=True)


class Stored:
    def __init__(self, copy):
        self.drain = copy.wait


class Spots:
    def __init__(self, n, ctxn, tpn):
        self.n, self.ctxn, self.tpn = n, ctxn, tpn
        self.ctx = lax.axis_index("ctx")
        self.here = lax.axis_index("dp") * ctxn + self.ctx
        self.mine = lax.axis_index("tp")
        self.half = n // 2
        self.chip, self.core = lax.div(self.here, 2), lax.rem(self.here, 2)
        self.sibling = self.spot(2 * self.chip + 1 - self.core)
        self.group = [self.spot(lax.rem(self.here + step, n)) for step in range(1, n)]
        self.line = [{"tp": lax.rem(self.mine + step, tpn)} for step in range(1, tpn)]
        self.row = [{"ctx": lax.rem(self.ctx + step, ctxn)} for step in range(1, ctxn)]
        self.after = {"ctx": lax.rem(self.ctx + 1, ctxn)}
        self.before = {"ctx": lax.rem(self.ctx + ctxn - 1, ctxn)}

    def spot(self, index):
        return {"dp": lax.div(index, self.ctxn), "ctx": lax.rem(index, self.ctxn)}

    def across(self, step):
        return 2 * lax.rem(self.chip + step, self.half) + self.core


class Gather:
    def __init__(self, at, source, place, sems):
        self.at, self.source, self.place, self.sems = at, source, place, sems

    def launch(self):
        at, sems = self.at, self.sems
        here = self.place(at.here)
        self.own = pltpu.make_async_copy(self.source, here, sems.at[4, 0])
        self.own.start()
        self.copies = []
        for step in range(1, at.half):
            copy = send_to(
                self.source, here, sems.at[0, step], sems.at[1, step], at.spot(at.across(step))
            )
            copy.start()
            self.copies.append(copy)
        self.beside = send_to(self.source, here, sems.at[0, 0], sems.at[1, 0], at.sibling)
        self.beside.start()

    def relay(self):
        at, sems = self.at, self.sems
        self.passed = []
        for step in range(1, at.half):
            origin = self.place(at.across(at.half - step))
            self.copies[step - 1].wait_recv()
            copy = send_to(origin, origin, sems.at[2, step], sems.at[3, step], at.sibling)
            copy.start()
            self.passed.append(copy)

    def finish(self):
        self.own.wait()
        self.beside.wait_recv()
        for copy in self.passed:
            copy.wait_recv()

    def drain(self):
        self.beside.wait_send()
        for copy in self.copies + self.passed:
            copy.wait_send()


class Swap:
    def __init__(self, peers, places, slots, sems):
        self.copies = []
        for step, peer in enumerate(peers):
            copy = send_to(places(step), slots, sems.at[0, step], sems.at[1, step], peer)
            copy.start()
            self.copies.append(copy)

    def arrive(self):
        for copy in self.copies:
            copy.wait_recv()

    def drain(self):
        for copy in self.copies:
            copy.wait_send()


class Shift:
    def __init__(self, source, target, sems, peer, sends, receives):
        self.copy = send_to(source, target, sems.at[0], sems.at[1], peer)
        self.sends, self.receives = sends, receives

        @pl.when(sends)
        def _():
            self.copy.start()

    def arrive(self):
        @pl.when(self.receives)
        def _():
            self.copy.wait_recv()

    def drain(self):
        @pl.when(self.sends)
        def _():
            self.copy.wait_send()


class LineSum:
    def __init__(self, at, part, full, inbox, outbox, sems, chunk, hop, counts, finish):
        self.at, self.part, self.full, self.finish = at, part, full, finish
        self.inbox, self.outbox, self.sems, self.chunk = inbox, outbox, sems, chunk
        self.half = part.shape[0] // 2 // chunk
        self.hop, self.counts, self.offsets = hop, counts, (0, counts[0])
        tpn = at.tpn
        self.steps = max(counts) + hop * (2 * tpn - 3)
        self.far = [tpn - 1 - at.mine, at.mine]
        up, down = {"tp": lax.rem(at.mine + 1, tpn)}, {"tp": lax.rem(at.mine + tpn - 1, tpn)}
        self.ahead, self.back = [down, up], [up, down]

    def place(self, stream, j):
        if stream == 0:
            return j
        return self.half + j - (j // self.half) * (2 * self.half - self.counts[0])

    def rows(self, stream, j):
        return span(self.place(stream, j), self.chunk)

    def reduction(self, stream, j, source):
        return send_to(
            source,
            self.inbox.at[self.offsets[stream] + j],
            self.sems.at[0, self.offsets[stream] + j],
            self.sems.at[1, self.offsets[stream] + j],
            self.ahead[stream],
        )

    def spreading(self, stream, j):
        where = self.full.at[self.rows(stream, j)]
        return send_to(
            where, where, self.sems.at[2, self.offsets[stream] + j], self.sems.at[3, self.offsets[stream] + j], self.back[stream]
        )

    def begin(self, stream, start=0, stop=LEAD):
        @pl.when(self.far[stream] == 0)
        def _():
            for j in range(start, min(stop, self.counts[stream])):
                self.reduction(stream, j, self.part.at[self.rows(stream, j)]).start()

    def tick(self, stream, t):
        if t < 0 or t >= self.steps:
            return
        self.begin(stream, t + LEAD, t + LEAD + 1)
        far, tpn = self.far[stream], self.at.tpn
        j = t - self.hop * (far - 1)

        @pl.when((far > 0) & (j >= 0) & (j < self.counts[stream]))
        def _():
            rows = self.rows(stream, j)
            self.reduction(stream, j, self.outbox.at[self.offsets[stream] + j]).wait_recv()
            total = (self.part[rows].astype(wide) + self.inbox[self.offsets[stream] + j].astype(wide)).astype(low)

            @pl.when(far < tpn - 1)
            def _():
                self.outbox[self.offsets[stream] + j] = total
                self.reduction(stream, j, self.outbox.at[self.offsets[stream] + j]).start()

            @pl.when(far == tpn - 1)
            def _():
                self.full[rows] = total
                self.spreading(stream, j).start()
                self.finish(self.place(stream, j))

        i = t - self.hop * (2 * tpn - 3 - far)

        @pl.when((far < tpn - 1) & (i >= 0) & (i < self.counts[stream]))
        def _():
            self.spreading(stream, i).wait_recv()

            @pl.when(far > 0)
            def _():
                self.spreading(stream, i).start()

            self.finish(self.place(stream, i))

    def drain(self):
        for stream in range(2):

            def one(j, carry):
                @pl.when(self.far[stream] < self.at.tpn - 1)
                def _():
                    self.reduction(stream, j, self.outbox.at[self.offsets[stream] + j]).wait_send()

                @pl.when(self.far[stream] > 0)
                def _():
                    self.spreading(stream, j).wait_send()

                return carry

            each(self.counts[stream], one)


class Scatter:
    def __init__(self, at, slot, beside_buf, out_buf, in_buf, sems):
        self.at, self.slot, self.sems = at, slot, sems
        self.beside_buf, self.out_buf, self.in_buf = beside_buf, out_buf, in_buf

    def pair(self):
        at, sems = self.at, self.sems
        self.beside = {}
        for step in list(range(1, at.half)) + [0]:
            other = 2 * lax.rem(at.chip + step, at.half) + 1 - at.core
            copy = send_to(
                self.slot(other),
                self.beside_buf.at[step],
                sems.at[0, step],
                sems.at[1, step],
                at.sibling,
            )
            copy.start()
            self.beside[step] = copy

    def cross(self):
        at, sems = self.at, self.sems
        self.copies = []
        for step in range(1, at.half):
            target = at.across(step)
            self.beside[step].wait_recv()
            self.out_buf[step] = (
                self.slot(target)[...].astype(wide) + self.beside_buf[step].astype(wide)
            ).astype(low)
            copy = send_to(
                self.out_buf.at[step],
                self.in_buf.at[step],
                sems.at[2, step],
                sems.at[3, step],
                at.spot(target),
            )
            copy.start()
            self.copies.append(copy)

    def collect(self):
        at = self.at
        self.beside[0].wait_recv()
        total = self.slot(at.here)[...].astype(wide) + self.beside_buf[0].astype(wide)
        for step in range(1, at.half):
            self.copies[step - 1].wait_recv()
            total = total + self.in_buf[step].astype(wide)
        return total

    def drain(self):
        for copy in list(self.beside.values()) + self.copies:
            copy.wait_send()


def chained(slots, count, here, heads, backward):
    rows = slots.shape[1] - heads
    width, lanes = rows // heads, slots.shape[2]
    before = jnp.zeros((rows, lanes), wide)
    for k in range(count):
        at = count - 1 - k if backward else k
        reached = at > here if backward else at < here
        grown = tallen(jnp.exp(slots[at, rows:]), width, lanes)
        before = jnp.where(reached, slots[at, :rows] + grown * before, before)
    return before


def conv_block(source, start, rows, width, kernel, offset):
    taps = kernel.shape[0]
    around = source[pl.ds(start + HALO - 8, rows + 8), :width]
    total = offset
    for k in range(taps):
        first = 9 - taps + k
        total = total + kernel[k : k + 1] * around[first : first + rows]
    return total


def front(at, r, heads, out_sum):
    length, width = r.tok.shape
    inner = r.x.shape[1]
    head = inner // heads
    state_width = r.state_t.shape[0]
    nstate = r.bc.shape[1] // 2
    rows, columns = r.in_w.shape[0], r.out_w.shape[1]
    size, count = STRETCH, length // STRETCH
    half_length = length // 2

    loads = [
        pltpu.make_async_copy(getattr(r, "h_" + name), getattr(r, name), r.load_sems.at[3 + k])
        for k, name in enumerate(SMALL_INPUTS)
    ]
    for copy in loads:
        copy.start()
    load = pltpu.make_async_copy(r.tokens, r.tok, r.load_sems.at[0])
    load.start()
    load_cot = pltpu.make_async_copy(r.cotangent, r.cot, r.load_sems.at[1])
    load_cot.start()
    load_out = pltpu.make_async_copy(r.out_w, r.out_v, r.load_sems.at[2])
    load_out.start()
    for copy in loads:
        copy.wait()
    for h in range(heads):
        r.skip_row[:, h * head : (h + 1) * head] = jnp.broadcast_to(
            r.skip_gain[:, h : h + 1], (1, head)
        )
    taps = r.state_kernel.shape[0]
    r.taps_own[...] = jnp.concatenate(
        [r.state_kernel[...], r.state_offset[...], jnp.zeros((7 - taps, state_width), wide)], axis=0
    )
    r.taps_all[at.mine] = r.taps_own[...]
    r.step_own[...] = jnp.concatenate(
        [r.step_t[...].astype(wide), jnp.zeros((PAD - heads, rows), wide)], axis=0
    ).astype(low)

    line_up(at.group + at.line)

    g_in = Gather(at, r.in_w, lambda i: r.full_in.at[span(i, rows)], r.gather_sems.at[0])
    g_step = Gather(at, r.step_own, lambda i: r.step_slots.at[i], r.gather_sems.at[1])
    g_state = Gather(
        at, r.state_own, lambda i: r.full_state.at[span(i, rows)], r.gather_sems.at[4]
    )
    g_gate = Gather(at, r.gate_w, lambda i: r.full_gate.at[span(i, rows)], r.gather_sems.at[2])
    g_out = Gather(
        at, r.out_own, lambda i: r.full_out.at[span(i, columns)], r.gather_sems.at[3]
    )
    r.state_all[at.mine] = r.state_t[...]
    taps_swap = Swap(at.line, lambda k: r.taps_own, r.taps_all.at[at.mine], r.taps_sems)
    st_swap = Swap(at.line, lambda k: r.state_t, r.state_all.at[at.mine], r.bc_sems)
    g_step.launch()
    g_in.launch()
    rim = Shift(
        r.tokens.at[pl.ds(length - HALO, HALO)],
        r.tok_rim,
        r.rim_sems,
        at.after,
        at.ctx < at.ctxn - 1,
        at.ctx > 0,
    )

    load.wait()
    gain = r.norm_gain[...]

    def normal(tokens):
        tokens = tokens.astype(wide)
        inv = lax.rsqrt(jnp.mean(tokens * tokens, axis=-1, keepdims=True) + epsilon)
        return (tokens * inv * gain).astype(low)

    def norm_block(i, carry):
        r.norm[pl.ds(pl.multiple_of(HALO + i * 32, 16), 32)] = normal(r.tok[span(i, 32)])
        return carry

    each(length // 32, norm_block)

    @pl.when(at.ctx == 0)
    def _():
        r.tok_rim[...] = jnp.zeros_like(r.tok_rim)

    for k in range(length // LANES):
        r.norm_t[:, k * LANES : (k + 1) * LANES] = r.norm[
            HALO + k * LANES : HALO + (k + 1) * LANES
        ].T
    load_out.wait()
    r.out_own[...] = r.out_v[...].T
    st_swap.arrive()
    r.state_own[...] = jnp.concatenate([r.state_all[k] for k in range(at.tpn)], axis=0).T
    g_state.launch()
    g_gate.launch()
    rim.arrive()
    r.norm[:HALO] = normal(r.tok_rim[...])
    g_step.relay()
    g_in.relay()
    g_step.finish()
    for k in range(at.n):
        r.full_step[:, k * rows : (k + 1) * rows] = r.step_slots[k]
    g_in.finish()
    r.xp[...] = mm(r.norm[...], r.full_in[...], ((1,), (0,)))
    step_pre = mm(r.norm[HALO:], r.full_step[...], ((1,), (1,)))
    g_state.relay()
    g_out.launch()
    step_row = step_pre[:, :heads].T + turned(r.step_bias[...])
    dt_row = jnp.maximum(step_row, 0.0) + jnp.log1p(jnp.exp(-jnp.abs(step_row)))
    r.sig_row[...] = jax.nn.sigmoid(step_row)
    r.dt_row[...] = dt_row
    decays = -dt_row * turned(jnp.exp(r.decay_log[...]))
    r.decays[...] = decays
    causal = causal_mask(size)
    ones = jnp.where(causal, 1.0, 0.0)
    totals = []
    for s in range(count):
        cut = slice(s * size, (s + 1) * size)
        run = mm(decays[:, cut], ones, ((1,), (1,)), exact_mode)
        r.run_row[:, cut] = run
        total = run[:, size - 1 :]
        totals.append(total)
        left = jnp.exp(total - run)
        dts = dt_row[:, cut]
        r.cols[cut, : 5 * heads] = jnp.concatenate(
            [run, dts, left * dts, jnp.exp(run), left], axis=0
        ).T

    def value_block(i, carry):
        start = pl.multiple_of(i * 32, 32)
        pre = conv_block(r.xp, start, 32, inner, r.input_kernel, r.input_offset[...])
        sig = jax.nn.sigmoid(pre)
        act = pre * sig
        r.x[pl.ds(start, 32)] = act
        r.dsil_in[pl.ds(start, 32)] = sig + act * (1.0 - sig)
        return carry

    each(length // 32, value_block)

    g_state.finish()
    r.sp[...] = mm(r.norm[...], r.full_state[...], ((1,), (0,)))

    def state_block(i, carry):
        start = pl.multiple_of(i * 32, 32)
        pre = conv_block(
            r.sp, start, 32, 2 * nstate, r.full_kernel[...], r.full_offset[...]
        )
        sig = jax.nn.sigmoid(pre)
        act = pre * sig
        r.dsil_st[pl.ds(start, 32)] = sig + act * (1.0 - sig)
        r.bc[pl.ds(start, 32)] = act.astype(low)
        return carry

    taps_swap.arrive()
    r.full_kernel[...] = jnp.concatenate(
        [r.taps_all[k, : r.full_kernel.shape[0]] for k in range(at.tpn)], axis=1
    )
    r.full_offset[...] = jnp.concatenate(
        [r.taps_all[k, r.full_kernel.shape[0] : r.full_kernel.shape[0] + 1] for k in range(at.tpn)],
        axis=1,
    )
    each(length // 32, state_block)

    fresh = []
    state = jnp.zeros((inner, nstate), wide)
    for s in range(count):
        cut = slice(s * size, (s + 1) * size)
        tail = widen(r.cols[cut, 2 * heads : 3 * heads], head)
        added = mm((r.x[cut] * tail).astype(low), r.bc[cut, :nstate], ((0,), (0,)))
        r.fresh[s] = added
        state = tallen(jnp.exp(totals[s]), head, nstate) * state + added
    logs = jnp.broadcast_to(sum(totals), (heads, nstate))
    r.chain_own[:inner] = state
    r.chain_own[inner:] = logs
    r.chain_all[at.ctx] = r.chain_own[...]
    chain = Swap(at.row, lambda k: r.chain_own, r.chain_all.at[at.ctx], r.chain_sems)

    g_gate.relay()
    for s in range(count):
        cut = slice(s * size, (s + 1) * size)
        scores = mm(r.bc[cut, nstate:], r.bc[cut, :nstate], ((1,), (1,)))
        r.scores[s] = scores
        run = r.cols[cut, :heads]
        for h in range(0, heads, 2):
            pair = []
            for k in (h, h + 1):
                fall = jnp.exp(
                    jnp.where(causal, run[:, k : k + 1] - r.run_row[k : k + 1, cut], -1e30)
                )
                mixing = (fall * scores * r.dt_row[k : k + 1, cut]).astype(low)
                x_low = r.x[cut, k * head : (k + 1) * head].astype(low)
                pair.append(mm(mixing, x_low, ((1,), (0,))))
            r.scanned[cut, h * head : (h + 2) * head] = jnp.concatenate(pair, axis=1)
        if s == 0:
            g_gate.finish()
            r.gate[...] = mm(r.norm[HALO:], r.full_gate[...], ((1,), (0,)))

    g_out.relay()
    g_out.finish()
    load_cot.wait()
    r.pull[...] = mm(r.cot[...], r.full_out[...], ((1,), (0,)))

    chain.arrive()
    state = chained(r.chain_all, at.ctxn, at.ctx, heads, False)
    for s in range(count):
        cut = slice(s * size, (s + 1) * size)
        kept = state.astype(low)
        r.kept[s] = kept
        if s + 1 < count:
            state = tallen(jnp.exp(totals[s]), head, nstate) * state + r.fresh[s]
        grown = widen(r.cols[cut, 3 * heads : 4 * heads], head)
        r.carried[cut] = mm(r.bc[cut, nstate:], kept, ((1,), (1,))) * grown

    def gate_block(i, carry):
        here = span(i, 32)
        gate = r.gate[here]
        sig = jax.nn.sigmoid(gate)
        scanned = r.scanned[here] + r.carried[here] + r.skip_row[...] * r.x[here]
        r.scanned[here] = scanned
        gated = scanned * (gate * sig)
        scaled = (gated * r.gated_gain[...]).astype(low)
        r.scaled[here] = scaled
        squares = jnp.sum(gated * gated, axis=1, keepdims=True)
        dots = jnp.sum(scaled.astype(wide) * r.pull[here], axis=1, keepdims=True)
        r.stat[here] = jnp.concatenate([squares, dots, jnp.zeros((32, 6), wide)], axis=1)
        return carry

    each(length // 32, gate_block)
    mine = r.stat[...].T
    r.stat_own[...] = mine
    r.stat_all[at.mine] = mine
    stats = Swap(at.line, lambda k: r.stat_own, r.stat_all.at[at.mine], r.stat_sems)
    r.po[...] = mm(r.scaled[...], r.full_out[...], ((1,), (1,))).astype(low)
    for stream in range(2):
        out_sum.begin(stream)
    stats.arrive()
    total = r.stat_all[0]
    for k in range(1, at.tpn):
        total = total + r.stat_all[k]
    channels = inner * at.tpn
    inv = lax.rsqrt(total[0:1] / channels + epsilon)
    rms = -0.5 * inv * inv * inv * total[1:2] / channels
    r.inv[...] = jnp.concatenate([inv, rms, jnp.zeros((6, length), wide)], axis=0).T
    return [g_in, g_step, g_state, g_gate, g_out, rim, st_swap, taps_swap, chain, stats]


def out_line(at, r):
    def block_rows(index):
        here = span(index, CHUNK)
        r.v_block[here] = (
            r.tok[here].astype(wide) + r.inv[here, 0:1] * r.po_full[here].astype(wide)
        ).astype(low)

    half = r.po.shape[0] // 2 // CHUNK
    return LineSum(at, r.po, r.po_full, r.po_in, r.po_out, r.po_sems, CHUNK, 3, (half, half), block_rows)


def back(at, r, heads, out_sum):
    length, width = r.tok.shape
    inner = r.x.shape[1]
    head = inner // heads
    state_width = r.state_t.shape[0]
    nstate = r.bc.shape[1] // 2
    states = 2 * nstate
    rows, columns = r.in_w.shape[0], r.out_w.shape[1]
    taps = r.input_kernel.shape[0]
    size, count = STRETCH, length // STRETCH
    hl = length // 2
    causal = causal_mask(size)
    ones = jnp.where(causal, 1.0, 0.0)
    drains = []

    def store(name):
        index = STORES.index(name)
        copy = pltpu.make_async_copy(
            getattr(r, "v_" + name), getattr(r, "o_" + name), r.store_sems.at[index]
        )
        copy.start()
        drains.append(Stored(copy))

    def token_copy(index):
        here = span(index, CHUNK)
        return pltpu.make_async_copy(
            r.v_tokens.at[here], r.o_tokens.at[here], r.token_sems.at[index]
        )

    def token_rows(index):
        here = span(index, CHUNK)
        tokens = r.tok[here].astype(wide)
        inv = lax.rsqrt(jnp.mean(tokens * tokens, axis=-1, keepdims=True) + epsilon)
        scaled = r.npl_full[here].astype(wide) * r.norm_gain[...]
        along = jnp.mean(scaled * tokens, axis=-1, keepdims=True)
        r.v_tokens[here] = (
            r.cot[here].astype(wide) + inv * scaled - tokens * (inv * inv * inv * along)
        )
        token_copy(index).start()

    whole_half = hl // CHUNK
    norm_sum = LineSum(
        at, r.npl, r.npl_full, r.npl_in, r.npl_out, r.npl_sems, CHUNK, 2, (whole_half - MOVED, whole_half + MOVED), token_rows
    )
    early = whole_half - 1
    out_ticks = iter(range(out_sum.steps))
    late_ticks = iter(range(norm_sum.steps))
    first_ticks = iter(range(norm_sum.steps))

    def serve():
        t = next(out_ticks, None)
        if t is None:
            return False
        for stream in range(2):
            out_sum.tick(stream, t)
        if t == out_sum.steps - 1:
            store("block")
        return True

    def lead():
        norm_sum.tick(1, next(late_ticks, -1))

    def tail():
        serve()
        t = next(first_ticks, None)
        if t is None:
            return False
        norm_sum.tick(0, t)
        lead()
        return True

    serve()
    def grad_block(i, carry):
        gains, skips = carry
        here = span(i, 32)
        inv, rms = r.inv[here, 0:1], r.inv[here, 1:2]
        gate, scanned = r.gate[here], r.scanned[here]
        sig = jax.nn.sigmoid(gate)
        silu = gate * sig
        gated = scanned * silu
        scaled_grad = inv * r.pull[here]
        gains = gains + fold(scaled_grad * gated)
        gated_grad = scaled_grad * r.gated_gain[...] + 2.0 * rms * gated
        dy = gated_grad * silu
        r.dy[here] = dy
        r.gate_low[here] = (gated_grad * scanned * (sig + silu * (1.0 - sig))).astype(low)
        skips = skips + fold(dy * r.x[here])
        r.proj_grad[here] = (inv * r.cot[here].astype(wide)).astype(low)
        return gains, skips

    zero = jnp.zeros((8, inner), wide)
    gains, skips = each(length // 32, grad_block, (zero, zero))
    gain_row, skip_row = summed(gains), per_head(summed(skips), heads)
    serve()

    state = jnp.zeros((inner, nstate), wide)
    totals = [r.run_row[:, (s + 1) * size - 1 : (s + 1) * size] for s in range(count)]
    for s in reversed(range(count)):
        cut = slice(s * size, (s + 1) * size)
        grown = widen(r.cols[cut, 3 * heads : 4 * heads], head)
        dy_grown = r.dy[cut] * grown
        dy_low = dy_grown.astype(low)
        added = mm(dy_low, r.bc[cut, nstate:], ((0,), (0,)))
        r.fresh[s] = added
        state = tallen(jnp.exp(totals[s]), head, nstate) * state + added
        kept = r.kept[s]
        r.dyc[cut] = per_head(dy_grown * mm(r.bc[cut, nstate:], kept, ((1,), (1,))), heads)
        r.dbc[cut, nstate:] = mm(dy_low, kept, ((1,), (0,)))
    r.turn_own[:inner] = state
    r.turn_own[inner:] = jnp.broadcast_to(sum(totals), (heads, nstate))
    r.turn_all[at.ctx] = r.turn_own[...]
    chain = Swap(at.row, lambda k: r.turn_own, r.turn_all.at[at.ctx], r.turn_sems)
    drains.append(chain)
    serve()

    def within(s, serves):
        cut = slice(s * size, (s + 1) * size)
        b, c = r.bc[cut, :nstate], r.bc[cut, nstate:]
        run = r.cols[cut, :heads]
        scores = r.scores[s]
        dscores = jnp.zeros((size, size), wide)
        across, down = [], []
        for h in range(0, heads, 2):
            pair = []
            for k in (h, h + 1):
                lanes = slice(k * head, (k + 1) * head)
                fall = jnp.exp(
                    jnp.where(causal, run[:, k : k + 1] - r.run_row[k : k + 1, cut], -1e30)
                )
                dt = r.dt_row[k : k + 1, cut]
                dy_low = r.dy[cut, lanes].astype(low)
                products = mm(dy_low, r.x[cut, lanes].astype(low), ((1,), (1,))) * fall
                dscores = dscores + products * dt
                terms = products * scores
                down.append(jnp.sum(terms, axis=0, keepdims=True))
                across.append(jnp.sum(terms * dt, axis=1, keepdims=True))
                mixing = (fall * scores * dt).astype(low)
                pair.append(mm(mixing, dy_low, ((0,), (0,))))
                if k == h:
                    serves()
            r.dx[cut, h * head : (h + 2) * head] = jnp.concatenate(pair, axis=1)
            serves()
        dscores = dscores.astype(low)
        r.dbc[cut, :nstate] = mm(dscores, c, ((0,), (0,)))
        r.dbc[cut, nstate:] += mm(dscores, b, ((1,), (0,)))
        r.down[:, cut] = jnp.concatenate(down, axis=0)
        r.dyc[cut] += jnp.concatenate(across, axis=1)

    decay_rates = turned(jnp.exp(r.decay_log[...]))
    bias_grad = jnp.zeros((heads, 1), wide)
    decay_grad = jnp.zeros((heads, 1), wide)

    def between(s, state):
        cut = slice(s * size, (s + 1) * size)
        state_low = state.astype(low)
        x = r.x[cut]
        spare = widen(r.cols[cut, 2 * heads : 3 * heads], head)
        fade = widen(r.cols[cut, 4 * heads : 5 * heads], head)
        pulled = mm(r.bc[cut, :nstate], state_low, ((1,), (1,)))
        r.dbc[cut, :nstate] += mm((x * spare).astype(low), state_low, ((1,), (0,)))
        tail_grad = per_head(x * fade * pulled, heads)
        r.dx[cut] += spare * pulled + r.skip_row[...] * r.dy[cut]
        shrink = tallen(jnp.exp(totals[s]), head, nstate)
        lost = shrink * state * r.kept[s].astype(wide)
        lost = jnp.concatenate(
            [summed(lost[h * head : (h + 1) * head]) for h in range(heads)], axis=0
        )
        both = jnp.concatenate([tail_grad, r.dyc[cut]], axis=1).T
        tail_row, drun = both[:heads], both[heads:]
        dt, down = r.dt_row[:, cut], r.down[:, cut]
        out_tail = tail_row * dt
        drun = drun - out_tail - down * dt
        dtotal = jnp.sum(lost, axis=1, keepdims=True) + jnp.sum(out_tail, axis=1, keepdims=True)
        ddecay = dtotal + mm(drun, ones, ((1,), (0,)), exact_mode)
        step_grad = (down + tail_row - ddecay * decay_rates) * r.sig_row[:, cut]
        r.step_low[cut] = jnp.concatenate(
            [step_grad.T, jnp.zeros((size, PAD - heads), wide)], axis=1
        ).astype(low)
        if s > 0:
            state = shrink * state + r.fresh[s]
        return (
            state,
            jnp.sum(step_grad, axis=1, keepdims=True),
            jnp.sum(ddecay * r.decays[:, cut], axis=1, keepdims=True),
        )

    def unpull(source, kernel, start, size):
        around = source[pl.ds(start, size + 8)]
        total = kernel[taps - 1 : taps] * around[:size]
        for k in range(taps - 1):
            first = taps - 1 - k
            total = total + kernel[k : k + 1] * around[first : first + size]
        return total

    def low_blocks(start, blocks):
        def block(i, carry):
            here = pl.ds(pl.multiple_of(start + i * 32, 32), 32)
            first = pl.multiple_of(start + i * 32, 32)
            r.input_low[here] = unpull(r.dp, r.input_kernel[...], first, 32).astype(low)
            r.st_low[here] = unpull(r.dpt, r.full_kernel[...], first, 32).astype(low)
            return carry

        each(blocks, block)

    def scale_blocks(start):
        def block(i, carry):
            here = pl.ds(pl.multiple_of(start + i * 32, 32), 32)
            r.dp[here] = r.dx[here] * r.dsil_in[here]
            r.dpt[here] = r.dbc[here] * r.dsil_st[here]
            return carry

        each(hl // 32, block)

    def norm_part(pieces):
        def take(ref):
            if len(pieces) == 1:
                return ref[pieces[0]]
            return jnp.concatenate([ref[cut] for cut in pieces], axis=0)

        value = (
            mm(take(r.gate_low), r.full_gate[...], ((1,), (1,)))
            + mm(take(r.input_low), r.full_in[...], ((1,), (1,)))
            + mm(take(r.st_low), r.full_state[...], ((1,), (1,)))
            + mm(take(r.step_low), r.full_step[...], ((1,), (0,)))
        )
        first = 0
        for cut in pieces:
            r.np_[cut] = value[first : first + cut.stop - cut.start]
            first += cut.stop - cut.start

    def part_blocks(start, blocks, carry):
        def block(i, carry):
            here = pl.ds(pl.multiple_of(start + i * 32, 32), 32)
            tokens = r.tok[here].astype(wide)
            inv = lax.rsqrt(jnp.mean(tokens * tokens, axis=-1, keepdims=True) + epsilon)
            value = r.np_[here]
            r.npl[here] = value.astype(low)
            return carry + fold(value * (tokens * inv))

        return each(blocks, block, carry)

    def send_states(half):
        base = half * hl
        quarter = hl // 2
        for k in range(at.tpn):
            lanes = slice(k * state_width, (k + 1) * state_width)
            r.ds_own[half, k] = jnp.concatenate(
                [
                    r.dbc[base : base + quarter, lanes],
                    r.dbc[base + quarter : base + hl, lanes],
                ],
                axis=1,
            ).astype(low)
        turn = Swap(
            at.line,
            lambda k: r.ds_own.at[half, lax.rem(at.mine + k + 1, at.tpn)],
            r.ds_all.at[half, at.mine],
            r.ds_sems.at[half],
        )
        drains.append(turn)
        r.ds_all[half, at.mine] = r.ds_own[half, at.mine]
        return turn

    half_count = count // 2
    turns = {}
    gain_sums = jnp.zeros((8, width), wide)
    is_last, is_first = at.ctx == at.ctxn - 1, at.ctx == 0
    calls = []

    def some():
        calls.append(0)
        if len(calls) % 6 == 0:
            serve()

    for s in reversed(range(half_count, count)):
        within(s, some)
    chain.arrive()
    state = chained(r.turn_all, at.ctxn, at.ctx, heads, True)
    for s in reversed(range(half_count, count)):
        state, more_bias, more_decay = between(s, state)
        bias_grad, decay_grad = bias_grad + more_bias, decay_grad + more_decay
        serve()
    scale_blocks(hl)
    low_blocks(hl, early)
    serve()
    norm_part([slice(hl, length - CHUNK)])
    gain_sums = part_blocks(hl, early, gain_sums)
    norm_sum.begin(1)
    serve()
    turns[1] = send_states(1)

    r.g_gate[...] = mm(r.norm_t[...], r.gate_low[...], ((1,), (0,))).astype(low)
    s_gate = Scatter(
        at,
        lambda i: r.g_gate.at[span(i, rows)],
        r.gate_b,
        r.gate_o,
        r.gate_i,
        r.scatter_sems.at[0],
    )
    s_gate.pair()
    serve()
    for k in range(length // LANES):
        r.proj_t[:, k * LANES : (k + 1) * LANES] = r.proj_grad[k * LANES : (k + 1) * LANES].T
    r.g_out[...] = mm(r.proj_t[...], r.scaled[...], ((1,), (0,))).astype(low)
    s_out = Scatter(
        at,
        lambda i: r.g_out.at[span(i, columns)],
        r.out_b,
        r.out_o,
        r.out_i,
        r.scatter_sems.at[1],
    )
    s_gate.cross()
    s_out.pair()
    serve()

    turn_taken = []

    def both_lines():
        turn_taken.append(0)
        if len(turn_taken) % 5 == 0:
            serve()
            lead_early()

    early_ticks = iter(range(early - LEAD))

    def lead_early():
        if next(early_ticks, None) is not None:
            lead()

    for s in reversed(range(half_count)):
        within(s, both_lines)
    s_out.cross()
    for s in reversed(range(half_count)):
        state, more_bias, more_decay = between(s, state)
        bias_grad, decay_grad = bias_grad + more_bias, decay_grad + more_decay
    turns[0] = send_states(0)
    scale_blocks(0)

    @pl.when(is_last)
    def _():
        r.dp[length:] = jnp.zeros((8, inner), wide)
        r.dpt[length:] = jnp.zeros((8, states), wide)

    rims = []
    for k, ref in enumerate((r.dp, r.dpt)):
        rims.append(
            Shift(
                ref.at[pl.ds(0, 8)],
                ref.at[pl.ds(length, 8)],
                r.back_sems.at[k],
                at.before,
                jnp.logical_not(is_first),
                jnp.logical_not(is_last),
            )
        )
    drains.extend(rims)
    serve()
    low_blocks(0, hl // 32)
    for rim in rims:
        rim.arrive()
    low_blocks(length - CHUNK, 1)
    lead_early()
    serve()
    norm_part([slice(length - CHUNK, length), slice(0, hl)])
    gain_sums = part_blocks(length - CHUNK, 1, gain_sums)
    gain_sums = part_blocks(0, hl // 32, gain_sums)
    for k in range(early):
        lead_early()
    norm_sum.begin(0)
    gain_part = summed(gain_sums)
    r.g_in[...] = mm(r.norm_t[...], r.input_low[...], ((1,), (0,))).astype(low)
    s_in = Scatter(
        at, lambda i: r.g_in.at[span(i, rows)], r.in_b, r.in_o, r.in_i, r.scatter_sems.at[2]
    )
    s_in.pair()
    tail()
    def tap_block(i, carry):
        around = r.xp[pl.ds(pl.multiple_of(i * 32, 32) + HALO - 8, 40)]
        grad = r.dp[span(i, 32)]
        out = [carry[0] + fold(grad)]
        for k in range(taps):
            first = 9 - taps + k
            out.append(carry[1 + k] + fold(grad * around[first : first + 32]))
        return tuple(out)

    tap_sums = each(length // 32, tap_block, (zero,) * (1 + taps))
    tap_sums = [summed(value) for value in tap_sums]
    s_in.cross()
    tail()

    tail()
    tail()
    quarter = hl // 2
    at_tp = lambda array: sum(
        jnp.where(at.mine == k, array[:, k * state_width : (k + 1) * state_width], 0.0)
        for k in range(at.tpn)
    )
    for half in (1, 0):
        turns[half].arrive()
        mine = r.ds_all[half, 0].astype(wide)
        for k in range(1, at.tpn):
            mine = mine + r.ds_all[half, k].astype(wide)
        for k in range(2):
            cut = slice(half * hl + k * quarter, half * hl + (k + 1) * quarter)
            r.dps[cut] = mine[:, k * state_width : (k + 1) * state_width] * at_tp(r.dsil_st[cut])

    @pl.when(is_last)
    def _():
        r.dps[length:] = jnp.zeros((8, state_width), wide)

    st_rim = Shift(
        r.dps.at[pl.ds(0, 8)],
        r.dps.at[pl.ds(length, 8)],
        r.back_sems.at[2],
        at.before,
        jnp.logical_not(is_first),
        jnp.logical_not(is_last),
    )
    drains.append(st_rim)
    st_grad = r.dps[:length]
    r.sp_own[...] = at_tp(r.sp[...])
    st_sums = [summed(st_grad)]
    for k in range(taps):
        first = HALO + 1 - taps + k
        st_sums.append(summed(st_grad * r.sp_own[first : first + length]))
    tail()
    st_rim.arrive()
    total = unpull(r.dps, r.state_kernel[...], 0, length)
    r.misc_low[...] = jnp.concatenate(
        [total, r.step_low[...].astype(wide)], axis=1
    ).astype(low)
    grads = mm(r.misc_low[...], r.norm[HALO:], ((0,), (0,))).astype(low)
    for k in range(at.n):
        r.g_misc[k] = grads[:, k * rows : (k + 1) * rows]
    s_misc = Scatter(
        at, lambda i: r.g_misc.at[i], r.misc_b, r.misc_o, r.misc_i, r.scatter_sems.at[3]
    )
    s_misc.pair()
    tail()

    r.small[...] = jnp.zeros_like(r.small)

    def put(row, values):
        lanes = values.shape[1]
        for k in range(-(-lanes // LANES)):
            stop = min(LANES, lanes - k * LANES)
            r.small[row + k : row + k + 1, :stop] = values[:, k * LANES : k * LANES + stop]

    place = {}
    at_row = 0
    for name, values in (
        [("gain", gain_part)]
        + [("in%d" % k, tap_sums[1 + k]) for k in range(taps)]
        + [("inoff", tap_sums[0]), ("gated", gain_row)]
        + [("st%d" % k, st_sums[1 + k]) for k in range(taps)]
        + [("stoff", st_sums[0]), ("skip", skip_row)]
        + [("bias", laid(bias_grad)), ("decay", laid(decay_grad))]
    ):
        place[name] = (at_row, values.shape[1])
        put(at_row, values)
        at_row += -(-values.shape[1] // LANES)
    r.small_in[at.here] = r.small[...]
    smalls = Swap(at.group, lambda k: r.small, r.small_in.at[at.here], r.small_sems)
    drains.append(smalls)
    tail()
    s_misc.cross()

    r.v_gate[...] = s_gate.collect()
    store("gate")
    tail()
    r.v_out[...] = s_out.collect().T
    store("out")
    tail()

    smalls.arrive()
    total = r.small_in[0]
    for k in range(1, at.n):
        total = total + r.small_in[k]
    r.total[...] = total
    gain_rows = width // LANES
    r.gain_own[...] = total[:gain_rows]
    r.gain_all[at.mine] = total[:gain_rows]
    gains = Swap(at.line, lambda k: r.gain_own, r.gain_all.at[at.mine], r.gain_sems)
    drains.append(gains)
    tail()

    def get(name):
        row, lanes = place[name]
        return [
            r.total[row + k : row + k + 1, : min(LANES, lanes - k * LANES)]
            for k in range(-(-lanes // LANES))
        ]

    def lay(target, row, name):
        for k, value in enumerate(get(name)):
            target[row : row + 1, k * LANES : k * LANES + value.shape[1]] = value

    for k in range(taps):
        lay(r.v_in_kernel, k, "in%d" % k)
        lay(r.v_st_kernel, k, "st%d" % k)
    lay(r.v_in_offset, 0, "inoff")
    lay(r.v_st_offset, 0, "stoff")
    lay(r.v_gated, 0, "gated")
    lay(r.v_skip, 0, "skip")
    lay(r.v_bias, 0, "bias")
    lay(r.v_decay, 0, "decay")
    for name in ("in_kernel", "st_kernel", "in_offset", "st_offset", "gated", "skip"):
        store(name)
    store("bias")
    store("decay")
    tail()
    r.v_in[...] = s_in.collect()
    store("in")
    tail()
    misc = s_misc.collect()
    r.v_state[...] = misc[:state_width]
    r.v_step[...] = misc[state_width : state_width + heads]
    store("state")
    store("step")
    tail()
    gains.arrive()
    total = r.gain_all[0]
    for k in range(1, at.tpn):
        total = total + r.gain_all[k]
    r.v_gain[...] = total
    store("gain")

    while tail():
        pass

    def token_wait(i, carry):
        token_copy(i).wait()
        return carry

    each(length // CHUNK, token_wait)

    for scatter in (s_gate, s_out, s_in, s_misc):
        scatter.drain()
    out_sum.drain()
    norm_sum.drain()
    return drains


def whole_kernel(n, ctxn, tpn, heads, names, *refs):
    r = SimpleNamespace(**dict(zip(names, refs)))
    r.dx, r.dy, r.np_ = r.carried, r.pull, r.v_tokens
    at = Spots(n, ctxn, tpn)
    out_sum = out_line(at, r)
    drains = front(at, r, heads, out_sum)
    drains += back(at, r, heads, out_sum)
    for item in drains:
        item.drain()


def emit_kernel(count, *refs):
    sources, targets, held = refs[:count], refs[count : 2 * count], refs[2 * count : 3 * count]
    sems = refs[3 * count]
    loads = [pltpu.make_async_copy(sources[k], held[k], sems.at[0, k]) for k in range(count)]
    stores = [pltpu.make_async_copy(held[k], targets[k], sems.at[1, k]) for k in range(count)]
    for copy in loads:
        copy.start()
    for k in range(count):
        loads[k].wait()
        stores[k].start()
    for copy in stores:
        copy.wait()


def emit(arrays):
    count = len(arrays)
    return pl.pallas_call(
        functools.partial(emit_kernel, count),
        out_shape=tuple(jax.ShapeDtypeStruct(a.shape, a.dtype) for a in arrays),
        in_specs=[pl.BlockSpec(memory_space=pl.ANY)] * count,
        out_specs=(pl.BlockSpec(memory_space=pl.ANY),) * count,
        scratch_shapes=[pltpu.VMEM(a.shape, a.dtype) for a in arrays]
        + [pltpu.SemaphoreType.DMA((2, count))],
        compiler_params=pltpu.CompilerParams(vmem_limit_bytes=62 * 2**20),
    )(*arrays)


def per_device(
    tokens,
    norm_gain,
    gate_weight,
    input_weight,
    state_weight,
    step_weight,
    input_kernel,
    input_offset,
    state_kernel,
    state_offset,
    step_bias,
    decay_log,
    skip_gain,
    gated_gain,
    out_weight,
    cotangent,
):
    ctxn = lax.axis_size("ctx")
    n, tpn = lax.axis_size("dp") * ctxn, lax.axis_size("tp")
    length, width = tokens.shape
    rows, inner = input_weight.shape
    state_width, heads = state_weight.shape[1], step_weight.shape[1]
    columns = out_weight.shape[1]
    nstate = state_width * tpn // 2
    head = inner // heads
    taps = input_kernel.shape[0]
    count = length // STRETCH
    half = n // 2
    steps = length // 2 // CHUNK
    hl = length // 2
    row = lambda a: a.reshape(1, a.shape[0])
    inputs = dict(
        tokens=tokens,
        cotangent=cotangent,
        in_w=input_weight,
        gate_w=gate_weight,
        out_w=out_weight,
        h_state_t=state_weight.T,
        h_step_t=step_weight.T,
        h_norm_gain=row(norm_gain),
        h_input_kernel=input_kernel,
        h_input_offset=row(input_offset),
        h_state_kernel=state_kernel,
        h_state_offset=row(state_offset),
        h_step_bias=row(step_bias),
        h_decay_log=row(decay_log),
        h_skip_gain=row(skip_gain),
        h_gated_gain=row(gated_gain),
    )
    outputs = dict(
        o_block=((length, width), low),
        o_tokens=((length, width), wide),
        o_gain=((width // LANES, LANES), wide),
        o_gate=((rows, inner), wide),
        o_in=((rows, inner), wide),
        o_state=((state_width, rows), wide),
        o_step=((heads, rows), wide),
        o_in_kernel=((taps, inner), wide),
        o_in_offset=((1, inner), wide),
        o_st_kernel=((taps, state_width), wide),
        o_st_offset=((1, state_width), wide),
        o_bias=((1, heads), wide),
        o_decay=((1, heads), wide),
        o_skip=((1, heads), wide),
        o_gated=((1, inner), wide),
        o_out=((inner, columns), wide),
    )
    small_rows = width // LANES + (taps + 2) * inner // LANES + (taps + 1) + 3
    small_rows = -(-small_rows // 8) * 8
    both = (length, inner)
    scratch = {
        name: (inputs["h_" + name].shape, inputs["h_" + name].dtype) for name in SMALL_INPUTS
    }
    scratch.update({"v" + name[1:]: value for name, value in outputs.items()})
    scratch.update(
        skip_row=((1, inner), wide),
        tok=((length, width), low),
        cot=((length, width), low),
        tok_rim=((HALO, width), low),
        step_own=((PAD, rows), low),
        step_slots=((n, PAD, rows), low),
        full_step=((PAD, width), low),
        state_own=((rows, 2 * nstate), low),
        state_all=((tpn, state_width, rows), low),
        full_state=((width, 2 * nstate), low),
        taps_own=((8, state_width), wide),
        taps_all=((tpn, 8, state_width), wide),
        full_kernel=((taps, 2 * nstate), wide),
        full_offset=((1, 2 * nstate), wide),
        norm=((HALO + length, width), low),
        norm_t=((width, length), low),
        full_in=((width, inner), low),
        full_gate=((width, inner), low),
        full_out=((width, inner), low),
        out_v=((inner, columns), low),
        out_own=((columns, inner), low),
        sp=((HALO + length, 2 * nstate), wide),
        sp_own=((HALO + length, state_width), wide),
        dsil_st=((length, 2 * nstate), wide),
        bc=((length, 2 * nstate), low),
        xp=((HALO + length, inner), wide),
        x=(both, wide),
        dsil_in=(both, wide),
        sig_row=((heads, length), wide),
        dt_row=((heads, length), wide),
        decays=((heads, length), wide),
        run_row=((heads, length), wide),
        cols=((length, 5 * heads), wide),
        fresh=((count, inner, nstate), wide),
        chain_own=((inner + heads, nstate), wide),
        chain_all=((ctxn, inner + heads, nstate), wide),
        turn_own=((inner + heads, nstate), wide),
        turn_all=((ctxn, inner + heads, nstate), wide),
        scores=((count, STRETCH, STRETCH), wide),
        scanned=(both, wide),
        carried=(both, wide),
        gate=(both, wide),
        pull=(both, wide),
        kept=((count, inner, nstate), low),
        scaled=(both, low),
        proj_t=((width, length), low),
        stat=((length, 8), wide),
        stat_own=((8, length), wide),
        stat_all=((tpn, 8, length), wide),
        inv=((length, 8), wide),
        po=((length, width), low),
        po_full=((length, width), low),
        po_in=((2 * steps, CHUNK, width), low),
        po_out=((2 * steps, CHUNK, width), low),
        gate_low=(both, low),
        proj_grad=((length, width), low),
        dyc=((length, heads), wide),
        dbc=((length, 2 * nstate), wide),
        g_gate=((width, inner), low),
        gate_b=((half, rows, inner), low),
        gate_o=((half, rows, inner), low),
        gate_i=((half, rows, inner), low),
        g_in=((width, inner), low),
        in_b=((half, rows, inner), low),
        in_o=((half, rows, inner), low),
        in_i=((half, rows, inner), low),
        g_out=((width, inner), low),
        out_b=((half, columns, inner), low),
        out_o=((half, columns, inner), low),
        out_i=((half, columns, inner), low),
        g_misc=((n, MISC, rows), low),
        misc_b=((half, MISC, rows), low),
        misc_o=((half, MISC, rows), low),
        misc_i=((half, MISC, rows), low),
        down=((heads, length), wide),
        step_low=((length, PAD), low),
        st_low=((length, 2 * nstate), low),
        ds_own=((2, tpn, hl // 2, 2 * state_width), low),
        ds_all=((2, tpn, hl // 2, 2 * state_width), low),
        dpt=((length + 8, 2 * nstate), wide),
        dp=((length + 8, inner), wide),
        dps=((length + 8, state_width), wide),
        input_low=(both, low),
        misc_low=((length, MISC), low),
        npl=((length, width), low),
        npl_full=((length, width), low),
        npl_in=((2 * steps, CHUNK, width), low),
        npl_out=((2 * steps, CHUNK, width), low),
        small=((small_rows, LANES), wide),
        small_in=((n, small_rows, LANES), wide),
        total=((small_rows, LANES), wide),
        gain_own=((width // LANES, LANES), wide),
        gain_all=((tpn, width // LANES, LANES), wide),
    )
    sems = dict(
        store_sems=(len(STORES),),
        token_sems=(2 * steps,),
        load_sems=(3 + len(SMALL_INPUTS),),
        gather_sems=(5, 5, half),
        rim_sems=(2,),
        bc_sems=(2, tpn),
        taps_sems=(2, tpn),
        chain_sems=(2, ctxn),
        turn_sems=(2, ctxn),
        stat_sems=(2, tpn),
        po_sems=(4, 2 * steps),
        npl_sems=(4, 2 * steps),
        scatter_sems=(4, 4, half),
        ds_sems=(2, 2, tpn),
        back_sems=(3, 2),
        small_sems=(2, n),
        gain_sems=(2, tpn),
    )
    names = list(inputs) + list(outputs) + list(scratch) + list(sems)
    results = pl.pallas_call(
        functools.partial(whole_kernel, n, ctxn, tpn, heads, names),
        out_shape=tuple(jax.ShapeDtypeStruct(*o) for o in outputs.values()),
        in_specs=[pl.BlockSpec(memory_space=pl.ANY)] * len(inputs),
        out_specs=(pl.BlockSpec(memory_space=pl.ANY),) * len(outputs),
        scratch_shapes=[pltpu.VMEM(*s) for s in scratch.values()]
        + [pltpu.SemaphoreType.DMA(s) for s in sems.values()],
        compiler_params=pltpu.CompilerParams(
            collective_id=0, has_side_effects=True, vmem_limit_bytes=62 * 2**20
        ),
    )(*inputs.values())
    o = SimpleNamespace(**dict(zip(outputs, emit(results))))
    return (
        o.o_block,
        o.o_tokens,
        o.o_gain.reshape(-1),
        o.o_gate,
        o.o_in,
        o.o_state.T,
        o.o_step.T,
        o.o_in_kernel,
        o.o_in_offset.reshape(-1),
        o.o_st_kernel,
        o.o_st_offset.reshape(-1),
        o.o_bias.reshape(-1),
        o.o_decay.reshape(-1),
        o.o_skip.reshape(-1),
        o.o_gated.reshape(-1),
        o.o_out,
    )


def solution(mesh):
    placed = (
        P(("dp", "ctx"), None),
        P(),
        P(("dp", "ctx"), "tp"),
        P(("dp", "ctx"), "tp"),
        P(("dp", "ctx"), "tp"),
        P(("dp", "ctx"), "tp"),
        P(None, "tp"),
        P("tp"),
        P(None, "tp"),
        P("tp"),
        P("tp"),
        P("tp"),
        P("tp"),
        P("tp"),
        P("tp", ("dp", "ctx")),
        P(("dp", "ctx"), None),
    )
    return jax.shard_map(
        per_device,
        mesh=mesh,
        in_specs=placed,
        out_specs=(
            P(("dp", "ctx"), None),
            P(("dp", "ctx"), None),
            P(),
            P(("dp", "ctx"), "tp"),
            P(("dp", "ctx"), "tp"),
            P(("dp", "ctx"), "tp"),
            P(("dp", "ctx"), "tp"),
            P(None, "tp"),
            P("tp"),
            P(None, "tp"),
            P("tp"),
            P("tp"),
            P("tp"),
            P("tp"),
            P("tp"),
            P("tp", ("dp", "ctx")),
        ),
        check_vma=False,
    )
```
